32 devices in a mesh: dp: 8 (over z, x), tensor: 4 (over y, core).
Axes of the slice: x: 2, y: 2, z: 4, core: 2. Of those that a mesh axis runs over, the one named last changes fastest.
Arguments:
- inputs: bfloat16 [2, 8, 1024, 1152], P(None, 'dp', 'tensor'), may hold values from -6 to 6
- lengths: int32 [2, 8], P(None, 'dp'), may hold values from 256 to 1024, as said below
- gain_attn: bfloat16 [1152], P('dp'), may hold values from 0.5 to 1.5
- gain_mlp: bfloat16 [1152], P('dp'), may hold values from 0.5 to 1.5
- w_query: bfloat16 [1152, 1152], P('dp'), may hold values from -0.1875 to 0.1875
- key_weight: bfloat16 [1152, 384], P('dp'), may hold values from -0.1875 to 0.1875
- value_weight: bfloat16 [1152, 384], P('dp'), may hold values from -0.1875 to 0.1875
- w_gate: bfloat16 [1152, 3072], P('dp', 'tensor'), may hold values from -0.1875 to 0.1875
- w_up: bfloat16 [1152, 3072], P('dp', 'tensor'), may hold values from -0.1875 to 0.1875
- w_out: bfloat16 [1152, 1152], P('dp'), may hold values from -0.75 to 0.75
- w_down: bfloat16 [3072, 1152], P('tensor', 'dp'), may hold values from -0.21875 to 0.21875
- cotangent: bfloat16 [2, 8, 1024, 1152], P(None, 'dp', 'tensor'), may hold values from -6 to 6
Outputs:
- out_act: bfloat16 [2, 8, 1024, 1152], P(None, 'dp', 'tensor')
- grad_inputs: bfloat16 [2, 8, 1024, 1152], P(None, 'dp', 'tensor')
- grad_gain_attn: float32 [1152], P('dp')
- grad_gain_mlp: float32 [1152], P('dp')
- grad_w_query: float32 [1152, 1152], P('dp')
- grad_w_key: float32 [1152, 384], P('dp')
- grad_w_value: float32 [1152, 384], P('dp')
- grad_w_gate: float32 [1152, 3072], P('dp', 'tensor')
- grad_w_up: float32 [1152, 3072], P('dp', 'tensor')
- grad_w_out: float32 [1152, 1152], P('dp')
- grad_w_down: float32 [3072, 1152], P('tensor', 'dp')
The draws below stay inside these ranges and needn't reach their ends.
Inputs may be any that keep to these rules, and one draw needn't show every extreme that they name: `lengths`: each sequence's valid tokens; in every micro-batch one sequence fills all 1024 slots.
All inputs are finite; a program needn't handle non-finite values.
Results may differ from the reference program's by a relative error of at most 0.023.
Values may be sent and summed in bfloat16 or wider, within the bound.
No kernel may reach another device: no remote copies, remote signals or barrier semaphores. Data moves between devices by JAX's collectives and lax.ppermute only.
A program may use at most 192 MiB of HBM per device.

```python
import jax
import jax.numpy as jnp
from jax import lax

MODEL_WIDTH = 1152
QUERY_HEAD_COUNT = 18
KEY_VALUE_HEADS = 6
HEAD_SIZE = 64
FF = 3072
SEQ = 1024
MICRO = 2
SEQS = 8
MIN_LEN = 256


def draw_lengths(key, part):
    draw_key, pick_key = jax.random.split(jax.random.fold_in(key, 11))
    lengths_drawn = jax.random.randint(draw_key, (MICRO, SEQS), MIN_LEN, SEQ + 1)
    chosen_slot = jax.random.randint(pick_key, (MICRO, 1), 0, SEQS)
    columns = jnp.arange(SEQS, dtype=jnp.int32)[None, :]
    return jnp.where(columns == chosen_slot, SEQ, lengths_drawn).astype(jnp.int32)


def draw_inputs(key, part):
    noise_key, scale_key = jax.random.split(jax.random.fold_in(key, 23))
    full_shape = (MICRO, SEQS, SEQ, MODEL_WIDTH)
    noise = jnp.clip(jax.random.normal(noise_key, full_shape, jnp.float32), -6.0, 6.0)
    row_scale = jnp.exp(jax.random.uniform(scale_key, (MICRO, SEQS, SEQ, 1), jnp.float32, -1.386, 0.0))
    return (noise * row_scale).astype(jnp.bfloat16)


def shard_levels(stream_key, shape, shards, smallest, top_value):
    loudness = 1.0
    for dim, blocks in shards:
        steps = jax.random.uniform(jax.random.fold_in(jax.random.fold_in(stream_key, 6), dim), (blocks,), jnp.float32, smallest / len(shards), top_value / len(shards))
        loudness = loudness * jnp.repeat(jnp.exp(steps), shape[dim] // blocks).reshape((-1,) + (1,) * (len(shape) - 1 - dim))
    return loudness


def gaussian(rng, shape, deviation, reach, cuts=(), kind=jnp.bfloat16):
    drawn = jax.random.normal(rng, shape, jnp.float32) * deviation
    if len(cuts) > 0:
        drawn = shard_levels(rng, shape, cuts, -0.22, 0.18) * drawn
    return jnp.clip(drawn, min=-reach, max=reach).astype(kind)


def setup_inputs(seed: int = 0) -> dict:
    keys = jax.random.split(jax.random.key(seed), 13)
    return {
        "inputs": draw_inputs(jax.random.fold_in(keys[12], 71), 0),
        "lengths": draw_lengths(jax.random.fold_in(keys[12], 71), 0),
        "gain_attn": jnp.clip(1.0 + 0.1 * jax.random.normal(keys[2], (MODEL_WIDTH,), jnp.float32), 0.5, 1.5).astype(jnp.bfloat16),
        "gain_mlp": jnp.clip(1.0 + 0.1 * jax.random.normal(keys[3], (MODEL_WIDTH,), jnp.float32), 0.5, 1.5).astype(jnp.bfloat16),
        "w_query": gaussian(keys[4], (MODEL_WIDTH, QUERY_HEAD_COUNT * HEAD_SIZE), MODEL_WIDTH ** -0.5, 0.1875, ((0, 8),)),
        "key_weight": gaussian(keys[5], (MODEL_WIDTH, KEY_VALUE_HEADS * HEAD_SIZE), MODEL_WIDTH ** -0.5, 0.1875, ((0, 8),)),
        "value_weight": gaussian(keys[6], (MODEL_WIDTH, KEY_VALUE_HEADS * HEAD_SIZE), MODEL_WIDTH ** -0.5, 0.1875, ((0, 8),)),
        "w_gate": gaussian(keys[7], (MODEL_WIDTH, FF), MODEL_WIDTH ** -0.5, 0.1875, ((0, 8), (1, 4))),
        "w_up": gaussian(keys[8], (MODEL_WIDTH, FF), MODEL_WIDTH ** -0.5, 0.1875, ((0, 8), (1, 4))),
        "w_out": gaussian(keys[9], (QUERY_HEAD_COUNT * HEAD_SIZE, MODEL_WIDTH), (QUERY_HEAD_COUNT * HEAD_SIZE // 16) ** -0.5, 0.75, ((0, 8),)),
        "w_down": gaussian(keys[10], (FF, MODEL_WIDTH), (FF // 4) ** -0.5, 0.21875, ((0, 4), (1, 8))),
        "cotangent": gaussian(keys[11], (MICRO, SEQS, SEQ, MODEL_WIDTH), 1.0, 6.0, ((1, 8), (2, 4))),
    }


@jax.custom_vjp
def reduced_precision(v):
    return lax.optimization_barrier(v.astype(jnp.bfloat16)).astype(jnp.float32)

@jax.custom_vjp
def reduced_backward(v):
    return v

def low_keep(v):
    return (reduced_precision(v), None)

def low_pass(kept, grad):
    return (grad,)

def back_keep(v):
    return (v, None)

def back_low(kept, grad):
    return (reduced_precision(grad),)
reduced_precision.defvjp(low_keep, low_pass)
reduced_backward.defvjp(back_keep, back_low)
EPSILON = 1e-05
ROPE_BASE = 10000.0
MASKED = -1e+30

def rope_tables(positions, head_dim):
    half_dim = head_dim // 2
    exponent = jnp.arange(half_dim, dtype=jnp.float32) * (2.0 / head_dim)
    frequency = ROPE_BASE ** (-exponent)
    angles = positions[:, None] * frequency[None, :]
    cosine_table = jnp.concatenate([jnp.cos(angles), jnp.cos(angles)], axis=1)
    sine_table = jnp.concatenate([jnp.sin(angles), jnp.sin(angles)], axis=1)
    return (cosine_table, sine_table)

def rotate_half(values):
    half_dim = values.shape[-1] // 2
    return jnp.concatenate([-values[..., half_dim:], values[..., :half_dim]], axis=-1)

def apply_rotary(values, cosine_table, sine_table):
    return values * cosine_table[:, None, :] + rotate_half(values) * sine_table[:, None, :]

def rms_normed(values, gain_full):
    row_scale = lax.rsqrt(lax.optimization_barrier(jnp.mean(values * values, axis=-1, keepdims=True)) + EPSILON)
    return values * row_scale * gain_full

def matrix_product(left_side, right_side):
    return jnp.dot(left_side, right_side, precision=lax.Precision.HIGHEST)

def layer_forward(seq_inputs, valid_count, weights):
    gain_attn, gain_mlp, w_query, key_weight, value_weight, w_gate, w_up, w_out, w_down = weights
    position_count = seq_inputs.shape[0]
    group_width = QUERY_HEAD_COUNT // KEY_VALUE_HEADS
    cosine_table, sine_table = rope_tables(jnp.arange(position_count, dtype=jnp.float32), HEAD_SIZE)
    first_normalized = reduced_precision(rms_normed(seq_inputs, gain_attn))
    query_unrotated = reduced_backward(matrix_product(first_normalized, w_query)).reshape(position_count, QUERY_HEAD_COUNT, HEAD_SIZE)
    key_unrotated = reduced_backward(matrix_product(first_normalized, key_weight)).reshape(position_count, KEY_VALUE_HEADS, HEAD_SIZE)
    value_reduced = reduced_precision(reduced_backward(matrix_product(first_normalized, value_weight))).reshape(position_count, KEY_VALUE_HEADS, HEAD_SIZE)
    query_rows = reduced_precision(apply_rotary(query_unrotated, cosine_table, sine_table)).reshape(position_count, KEY_VALUE_HEADS, group_width, HEAD_SIZE)
    keys_rot = reduced_precision(apply_rotary(key_unrotated, cosine_table, sine_table))
    positions = jnp.arange(position_count, dtype=jnp.int32)
    allowed = (positions[None, :] <= positions[:, None]) & (positions[None, :] < valid_count)
    scores = jnp.einsum('qhgd,shd->hgqs', query_rows, keys_rot, precision=lax.Precision.HIGHEST) * HEAD_SIZE ** (-0.5)
    scores = reduced_backward(jnp.where(allowed, scores, MASKED))
    soft_low = reduced_precision(jax.nn.softmax(scores, axis=-1))
    attended = jnp.einsum('hgqs,shd->qhgd', soft_low, value_reduced, precision=lax.Precision.HIGHEST)
    attended = reduced_precision(reduced_backward(attended.reshape(position_count, QUERY_HEAD_COUNT * HEAD_SIZE)))
    middle = seq_inputs + reduced_backward(matrix_product(attended, w_out))
    normed_two = reduced_precision(rms_normed(middle, gain_mlp))
    gate_proj = reduced_backward(matrix_product(normed_two, w_gate))
    up_proj = reduced_backward(matrix_product(normed_two, w_up))
    activated = reduced_precision(jax.nn.silu(gate_proj) * up_proj)
    ffn_out = reduced_backward(matrix_product(activated, w_down))
    valid = (positions < valid_count).astype(jnp.float32)[:, None]
    return valid * (middle + ffn_out)

def reference(inputs, lengths, gain_attn, gain_mlp, w_query, key_weight, value_weight, w_gate, w_up, w_out, w_down, cotangent):
    weights = tuple((weight_item.astype(jnp.float32) for weight_item in (gain_attn, gain_mlp, w_query, key_weight, value_weight, w_gate, w_up, w_out, w_down)))
    full_shape = inputs.shape
    flat_inputs = inputs.astype(jnp.float32).reshape(-1, SEQ, MODEL_WIDTH)
    flat_lengths = lengths.reshape(-1).astype(jnp.int32)
    flat_cot = cotangent.astype(jnp.float32).reshape(-1, SEQ, MODEL_WIDTH)
    step_layer = jax.checkpoint(layer_forward)

    def forward(all_inputs, all_weights):

        def scan_step(state_carry, scan_item):
            return (state_carry, step_layer(scan_item[0], scan_item[1], all_weights))
        unused, outputs = lax.scan(scan_step, jnp.zeros((), jnp.float32), (all_inputs, flat_lengths))
        return outputs
    outputs, pullback = jax.vjp(forward, flat_inputs, weights)
    grad_flat, grad_weights = pullback(flat_cot)
    return (outputs.reshape(full_shape).astype(jnp.bfloat16), grad_flat.reshape(full_shape).astype(jnp.bfloat16), grad_weights[0], grad_weights[1], grad_weights[2], grad_weights[3], grad_weights[4], grad_weights[5], grad_weights[6], grad_weights[7], grad_weights[8])
```

```python
import jax
import jax.numpy as jnp
from jax import lax
from jax.sharding import PartitionSpec as P

HEAD_SIZE = 64
EPSILON = 1e-05
ROPE_BASE = 10000.0
MASKED = -1e30
BF16 = jnp.bfloat16
F32 = jnp.float32

BLOCK_XOR = (0, 2, 1, 3)


def near(value):
    count = lax.axis_size("tensor")
    return lax.ppermute(value, "tensor", [(i, i ^ 1) for i in range(count)])


def far(value):
    count = lax.axis_size("tensor")
    return lax.ppermute(value, "tensor", [(i, i ^ 2) for i in range(count)])


def gather_rows(own):
    pair = jnp.concatenate([own, far(own)], axis=0)
    return jnp.concatenate([pair, near(pair)], axis=0)


def scatter_rows(partial):
    half = partial.shape[0] // 2
    quarter = half // 2
    kept = partial[:half].astype(F32) + near(partial[half:].astype(BF16)).astype(F32)
    return kept[:quarter] + far(kept[quarter:].astype(BF16)).astype(F32)


def dot(left_side, right_side):
    return jnp.dot(left_side, right_side, preferred_element_type=F32)


def contract_rows(left_side, right_side):
    return lax.dot_general(
        left_side, right_side, (((0,), (0,)), ((), ())), preferred_element_type=F32
    )


def contract_last(left_side, right_side):
    return lax.dot_general(
        left_side, right_side, (((1,), (1,)), ((), ())), preferred_element_type=F32
    )


def rope_tables(positions, head_dim):
    half_dim = head_dim // 2
    exponent = jnp.arange(half_dim, dtype=F32) * (2.0 / head_dim)
    frequency = ROPE_BASE ** (-exponent)
    angles = positions[:, None] * frequency[None, :]
    cosine_table = jnp.concatenate([jnp.cos(angles), jnp.cos(angles)], axis=1)
    sine_table = jnp.concatenate([jnp.sin(angles), jnp.sin(angles)], axis=1)
    return (cosine_table, sine_table)


def rotate_half(values):
    half_dim = values.shape[-1] // 2
    return jnp.concatenate([-values[..., half_dim:], values[..., :half_dim]], axis=-1)


def apply_rotary(values, cosine_table, sine_table):
    return values * cosine_table[:, None, :] + rotate_half(values) * sine_table[:, None, :]


def unrope(grads_in, cosine_table, sine_table):
    half_dim = grads_in.shape[-1] // 2
    scaled = grads_in * sine_table[:, None, :]
    turned = jnp.concatenate([scaled[..., half_dim:], -scaled[..., :half_dim]], axis=-1)
    return grads_in * cosine_table[:, None, :] + turned


def row_scale_of(values):
    return lax.rsqrt(jnp.mean(values * values, axis=-1, keepdims=True) + EPSILON)


def norm_backward(grad_normed, row_values, row_scale, gain_full):
    gain_grad = jnp.sum(grad_normed * row_values * row_scale, axis=0)
    inner_grad = grad_normed * gain_full
    row_grad = row_scale * inner_grad - row_values * row_scale**3 * jnp.mean(
        inner_grad * row_values, axis=-1, keepdims=True
    )
    return (row_grad, gain_grad)


def attention_scores(query_rows, keys_all, allowed):
    raw_scores = jnp.einsum(
        "qhgd,shd->hgqs", query_rows, keys_all, preferred_element_type=F32
    ) * HEAD_SIZE ** (-0.5)
    return jnp.where(allowed, raw_scores, MASKED)


def attend(query_rows, keys_all, values_all, allowed):
    row_count = query_rows.shape[0]
    scores = attention_scores(query_rows, keys_all, allowed)
    maxima = jnp.max(scores, axis=-1, keepdims=True)
    log_total = maxima + jnp.log(jnp.sum(jnp.exp(scores - maxima), axis=-1, keepdims=True))
    soft_low = jnp.exp(scores - log_total).astype(BF16)
    attended = jnp.einsum("hgqs,shd->qhgd", soft_low, values_all, preferred_element_type=F32)
    return attended.reshape(row_count, -1).astype(BF16), log_total


def attend_backward(grad_att, query_rows, keys_all, values_all, allowed, log_total):
    row_count, position_count = query_rows.shape[0], keys_all.shape[0]
    soft_float = jnp.exp(attention_scores(query_rows, keys_all, allowed) - log_total)
    grad_soft = jnp.einsum("qhgd,shd->hgqs", grad_att, values_all, preferred_element_type=F32)
    grad_scores = (
        soft_float * (grad_soft - jnp.sum(soft_float * grad_soft, axis=-1, keepdims=True))
    ).astype(BF16)
    value_part = jnp.einsum(
        "hgqs,qhgd->shd", soft_float.astype(BF16), grad_att, preferred_element_type=F32
    )
    score_scale = HEAD_SIZE ** (-0.5)
    key_part = (
        jnp.einsum("hgqs,qhgd->shd", grad_scores, query_rows, preferred_element_type=F32)
        * score_scale
    )
    grad_queries = (
        jnp.einsum("hgqs,shd->qhgd", grad_scores, keys_all, preferred_element_type=F32)
        * score_scale
    )
    return (
        grad_queries.reshape(row_count, -1),
        jnp.concatenate(
            [key_part.reshape(position_count, -1), value_part.reshape(position_count, -1)], axis=1
        ),
    )


def shards(
    inputs,
    lengths,
    gain_attn,
    gain_mlp,
    w_query,
    key_weight,
    value_weight,
    w_gate,
    w_up,
    w_out,
    w_down,
    cotangent,
):
    micro = inputs.shape[0]
    row_share = inputs.shape[2]
    model_width = inputs.shape[3]
    tensor_count = lax.axis_size("tensor")
    tensor_index = lax.axis_index("tensor")
    query_width = w_query.shape[1]
    key_width = key_weight.shape[1]
    hidden_share = w_gate.shape[1]
    query_heads = query_width // HEAD_SIZE
    key_heads = key_width // HEAD_SIZE
    group_width = query_heads // key_heads

    attn_local = jnp.concatenate([w_query, key_weight, value_weight, w_out], axis=1)
    attn_width = attn_local.shape[1]
    block_width = attn_width // tensor_count
    attn_quarter = lax.dynamic_slice_in_dim(attn_local, tensor_index * block_width, block_width, 1)
    attn_blocks = lax.all_gather(attn_quarter, ("tensor", "dp"), axis=0, tiled=True)
    attn_full = jnp.concatenate(
        [attn_blocks[b * model_width : (b + 1) * model_width] for b in range(tensor_count)], axis=1
    )
    mlp_local = jnp.concatenate([w_gate, w_up, w_down.T], axis=1)
    mlp_full = lax.all_gather(mlp_local, "dp", axis=0, tiled=True)
    gains = lax.all_gather(jnp.stack([gain_attn, gain_mlp]), "dp", axis=1, tiled=True).astype(F32)
    gain_one, gain_two = gains[0:1], gains[1:2]
    full_query = attn_full[:, :query_width]
    full_key = attn_full[:, query_width : query_width + key_width]
    full_value = attn_full[:, query_width + key_width : query_width + 2 * key_width]
    full_out = attn_full[:, query_width + 2 * key_width :]
    full_gate = mlp_full[:, :hidden_share]
    full_up = mlp_full[:, hidden_share : 2 * hidden_share]
    full_down_t = mlp_full[:, 2 * hidden_share :]

    row_start = tensor_index * row_share
    query_pos = row_start + jnp.arange(row_share, dtype=jnp.int32)
    block_start = jnp.stack([(tensor_index ^ x) * row_share for x in BLOCK_XOR])
    key_pos = (block_start[:, None] + jnp.arange(row_share, dtype=jnp.int32)[None, :]).reshape(-1)
    cosine_table, sine_table = rope_tables(query_pos.astype(F32), HEAD_SIZE)

    valids = [
        (query_pos < lengths[b, 0]).astype(F32)[:, None] for b in range(micro)
    ]
    grad_rows = [cotangent[b, 0].astype(F32) * valids[b] for b in range(micro)]
    grad_own = [g.astype(BF16) for g in grad_rows]
    grad_far = far(jnp.stack(grad_own))
    grad_near = near(jnp.stack([jnp.stack(grad_own), grad_far]))
    grad_ffn = [
        jnp.concatenate([grad_own[b], grad_far[b], grad_near[0, b], grad_near[1, b]], axis=0)
        for b in range(micro)
    ]

    kept = []
    for b in range(micro):
        row_values = inputs[b, 0].astype(F32)
        scale_one = row_scale_of(row_values)
        hidden_one = (row_values * scale_one * gain_one).astype(BF16)
        key_unrotated = dot(hidden_one, full_key).reshape(row_share, key_heads, HEAD_SIZE)
        values_own = dot(hidden_one, full_value).astype(BF16)
        keys_own = (
            apply_rotary(key_unrotated, cosine_table, sine_table)
            .astype(BF16)
            .reshape(row_share, key_width)
        )
        pairs_all = gather_rows(jnp.concatenate([keys_own, values_own], axis=1))
        query_unrotated = dot(hidden_one, full_query).reshape(row_share, query_heads, HEAD_SIZE)
        query_rows = (
            apply_rotary(query_unrotated, cosine_table, sine_table)
            .astype(BF16)
            .reshape(row_share, key_heads, group_width, HEAD_SIZE)
        )
        keys_all = pairs_all[:, :key_width].reshape(-1, key_heads, HEAD_SIZE)
        values_all = pairs_all[:, key_width:].reshape(-1, key_heads, HEAD_SIZE)
        allowed = (key_pos[None, :] <= query_pos[:, None]) & (key_pos[None, :] < lengths[b, 0])
        attended, log_total = attend(query_rows, keys_all, values_all, allowed)
        middle = row_values + dot(attended, full_out)
        scale_two = row_scale_of(middle)
        hidden_two = gather_rows((middle * scale_two * gain_two).astype(BF16))
        kept.append(
            dict(
                row_values=row_values,
                scale_one=scale_one,
                hidden_one=hidden_one,
                query_rows=query_rows,
                keys_all=keys_all,
                values_all=values_all,
                allowed=allowed,
                log_total=log_total,
                attended=attended,
                middle=middle,
                scale_two=scale_two,
                hidden_two=hidden_two,
            )
        )

    for b in range(micro):
        k = kept[b]
        gate_proj = dot(k["hidden_two"], full_gate)
        up_proj = dot(k["hidden_two"], full_up)
        grad_act = dot(grad_ffn[b], full_down_t)
        sigmoid_gate = jax.nn.sigmoid(gate_proj)
        k["activated"] = (gate_proj * sigmoid_gate * up_proj).astype(BF16)
        k["grad_gate"] = (
            grad_act * up_proj * sigmoid_gate * (1.0 + gate_proj * (1.0 - sigmoid_gate))
        ).astype(BF16)
        k["grad_up"] = (grad_act * gate_proj * sigmoid_gate).astype(BF16)
        grad_partial = contract_last(k["grad_gate"], full_gate) + contract_last(
            k["grad_up"], full_up
        )
        k["grad_normed_two"] = scatter_rows(grad_partial)
    def total(left_side, right_side):
        parts = [contract_rows(left_side(b), right_side(b)) for b in range(micro)]
        return sum(parts[1:], parts[0])

    grad_mlp_w = jnp.concatenate(
        [
            total(lambda b: kept[b]["hidden_two"], lambda b: kept[b]["grad_gate"]).astype(BF16),
            total(lambda b: kept[b]["hidden_two"], lambda b: kept[b]["grad_up"]).astype(BF16),
            total(lambda b: grad_ffn[b], lambda b: kept[b]["activated"]).astype(BF16),
        ],
        axis=1,
    )
    grad_mlp_w = lax.psum_scatter(grad_mlp_w, "dp", scatter_dimension=0, tiled=True).astype(F32)
    grad_gate_w = grad_mlp_w[:, :hidden_share]
    grad_up_w = grad_mlp_w[:, hidden_share : 2 * hidden_share]
    grad_down_w = grad_mlp_w[:, 2 * hidden_share :].T

    gain_two_grads = []
    for b in range(micro):
        k = kept[b]
        row_grad_two, gain_two_grad = norm_backward(
            k["grad_normed_two"], k["middle"], k["scale_two"], gain_two
        )
        gain_two_grads.append(gain_two_grad)
        k["grad_middle"] = grad_rows[b] + row_grad_two
        k["grad_branch"] = k["grad_middle"].astype(BF16)
        grad_att = (
            contract_last(k["grad_branch"], full_out)
            .astype(BF16)
            .reshape(row_share, key_heads, group_width, HEAD_SIZE)
        )
        grad_queries, pair_partial = attend_backward(
            grad_att, k["query_rows"], k["keys_all"], k["values_all"], k["allowed"], k["log_total"]
        )
        pair_own = scatter_rows(pair_partial)
        k["grad_queries"] = (
            unrope(grad_queries.reshape(row_share, query_heads, HEAD_SIZE), cosine_table, sine_table)
            .astype(BF16)
            .reshape(row_share, query_width)
        )
        grad_keys = (
            unrope(
                pair_own[:, :key_width].reshape(row_share, key_heads, HEAD_SIZE),
                cosine_table,
                sine_table,
            )
            .astype(BF16)
            .reshape(row_share, key_width)
        )
        k["grad_pairs"] = jnp.concatenate(
            [k["grad_queries"], grad_keys, pair_own[:, key_width:].astype(BF16)], axis=1
        )

    outputs, input_grads, gain_one_grads = [], [], []
    full_qkv = attn_full[:, : query_width + 2 * key_width]
    for b in range(micro):
        k = kept[b]
        grad_normed_one = contract_last(k["grad_pairs"], full_qkv)
        row_grad_one, gain_one_grad = norm_backward(
            grad_normed_one, k["row_values"], k["scale_one"], gain_one
        )
        gain_one_grads.append(gain_one_grad)
        input_grads.append((k["grad_middle"] + row_grad_one).astype(BF16))
        ffn_out = scatter_rows(contract_last(k["activated"], full_down_t))
        outputs.append((valids[b] * (k["middle"] + ffn_out)).astype(BF16))

    grad_gains = jnp.stack(
        [sum(gain_one_grads[1:], gain_one_grads[0]), sum(gain_two_grads[1:], gain_two_grads[0])]
    )
    grad_attn_w = jnp.concatenate(
        [
            total(lambda b: kept[b]["hidden_one"], lambda b: kept[b]["grad_pairs"]),
            total(lambda b: kept[b]["attended"], lambda b: kept[b]["grad_branch"]),
        ],
        axis=1,
    )
    blocks = [grad_attn_w[:, b * block_width : (b + 1) * block_width] for b in range(tensor_count)]
    odd = (tensor_index & 1) == 1
    high = (tensor_index & 2) == 2
    sent = [jnp.where(odd, blocks[0], blocks[1]), jnp.where(odd, blocks[2], blocks[3])]
    mine = [jnp.where(odd, blocks[1], blocks[0]), jnp.where(odd, blocks[3], blocks[2])]
    came = near(jnp.stack(sent).astype(BF16)).astype(F32)
    low_sum, high_sum = mine[0] + came[0], mine[1] + came[1]
    came = far(jnp.where(high, low_sum, high_sum).astype(BF16)).astype(F32)
    quarter = (jnp.where(high, high_sum, low_sum) + came).astype(BF16)
    quarter = lax.psum_scatter(quarter, "dp", scatter_dimension=0, tiled=True)
    other = far(quarter)
    pair = jnp.stack([jnp.where(high, other, quarter), jnp.where(high, quarter, other)])
    other = near(pair)
    even_pair, odd_pair = jnp.where(odd, other, pair), jnp.where(odd, pair, other)
    grad_attn = jnp.concatenate(
        [even_pair[0], odd_pair[0], even_pair[1], odd_pair[1]], axis=1
    ).astype(F32)
    gains_own = lax.psum_scatter(
        lax.psum(grad_gains, "tensor"), "dp", scatter_dimension=1, tiled=True
    )
    return (
        jnp.stack(outputs)[:, None],
        jnp.stack(input_grads)[:, None],
        gains_own[0],
        gains_own[1],
        grad_attn[:, :query_width],
        grad_attn[:, query_width : query_width + key_width],
        grad_attn[:, query_width + key_width : query_width + 2 * key_width],
        grad_gate_w,
        grad_up_w,
        grad_attn[:, query_width + 2 * key_width :],
        grad_down_w,
    )


def solution(mesh):
    in_specs = (
        P(None, "dp", "tensor", None),
        P(None, "dp"),
        P("dp"),
        P("dp"),
        P("dp", None),
        P("dp", None),
        P("dp", None),
        P("dp", "tensor"),
        P("dp", "tensor"),
        P("dp", None),
        P("tensor", "dp"),
        P(None, "dp", "tensor", None),
    )
    out_specs = (
        P(None, "dp", "tensor", None),
        P(None, "dp", "tensor", None),
        P("dp"),
        P("dp"),
        P("dp", None),
        P("dp", None),
        P("dp", None),
        P("dp", "tensor"),
        P("dp", "tensor"),
        P("dp", None),
        P("tensor", "dp"),
    )
    return jax.shard_map(shards, mesh=mesh, in_specs=in_specs, out_specs=out_specs, check_vma=False)
```

```python
import functools

import jax
import jax.numpy as jnp
from jax import lax
from jax.experimental import pallas as pl
from jax.experimental.pallas import tpu as pltpu
from jax.sharding import PartitionSpec as P

HEAD_SIZE = 64
EPSILON = 1e-05
ROPE_BASE = 10000.0
MASKED = -1e30
BF16 = jnp.bfloat16
F32 = jnp.float32

BLOCK_XOR = (0, 2, 1, 3)


def near(value):
    count = lax.axis_size("tensor")
    return lax.ppermute(value, "tensor", [(i, i ^ 1) for i in range(count)])


def far(value):
    count = lax.axis_size("tensor")
    return lax.ppermute(value, "tensor", [(i, i ^ 2) for i in range(count)])


def gather_rows(own):
    pair = jnp.concatenate([own, far(own)], axis=0)
    return jnp.concatenate([pair, near(pair)], axis=0)


def scatter_rows(partial):
    half = partial.shape[0] // 2
    quarter = half // 2
    kept = partial[:half].astype(F32) + near(partial[half:].astype(BF16)).astype(F32)
    return kept[:quarter] + far(kept[quarter:].astype(BF16)).astype(F32)


def dot(left_side, right_side):
    return jnp.dot(left_side, right_side, preferred_element_type=F32)


def contract_rows(left_side, right_side):
    return lax.dot_general(
        left_side, right_side, (((0,), (0,)), ((), ())), preferred_element_type=F32
    )


def contract_last(left_side, right_side):
    return lax.dot_general(
        left_side, right_side, (((1,), (1,)), ((), ())), preferred_element_type=F32
    )


def dot_nt(left_side, right_side):
    return lax.dot_general(
        left_side, right_side, (((1,), (1,)), ((), ())), preferred_element_type=F32
    )


def dot_nn(left_side, right_side):
    return lax.dot_general(
        left_side, right_side, (((1,), (0,)), ((), ())), preferred_element_type=F32
    )


def head_of(ref, index):
    return ref[:, index * HEAD_SIZE : (index + 1) * HEAD_SIZE]


def row_scale_of(values):
    return lax.rsqrt(jnp.mean(values * values, axis=-1, keepdims=True) + EPSILON)


def turn(values, cosine, sine):
    lane = lax.broadcasted_iota(jnp.int32, (values.shape[0], 128), 1)
    first_half = lane % HEAD_SIZE < HEAD_SIZE // 2
    parts = []
    for start in range(0, values.shape[1], 128):
        part = values[:, start : start + 128]
        later = pltpu.roll(part, 128 - HEAD_SIZE // 2, 1)
        earlier = pltpu.roll(part, HEAD_SIZE // 2, 1)
        parts.append(part * cosine + jnp.where(first_half, later, earlier) * sine)
    return jnp.concatenate(parts, axis=1)


def project_pairs_kernel(x_ref, gain_ref, cosine_ref, sine_ref, weight_ref, pair_ref, normed_ref):
    @pl.when(pl.program_id(0) == 0)
    def _():
        values = x_ref[...].astype(F32)
        normed_ref[...] = (values * row_scale_of(values) * gain_ref[...]).astype(BF16)

    product = dot_nn(normed_ref[...], weight_ref[...])

    @pl.when(pl.program_id(0) == 0)
    def _():
        pair_ref[...] = turn(product, cosine_ref[...], sine_ref[...]).astype(BF16)

    @pl.when(pl.program_id(0) == 1)
    def _():
        pair_ref[...] = product.astype(BF16)


def project_queries_kernel(normed_ref, cosine_ref, sine_ref, weight_ref, query_ref):
    product = dot_nn(normed_ref[...], weight_ref[...])
    turned = turn(product, cosine_ref[...], sine_ref[...])
    query_ref[...] = (turned * HEAD_SIZE ** (-0.5)).astype(BF16)


def chunk_spec(width, first):
    return pl.BlockSpec(
        (width, width // 3), lambda i: ((first + i) // 2, (first + i) % 2)
    )


def whole(shape):
    return pl.BlockSpec(shape, lambda i: (0,) * len(shape))


def cost(flops, *arrays):
    moved = sum(a.size * a.dtype.itemsize for a in arrays)
    return pl.CostEstimate(flops=int(flops), transcendentals=0, bytes_accessed=int(moved))


def project_pairs(x_rows, gain, cosine, sine, weights):
    rows, width = x_rows.shape
    third = width // 3
    return pl.pallas_call(
        project_pairs_kernel,
        grid=(2,),
        in_specs=[
            whole((rows, width)),
            whole((1, width)),
            whole((rows, 128)),
            whole((rows, 128)),
            chunk_spec(width, 3),
        ],
        out_specs=[pl.BlockSpec((rows, third), lambda i: (0, i)), whole((rows, width))],
        out_shape=[
            jax.ShapeDtypeStruct((rows, 2 * third), BF16),
            jax.ShapeDtypeStruct((rows, width), BF16),
        ],
        compiler_params=pltpu.CompilerParams(vmem_limit_bytes=40 << 20),
        cost_estimate=cost(4 * rows * width * third, x_rows, x_rows),
        name="project_pairs",
    )(x_rows, gain, cosine, sine, weights)


def project_queries(normed, cosine, sine, weights):
    rows, width = normed.shape
    third = width // 3
    return pl.pallas_call(
        project_queries_kernel,
        grid=(3,),
        in_specs=[
            whole((rows, width)),
            whole((rows, 128)),
            whole((rows, 128)),
            chunk_spec(width, 0),
        ],
        out_specs=pl.BlockSpec((rows, third), lambda i: (0, i)),
        out_shape=jax.ShapeDtypeStruct((rows, width), BF16),
        compiler_params=pltpu.CompilerParams(vmem_limit_bytes=40 << 20),
        cost_estimate=cost(6 * rows * width * third, normed, normed, normed),
        name="project_queries",
    )(normed, cosine, sine, weights)


def attend_kernel(group, counts, q_ref, k0, k1, k2, k3, v0, v1, v2, v3, o_ref):
    rows = q_ref.shape[0]
    k_refs, v_refs = (k0, k1, k2, k3), (v0, v1, v2, v3)
    row = lax.broadcasted_iota(jnp.int32, (rows, rows), 0)
    col = lax.broadcasted_iota(jnp.int32, (rows, rows), 1)
    allowed = [jnp.logical_and(col <= row, col < counts[0])]
    allowed += [col < counts[j] for j in range(1, 4)]
    allowed = [jnp.concatenate([a] * group, axis=0) for a in allowed]
    for pair in range(2):
        queries = jnp.concatenate([head_of(q_ref, pair * group + i) for i in range(group)], axis=0)
        scores = [
            jnp.where(allowed[j], dot_nt(queries, head_of(k_refs[j], pair)), MASKED)
            for j in range(4)
        ]
        top = functools.reduce(
            jnp.maximum, [jnp.max(s, axis=1, keepdims=True) for s in scores]
        )
        soft = [jnp.exp(s - top) for s in scores]
        total = functools.reduce(jnp.add, [jnp.sum(s, axis=1, keepdims=True) for s in soft])
        out = functools.reduce(
            jnp.add, [dot_nn(soft[j].astype(BF16), head_of(v_refs[j], pair)) for j in range(4)]
        )
        out = (out / total).astype(BF16)
        for i in range(group):
            start = (pair * group + i) * HEAD_SIZE
            o_ref[:, start : start + HEAD_SIZE] = out[i * rows : (i + 1) * rows]


def attend(counts, queries, pairs):
    rows, width = queries.shape
    key_heads = pairs[0].shape[1] // (2 * HEAD_SIZE)
    group = width // HEAD_SIZE // key_heads
    steps = key_heads // 2
    query_spec = pl.BlockSpec((rows, 2 * group * HEAD_SIZE), lambda i, c: (0, i))
    key_spec = pl.BlockSpec((rows, 2 * HEAD_SIZE), lambda i, c: (0, i))
    value_spec = pl.BlockSpec((rows, 2 * HEAD_SIZE), lambda i, c: (0, steps + i))
    return pl.pallas_call(
        functools.partial(attend_kernel, group),
        grid_spec=pltpu.PrefetchScalarGridSpec(
            num_scalar_prefetch=1,
            grid=(steps,),
            in_specs=[query_spec] + [key_spec] * 4 + [value_spec] * 4,
            out_specs=query_spec,
        ),
        out_shape=jax.ShapeDtypeStruct((rows, width), BF16),
        compiler_params=pltpu.CompilerParams(vmem_limit_bytes=48 << 20),
        cost_estimate=cost(4 * rows * 4 * rows * width, queries, queries, *pairs),
        name="attend",
    )(counts, queries, *pairs, *pairs)


def attend_back_kernel(
    group, counts, q_ref, g_ref, cos_ref, sin_ref,
    k0, k1, k2, k3, v0, v1, v2, v3, dq_ref, dk_ref, dv_ref, turned_ref,
):
    rows = q_ref.shape[0]
    half = HEAD_SIZE // 2
    keys = jnp.concatenate([k0[...], k1[...], k2[...], k3[...]], axis=0)
    values = jnp.concatenate([v0[...], v1[...], v2[...], v3[...]], axis=0)
    keys_t = keys.T
    row = lax.broadcasted_iota(jnp.int32, (rows, rows), 0)
    col = lax.broadcasted_iota(jnp.int32, (rows, rows), 1)
    allowed = [jnp.logical_and(row <= col, row < counts[0])]
    allowed += [row < counts[j] for j in range(1, 4)]
    allowed = jnp.concatenate([jnp.concatenate([a] * group, axis=1) for a in allowed], axis=0)
    key_grads, value_grads = [], []
    for pair in range(2):
        lanes = slice(pair * HEAD_SIZE, (pair + 1) * HEAD_SIZE)
        key, value = keys[:, lanes], values[:, lanes]
        queries = jnp.concatenate([head_of(q_ref, pair * group + i) for i in range(group)], axis=0)
        grads = jnp.concatenate([head_of(g_ref, pair * group + i) for i in range(group)], axis=0)
        scores = jnp.where(allowed, dot_nt(key, queries), MASKED)
        soft = jnp.exp(scores - jnp.max(scores, axis=0, keepdims=True))
        soft = soft * (1.0 / jnp.sum(soft, axis=0, keepdims=True))
        grad_soft = dot_nt(value, grads)
        both = soft * grad_soft
        grad_scores = (both - soft * jnp.sum(both, axis=0, keepdims=True)).astype(BF16)
        value_grads.append(dot_nn(soft.astype(BF16), grads))
        key_grads.append(dot_nn(grad_scores, queries))
        query_grad = dot_nn(keys_t[lanes, :], grad_scores) * HEAD_SIZE ** (-0.5)
        for i in range(group):
            part = query_grad[:, i * rows : (i + 1) * rows]
            first, second = part[:half], part[half:]
            start = (pair * group + i) * HEAD_SIZE
            turned_ref[start : start + half, :] = first * cos_ref[...] + second * sin_ref[...]
            turned_ref[start + half : start + HEAD_SIZE, :] = (
                second * cos_ref[...] - first * sin_ref[...]
            )
    dk_ref[...] = jnp.concatenate(key_grads, axis=1).astype(BF16)
    dv_ref[...] = jnp.concatenate(value_grads, axis=1).astype(BF16)
    dq_ref[...] = turned_ref[...].T.astype(BF16)


def attend_back(counts, queries, grads, cosine_t, sine_t, pairs):
    rows, width = queries.shape
    key_width = pairs[0].shape[1] // 2
    key_heads = key_width // HEAD_SIZE
    group = width // HEAD_SIZE // key_heads
    steps = key_heads // 2
    query_spec = pl.BlockSpec((rows, 2 * group * HEAD_SIZE), lambda i, c: (0, i))
    key_spec = pl.BlockSpec((rows, 2 * HEAD_SIZE), lambda i, c: (0, i))
    value_spec = pl.BlockSpec((rows, 2 * HEAD_SIZE), lambda i, c: (0, steps + i))
    table_spec = pl.BlockSpec(cosine_t.shape, lambda i, c: (0, 0))
    out_spec = pl.BlockSpec((4 * rows, 2 * HEAD_SIZE), lambda i, c: (0, i))
    return pl.pallas_call(
        functools.partial(attend_back_kernel, group),
        grid_spec=pltpu.PrefetchScalarGridSpec(
            num_scalar_prefetch=1,
            grid=(steps,),
            in_specs=[query_spec, query_spec, table_spec, table_spec]
            + [key_spec] * 4
            + [value_spec] * 4,
            out_specs=[query_spec, out_spec, out_spec],
            scratch_shapes=[pltpu.VMEM((2 * group * HEAD_SIZE, rows), F32)],
        ),
        out_shape=[
            jax.ShapeDtypeStruct((rows, width), BF16),
            jax.ShapeDtypeStruct((4 * rows, key_width), BF16),
            jax.ShapeDtypeStruct((4 * rows, key_width), BF16),
        ],
        compiler_params=pltpu.CompilerParams(vmem_limit_bytes=56 << 20),
        cost_estimate=cost(10 * rows * 4 * rows * width, queries, grads, queries, *pairs),
        name="attend_back",
    )(counts, queries, grads, cosine_t, sine_t, *pairs, *pairs)


def leave_kernel(x_ref, o_ref, gain_ref, w0, w1, w2, middle_ref, normed_ref):
    out = o_ref[...]
    added = jnp.concatenate([dot_nn(out, w[...]) for w in (w0, w1, w2)], axis=1)
    middle = x_ref[...].astype(F32) + added
    middle_ref[...] = middle
    normed_ref[...] = (middle * row_scale_of(middle) * gain_ref[...]).astype(BF16)


def out_specs_of(width):
    return [
        pl.BlockSpec((width, width // 3), lambda i, c=c: (c // 2, c % 2)) for c in (5, 6, 7)
    ]


def leave(x_rows, attended, gain, weights):
    rows, width = x_rows.shape
    return pl.pallas_call(
        leave_kernel,
        grid=(1,),
        in_specs=[whole((rows, width)), whole((rows, width)), whole((1, width))]
        + out_specs_of(width),
        out_specs=[whole((rows, width)), whole((rows, width))],
        out_shape=[
            jax.ShapeDtypeStruct((rows, width), F32),
            jax.ShapeDtypeStruct((rows, width), BF16),
        ],
        compiler_params=pltpu.CompilerParams(vmem_limit_bytes=40 << 20),
        cost_estimate=cost(2 * rows * width * width, x_rows, x_rows, x_rows),
        name="leave",
    )(x_rows, attended, gain, weights, weights, weights)


def enter_kernel(
    count, kept_ref, came_ref, middle_ref, cot_ref, gain_ref, w0, w1, w2,
    grad_middle_ref, branch_ref, out_ref, gain_grad_ref,
):
    rows, width = middle_ref.shape
    third = width // 3
    middle = middle_ref[...]
    grad_normed = kept_ref[...] + came_ref[...].astype(F32)
    scale = row_scale_of(middle)
    row = lax.broadcasted_iota(jnp.int32, (rows, width), 0)
    grad_row = jnp.where(row < count[0], cot_ref[...].astype(F32), 0.0)
    gain_grad = jnp.sum(grad_normed * middle * scale, axis=0, keepdims=True)
    gain_grad_ref[...] = jnp.broadcast_to(gain_grad, gain_grad_ref.shape)
    inner = grad_normed * gain_ref[...]
    grad_middle = grad_row + (
        scale * inner - middle * scale**3 * jnp.mean(inner * middle, axis=-1, keepdims=True)
    )
    grad_middle_ref[...] = grad_middle
    branch = grad_middle.astype(BF16)
    branch_ref[...] = branch
    weights = (w0, w1, w2)
    out = dot_nt(branch[:, :third], w0[...])
    for c in range(1, 3):
        out = out + dot_nt(branch[:, c * third : (c + 1) * third], weights[c][...])
    out_ref[...] = out.astype(BF16)


def enter(count, kept, came, middle, cot_rows, gain, weights):
    rows, width = middle.shape

    def spec(shape, block=(0, 0)):
        return pl.BlockSpec(shape, lambda i, c: block)

    full = spec((rows, width))
    weight_specs = [spec((width, width // 3), (c // 2, c % 2)) for c in (5, 6, 7)]
    return pl.pallas_call(
        enter_kernel,
        grid_spec=pltpu.PrefetchScalarGridSpec(
            num_scalar_prefetch=1,
            grid=(1,),
            in_specs=[full] * 4 + [spec((1, width))] + weight_specs,
            out_specs=[full, full, full, spec((8, width))],
        ),
        out_shape=[
            jax.ShapeDtypeStruct((rows, width), F32),
            jax.ShapeDtypeStruct((rows, width), BF16),
            jax.ShapeDtypeStruct((rows, width), BF16),
            jax.ShapeDtypeStruct((8, width), F32),
        ],
        compiler_params=pltpu.CompilerParams(vmem_limit_bytes=48 << 20),
        cost_estimate=cost(2 * rows * width * width, kept, middle, middle, cot_rows),
        name="enter",
    )(count, kept, came, middle, cot_rows, gain, weights, weights, weights)


def pairs_back_kernel(kept_ref, came_ref, cosine_ref, sine_ref, pair_ref):
    width = kept_ref.shape[1] // 2
    total = kept_ref[...].astype(F32) + came_ref[...].astype(F32)
    pair_ref[:, :width] = turn(total[:, :width], cosine_ref[...], -sine_ref[...]).astype(BF16)
    pair_ref[:, width:] = total[:, width:].astype(BF16)


def pairs_back(kept, came, cosine, sine):
    rows, width = kept.shape
    return pl.pallas_call(
        pairs_back_kernel,
        grid=(1,),
        in_specs=[whole((rows, width))] * 2 + [whole((rows, 128))] * 2,
        out_specs=whole((rows, width)),
        out_shape=jax.ShapeDtypeStruct((rows, width), BF16),
        cost_estimate=cost(0, kept, came, came),
        name="pairs_back",
    )(kept, came, cosine, sine)


def finish_kernel(
    x_ref, query_ref, pair_ref, middle_ref, gain_ref, w0, w1, w2, w3, w4, grad_ref, gain_grad_ref
):
    rows, width = x_ref.shape
    third = width // 3
    weights = (w0, w1, w2, w3, w4)
    grads = [query_ref[:, c * third : (c + 1) * third] for c in range(3)]
    grads += [pair_ref[:, :third], pair_ref[:, third:]]
    grad_normed = dot_nt(grads[0], w0[...])
    for c in range(1, 5):
        grad_normed = grad_normed + dot_nt(grads[c], weights[c][...])
    values = x_ref[...].astype(F32)
    scale = row_scale_of(values)
    gain_grad = jnp.sum(grad_normed * values * scale, axis=0, keepdims=True)
    gain_grad_ref[...] = jnp.broadcast_to(gain_grad, gain_grad_ref.shape)
    inner = grad_normed * gain_ref[...]
    grad_ref[...] = (
        middle_ref[...]
        + scale * inner
        - values * scale**3 * jnp.mean(inner * values, axis=-1, keepdims=True)
    ).astype(BF16)


def finish(x_rows, query_grads, pair_grads, grad_middle, gain, weights):
    rows, width = x_rows.shape
    weight_specs = [
        pl.BlockSpec((width, width // 3), lambda i, c=c: (c // 2, c % 2)) for c in range(5)
    ]
    return pl.pallas_call(
        finish_kernel,
        grid=(1,),
        in_specs=[
            whole((rows, width)),
            whole((rows, width)),
            whole(pair_grads.shape),
            whole((rows, width)),
            whole((1, width)),
        ]
        + weight_specs,
        out_specs=[whole((rows, width)), whole((8, width))],
        out_shape=[
            jax.ShapeDtypeStruct((rows, width), BF16),
            jax.ShapeDtypeStruct((8, width), F32),
        ],
        compiler_params=pltpu.CompilerParams(vmem_limit_bytes=48 << 20),
        cost_estimate=cost(10 * rows * width * width // 3, x_rows, query_grads, grad_middle),
        name="finish",
    )(x_rows, query_grads, pair_grads, grad_middle, gain, *([weights] * 5))


def shards(
    inputs,
    lengths,
    gain_attn,
    gain_mlp,
    w_query,
    key_weight,
    value_weight,
    w_gate,
    w_up,
    w_out,
    w_down,
    cotangent,
):
    micro = inputs.shape[0]
    row_share = inputs.shape[2]
    width = inputs.shape[3]
    tensor_count = lax.axis_size("tensor")
    tensor_index = lax.axis_index("tensor")
    query_width = w_query.shape[1]
    key_width = key_weight.shape[1]
    hidden_share = w_gate.shape[1]

    attn_local = jnp.concatenate([w_query, key_weight, value_weight, w_out], axis=1)
    attn_width = attn_local.shape[1]
    block_width = attn_width // tensor_count
    attn_quarter = lax.dynamic_slice_in_dim(attn_local, tensor_index * block_width, block_width, 1)
    attn_w = lax.all_gather(attn_quarter, ("tensor", "dp"), axis=0, tiled=True)
    mlp_local = jnp.concatenate([w_gate, w_up, w_down.T], axis=1)
    mlp_full = lax.all_gather(mlp_local, "dp", axis=0, tiled=True)
    gains = lax.all_gather(jnp.stack([gain_attn, gain_mlp]), "dp", axis=1, tiled=True).astype(F32)
    gain_one, gain_two = gains[0:1], gains[1:2]
    full_gate = mlp_full[:, :hidden_share]
    full_up = mlp_full[:, hidden_share : 2 * hidden_share]
    full_down_t = mlp_full[:, 2 * hidden_share :]

    query_pos = tensor_index * row_share + jnp.arange(row_share, dtype=jnp.int32)
    exponent = jnp.arange(HEAD_SIZE // 2, dtype=F32) * (2.0 / HEAD_SIZE)
    angles = query_pos.astype(F32)[:, None] * (ROPE_BASE ** (-exponent))[None, :]
    cosine, sine = jnp.cos(angles), jnp.sin(angles)
    cosine_t, sine_t = cosine.T, sine.T
    cosine = jnp.concatenate([cosine] * 4, axis=1)
    sine = jnp.concatenate([-sine, sine, -sine, sine], axis=1)

    def counts_of(b):
        counts = []
        for x in BLOCK_XOR:
            block = tensor_index ^ x
            count = jnp.clip(lengths[b, 0] - block * row_share, 0, row_share)
            counts.append(jnp.where(block <= tensor_index, count, 0))
        return jnp.stack(counts).astype(jnp.int32)

    counts = [counts_of(b) for b in range(micro)]
    valid_rows = [
        jnp.clip(lengths[b, 0] - tensor_index * row_share, 0, row_share).astype(jnp.int32)
        for b in range(micro)
    ]
    valids = [
        (jnp.arange(row_share, dtype=jnp.int32) < valid_rows[b])[:, None] for b in range(micro)
    ]

    grad_own = jnp.stack(
        [jnp.where(valids[b], cotangent[b, 0], jnp.zeros((), BF16)) for b in range(micro)]
    )
    grad_far = far(grad_own)
    grad_near = near(jnp.stack([grad_own, grad_far]))
    grad_ffn = [
        jnp.concatenate([grad_own[b], grad_far[b], grad_near[0, b], grad_near[1, b]], axis=0)
        for b in range(micro)
    ]

    x_rows = inputs[:, 0].reshape(micro * row_share, width)
    cosine_all = jnp.concatenate([cosine] * micro, axis=0)
    sine_all = jnp.concatenate([sine] * micro, axis=0)
    pairs_own, normed = project_pairs(x_rows, gain_one, cosine_all, sine_all, attn_w)
    queries = project_queries(normed, cosine_all, sine_all, attn_w)
    kept = []
    for b in range(micro):
        rows = slice(b * row_share, (b + 1) * row_share)
        own = pairs_own[rows]
        across = far(own)
        pairs = [own, across, near(own), near(across)]
        attended = attend(counts[b], queries[rows], pairs)
        middle, hidden_own = leave(x_rows[rows], attended, gain_two, attn_w)
        kept.append(
            dict(
                x_rows=x_rows[rows],
                normed=normed[rows],
                queries=queries[rows],
                pairs=pairs,
                attended=attended,
                middle=middle,
                hidden=gather_rows(hidden_own),
            )
        )

    for b in range(micro):
        k = kept[b]
        gate_proj = dot(k["hidden"], full_gate)
        up_proj = dot(k["hidden"], full_up)
        grad_act = dot(grad_ffn[b], full_down_t)
        sigmoid_gate = jax.nn.sigmoid(gate_proj)
        k["activated"] = (gate_proj * sigmoid_gate * up_proj).astype(BF16)
        k["grad_gate"] = (
            grad_act * up_proj * sigmoid_gate * (1.0 + gate_proj * (1.0 - sigmoid_gate))
        ).astype(BF16)
        k["grad_up"] = (grad_act * gate_proj * sigmoid_gate).astype(BF16)
        grad_partial = contract_last(k["grad_gate"], full_gate) + contract_last(
            k["grad_up"], full_up
        )
        half = 2 * row_share
        summed = grad_partial[:half] + near(grad_partial[half:].astype(BF16)).astype(F32)
        k["normed_kept"] = summed[:row_share]
        k["normed_came"] = far(summed[row_share:].astype(BF16))

    def total(left_side, right_side):
        parts = [contract_rows(left_side(b), right_side(b)) for b in range(micro)]
        return sum(parts[1:], parts[0])

    grad_mlp_w = jnp.concatenate(
        [
            total(lambda b: kept[b]["hidden"], lambda b: kept[b]["grad_gate"]).astype(BF16),
            total(lambda b: kept[b]["hidden"], lambda b: kept[b]["grad_up"]).astype(BF16),
            total(lambda b: grad_ffn[b], lambda b: kept[b]["activated"]).astype(BF16),
        ],
        axis=1,
    )
    grad_mlp_w, kept[0]["middle"] = lax.optimization_barrier((grad_mlp_w, kept[0]["middle"]))
    grad_mlp_w = lax.psum_scatter(grad_mlp_w, "dp", scatter_dimension=0, tiled=True)

    gain_two_grads = []
    for b in range(micro):
        k = kept[b]
        k["grad_middle"], k["grad_branch"], grad_att, gain_two_grad = enter(
            valid_rows[b][None],
            k["normed_kept"],
            k["normed_came"],
            k["middle"],
            cotangent[b, 0],
            gain_two,
            attn_w,
        )
        gain_two_grads.append(gain_two_grad[0:1])
        k["grad_queries"], key_part, value_part = attend_back(
            counts[b], k["queries"], grad_att, cosine_t, sine_t, k["pairs"]
        )
        half = 2 * row_share
        came = near(jnp.concatenate([key_part[half:], value_part[half:]], axis=1))
        summed = jnp.concatenate([key_part[:half], value_part[:half]], axis=1).astype(
            F32
        ) + came.astype(F32)
        k["grad_pairs"] = pairs_back(
            summed[:row_share], far(summed[row_share:].astype(BF16)), cosine, sine
        )

    outputs, input_grads, gain_one_grads = [], [], []
    for b in range(micro):
        k = kept[b]
        input_grad, gain_one_grad = finish(
            k["x_rows"], k["grad_queries"], k["grad_pairs"], k["grad_middle"], gain_one, attn_w
        )
        gain_one_grads.append(gain_one_grad[0:1])
        input_grads.append(input_grad)
        ffn_out = scatter_rows(contract_last(k["activated"], full_down_t))
        outputs.append(jnp.where(valids[b], k["middle"] + ffn_out, 0.0).astype(BF16))

    gain_part = jnp.concatenate(
        [sum(gain_one_grads[1:], gain_one_grads[0]), sum(gain_two_grads[1:], gain_two_grads[0])],
        axis=0,
    )
    gain_part = jnp.pad(gain_part.T, ((0, 0), (0, 126))).astype(BF16)
    third = key_width

    def pick(flag, first, second):
        return jnp.where(flag, first, second)

    odd = (tensor_index & 1) == 1
    high = (tensor_index & 2) == 2

    def halves(flag):
        low_block, left, right = [], [], []
        for b in range(micro):
            k = kept[b]
            grads = jnp.concatenate([k["grad_queries"], k["grad_pairs"]], axis=1)
            low_block.append(
                contract_rows(
                    k["normed"],
                    pick(flag, grads[:, block_width : 2 * block_width], grads[:, :block_width]),
                )
            )
            left.append(
                contract_rows(
                    pick(flag, k["attended"], k["normed"]),
                    pick(flag, k["grad_branch"][:, third : 2 * third], k["grad_pairs"][:, third:]),
                )
            )
            right.append(
                contract_rows(
                    k["attended"],
                    pick(flag, k["grad_branch"][:, 2 * third :], k["grad_branch"][:, :third]),
                )
            )
        left, right = sum(left[1:], left[0]), sum(right[1:], right[0])
        return jnp.stack(
            [
                sum(low_block[1:], low_block[0]).astype(BF16),
                jnp.concatenate([left, right], axis=1).astype(BF16),
            ]
        )

    summed = halves(odd).astype(F32) + near(halves(jnp.logical_not(odd))).astype(F32)
    came = far(pick(high, summed[0], summed[1]).astype(BF16)).astype(F32)
    quarter = (pick(high, summed[1], summed[0]) + came).astype(BF16)
    quarter = jnp.concatenate([quarter, gain_part], axis=1)
    quarter, grad_mlp_w = lax.optimization_barrier((quarter, grad_mlp_w))
    quarter = lax.psum_scatter(quarter, "dp", scatter_dimension=0, tiled=True)
    other = far(quarter)
    pair = jnp.stack([pick(high, other, quarter), pick(high, quarter, other)])
    other = near(pair)
    even_pair, odd_pair = pick(odd, other, pair), pick(odd, pair, other)
    blocks = [even_pair[0], odd_pair[0], even_pair[1], odd_pair[1]]
    grad_attn = jnp.concatenate([p[:, :block_width] for p in blocks], axis=1).astype(F32)
    gain_sum = sum(p[:, block_width : block_width + 2].astype(F32) for p in blocks)
    grad_mlp_w = grad_mlp_w.astype(F32)
    return (
        jnp.stack(outputs)[:, None],
        jnp.stack(input_grads)[:, None],
        gain_sum[:, 0],
        gain_sum[:, 1],
        grad_attn[:, :query_width],
        grad_attn[:, query_width : query_width + key_width],
        grad_attn[:, query_width + key_width : query_width + 2 * key_width],
        grad_mlp_w[:, :hidden_share],
        grad_mlp_w[:, hidden_share : 2 * hidden_share],
        grad_attn[:, query_width + 2 * key_width :],
        grad_mlp_w[:, 2 * hidden_share :].T,
    )


def solution(mesh):
    in_specs = (
        P(None, "dp", "tensor", None),
        P(None, "dp"),
        P("dp"),
        P("dp"),
        P("dp", None),
        P("dp", None),
        P("dp", None),
        P("dp", "tensor"),
        P("dp", "tensor"),
        P("dp", None),
        P("tensor", "dp"),
        P(None, "dp", "tensor", None),
    )
    out_specs = (
        P(None, "dp", "tensor", None),
        P(None, "dp", "tensor", None),
        P("dp"),
        P("dp"),
        P("dp", None),
        P("dp", None),
        P("dp", None),
        P("dp", "tensor"),
        P("dp", "tensor"),
        P("dp", None),
        P("tensor", "dp"),
    )
    return jax.shard_map(shards, mesh=mesh, in_specs=in_specs, out_specs=out_specs, check_vma=False)
```

```python
import functools

import jax
import jax.numpy as jnp
from jax import lax
from jax.experimental import pallas as pl
from jax.experimental.layout import Layout, with_layout_constraint
from jax.experimental.pallas import tpu as pltpu
from jax.sharding import PartitionSpec as P

HEAD_SIZE = 64
EPSILON = 1e-05
ROPE_BASE = 10000.0
MASKED = -1e30
BF16 = jnp.bfloat16
F32 = jnp.float32

BLOCK_XOR = (0, 2, 1, 3)


def near(value):
    count = lax.axis_size("tensor")
    return lax.ppermute(value, "tensor", [(i, i ^ 1) for i in range(count)])


def far(value):
    count = lax.axis_size("tensor")
    return lax.ppermute(value, "tensor", [(i, i ^ 2) for i in range(count)])


def scatter_rows(partial):
    half = partial.shape[0] // 2
    quarter = half // 2
    kept = partial[:half].astype(F32) + near(partial[half:].astype(BF16)).astype(F32)
    return kept[:quarter] + far(kept[quarter:].astype(BF16)).astype(F32)


def dot(left_side, right_side):
    return jnp.dot(left_side, right_side, preferred_element_type=F32)


def contract_rows(left_side, right_side):
    return lax.dot_general(
        left_side, right_side, (((0,), (0,)), ((), ())), preferred_element_type=F32
    )


def contract_last(left_side, right_side):
    return lax.dot_general(
        left_side, right_side, (((1,), (1,)), ((), ())), preferred_element_type=F32
    )


def dot_nt(left_side, right_side):
    return lax.dot_general(
        left_side, right_side, (((1,), (1,)), ((), ())), preferred_element_type=F32
    )


def dot_nn(left_side, right_side):
    return lax.dot_general(
        left_side, right_side, (((1,), (0,)), ((), ())), preferred_element_type=F32
    )


def head_of(ref, index):
    return ref[:, index * HEAD_SIZE : (index + 1) * HEAD_SIZE]


def row_scale_of(values):
    return lax.rsqrt(jnp.mean(values * values, axis=-1, keepdims=True) + EPSILON)


def turn(values, cosine, sine):
    lane = lax.broadcasted_iota(jnp.int32, (values.shape[0], 128), 1)
    first_half = lane % HEAD_SIZE < HEAD_SIZE // 2
    parts = []
    for start in range(0, values.shape[1], 128):
        part = values[:, start : start + 128]
        later = pltpu.roll(part, 128 - HEAD_SIZE // 2, 1)
        earlier = pltpu.roll(part, HEAD_SIZE // 2, 1)
        parts.append(part * cosine + jnp.where(first_half, later, earlier) * sine)
    return jnp.concatenate(parts, axis=1)


PAIR_CHUNKS = ((0, 0), (1, 0))
QUERY_CHUNKS = ((0, 1), (1, 1), (2, 1))
OUT_CHUNKS = ((3, 1), (2, 0), (3, 0))


def call(kernel, name, arrays, specs, outs, out_specs, flops=0, scalars=(), aliases=None, **more):
    moved = sum(x.size * x.dtype.itemsize for x in (*arrays, *jax.tree.leaves(outs)))
    return pl.pallas_call(
        kernel,
        grid_spec=pltpu.PrefetchScalarGridSpec(
            num_scalar_prefetch=len(scalars),
            grid=more.get("grid", (1,)),
            in_specs=specs,
            out_specs=out_specs,
            scratch_shapes=more.get("scratch", ()),
        ),
        out_shape=outs,
        input_output_aliases=aliases or {},
        compiler_params=pltpu.CompilerParams(vmem_limit_bytes=52 << 20),
        cost_estimate=pl.CostEstimate(flops=1, transcendentals=0, bytes_accessed=1),
        name=name,
    )(*scalars, *arrays)


def block(shape, at=(0, 0)):
    return pl.BlockSpec(shape, lambda *_: at)


def chunk_specs(width, chunks):
    return [block((width, width // 3), c) for c in chunks]


def array(shape, kind=BF16):
    return jax.ShapeDtypeStruct(shape, kind)


ANY = pl.BlockSpec(memory_space=pl.ANY)


def project_pairs_kernel(x_ref, gain_ref, cosine_ref, sine_ref, wk, wv, pair_ref, normed_ref):
    values = x_ref[...].astype(F32)
    normed = (values * row_scale_of(values) * gain_ref[...]).astype(BF16)
    normed_ref[...] = normed
    keys = turn(dot_nn(normed, wk[...]), cosine_ref[...], sine_ref[...]).astype(BF16)
    values = dot_nn(normed, wv[...]).astype(BF16)
    for i in range(keys.shape[1] // 128):
        pair_ref[:, 256 * i : 256 * i + 128] = keys[:, 128 * i : 128 * (i + 1)]
        pair_ref[:, 256 * i + 128 : 256 * (i + 1)] = values[:, 128 * i : 128 * (i + 1)]


def project_pairs(x_rows, gain, cosine, sine, weights):
    rows, width = x_rows.shape
    pair_width = 2 * (width // 3)
    return call(
        project_pairs_kernel,
        "project_pairs",
        (x_rows, gain, cosine, sine, weights, weights),
        [block(x.shape) for x in (x_rows, gain, cosine, sine)] + chunk_specs(width, PAIR_CHUNKS),
        [array((rows, pair_width)), array((rows, width))],
        [block((rows, pair_width)), block((rows, width))],
        2 * rows * width * pair_width,
    )


def project_queries_kernel(normed_ref, cosine_ref, sine_ref, w0, w1, w2, query_ref):
    third = w0.shape[1]
    for i, w in enumerate((w0, w1, w2)):
        turned = turn(dot_nn(normed_ref[...], w[...]), cosine_ref[...], sine_ref[...])
        query_ref[:, i * third : (i + 1) * third] = (turned * HEAD_SIZE ** (-0.5)).astype(BF16)


def project_queries(normed, cosine, sine, weights):
    rows, width = normed.shape
    return call(
        project_queries_kernel,
        "project_queries",
        (normed, cosine, sine, weights, weights, weights),
        [block(x.shape) for x in (normed, cosine, sine)] + chunk_specs(width, QUERY_CHUNKS),
        array((rows, width)),
        block((rows, width)),
        2 * rows * width * width,
    )


def attend_kernel(group, counts, q_ref, p0, p1, p2, p3, *rest):
    o_ref = rest[-1]
    rows = q_ref.shape[0]
    refs = (p0, p1, p2, p3)
    row = lax.broadcasted_iota(jnp.int32, (rows, rows), 0)
    col = lax.broadcasted_iota(jnp.int32, (rows, rows), 1)
    allowed = [jnp.logical_and(col <= row, col < counts[0])]
    allowed += [col < counts[j] for j in range(1, 4)]
    allowed = [jnp.concatenate([a] * group, axis=0) for a in allowed]
    for pair in range(2):
        queries = jnp.concatenate([head_of(q_ref, pair * group + i) for i in range(group)], axis=0)
        scores = [
            jnp.where(allowed[j], dot_nt(queries, head_of(refs[j], pair)), MASKED)
            for j in range(4)
        ]
        top = functools.reduce(jnp.maximum, [jnp.max(s, axis=1, keepdims=True) for s in scores])
        soft = [jnp.exp(s - top) for s in scores]
        total = functools.reduce(jnp.add, [jnp.sum(s, axis=1, keepdims=True) for s in soft])
        out = functools.reduce(
            jnp.add, [dot_nn(soft[j].astype(BF16), head_of(refs[j], 2 + pair)) for j in range(4)]
        )
        out = (out / total).astype(BF16)
        for i in range(group):
            start = (pair * group + i) * HEAD_SIZE
            o_ref[:, start : start + HEAD_SIZE] = out[i * rows : (i + 1) * rows]


def attention_sizes(queries, pairs_own):
    rows = queries.shape[0] // 2
    steps = pairs_own.shape[1] // (4 * HEAD_SIZE)
    group = queries.shape[1] // (2 * HEAD_SIZE * steps)
    return rows, steps, group


def attend(b, counts, queries, pairs_own, others, earlier):
    rows, steps, group = attention_sizes(queries, pairs_own)
    width = queries.shape[1]
    query_spec = pl.BlockSpec((rows, width // steps), lambda i, c: (b, i))
    own_spec = pl.BlockSpec((rows, 4 * HEAD_SIZE), lambda i, c: (b, i))
    pair_spec = pl.BlockSpec((rows, 4 * HEAD_SIZE), lambda i, c: (0, i))
    more = [] if earlier is None else [earlier]
    return call(
        functools.partial(attend_kernel, group),
        "attend",
        (queries, pairs_own, *others, *more),
        [query_spec, own_spec] + [pair_spec] * 3 + [ANY] * len(more),
        array(queries.shape),
        query_spec,
        16 * rows * rows * width,
        (counts,),
        {6: 0} if more else None,
        grid=(steps,),
    )


def attend_back_kernel(group, counts, q_ref, g_ref, cos_ref, sin_ref, p0, p1, p2, p3, *rest):
    dq_ref, kept_ref, sent_ref, turned_ref = rest[-4:]
    rows = q_ref.shape[0]
    half = HEAD_SIZE // 2
    both = jnp.concatenate([p0[...], p1[...], p2[...], p3[...]], axis=0)
    keys, values = both[:, :128], both[:, 128:]
    keys_t = keys.T
    row = lax.broadcasted_iota(jnp.int32, (rows, rows), 0)
    col = lax.broadcasted_iota(jnp.int32, (rows, rows), 1)
    allowed = [jnp.logical_and(row <= col, row < counts[0])]
    allowed += [row < counts[j] for j in range(1, 4)]
    allowed = jnp.concatenate([jnp.concatenate([a] * group, axis=1) for a in allowed], axis=0)
    key_grads, value_grads = [], []
    for pair in range(2):
        lanes = slice(pair * HEAD_SIZE, (pair + 1) * HEAD_SIZE)
        key, value = keys[:, lanes], values[:, lanes]
        queries = jnp.concatenate([head_of(q_ref, pair * group + i) for i in range(group)], axis=0)
        grads = jnp.concatenate([head_of(g_ref, pair * group + i) for i in range(group)], axis=0)
        scores = jnp.where(allowed, dot_nt(key, queries), MASKED)
        soft = jnp.exp(scores - jnp.max(scores, axis=0, keepdims=True))
        soft = soft * (1.0 / jnp.sum(soft, axis=0, keepdims=True))
        grad_soft = dot_nt(value, grads)
        scaled = soft * grad_soft
        grad_scores = (scaled - soft * jnp.sum(scaled, axis=0, keepdims=True)).astype(BF16)
        value_grads.append(dot_nn(soft.astype(BF16), grads))
        key_grads.append(dot_nn(grad_scores, queries))
        query_grad = dot_nn(keys_t[lanes, :], grad_scores) * HEAD_SIZE ** (-0.5)
        for i in range(group):
            part = query_grad[:, i * rows : (i + 1) * rows]
            first, second = part[:half], part[half:]
            start = (pair * group + i) * HEAD_SIZE
            turned_ref[start : start + half, :] = first * cos_ref[...] + second * sin_ref[...]
            turned_ref[start + half : start + HEAD_SIZE, :] = (
                second * cos_ref[...] - first * sin_ref[...]
            )
    grads = jnp.concatenate(key_grads + value_grads, axis=1).astype(BF16)
    kept_ref[...] = grads[: 2 * rows]
    sent_ref[...] = grads[2 * rows :]
    dq_ref[...] = turned_ref[...].T.astype(BF16)


def attend_back(b, counts, queries, grads, cosine_t, sine_t, pairs_own, others, earlier):
    rows, steps, group = attention_sizes(queries, pairs_own)
    width = queries.shape[1]
    query_spec = pl.BlockSpec((rows, width // steps), lambda i, c: (b, i))
    grad_spec = pl.BlockSpec((rows, width // steps), lambda i, c: (0, i))
    own_spec = pl.BlockSpec((rows, 4 * HEAD_SIZE), lambda i, c: (b, i))
    pair_spec = pl.BlockSpec((rows, 4 * HEAD_SIZE), lambda i, c: (0, i))
    half_spec = pl.BlockSpec((2 * rows, 4 * HEAD_SIZE), lambda i, c: (0, i))
    more = [] if earlier is None else [earlier]
    return call(
        functools.partial(attend_back_kernel, group),
        "attend_back",
        (queries, grads, cosine_t, sine_t, pairs_own, *others, *more),
        [query_spec, grad_spec, block(cosine_t.shape), block(sine_t.shape), own_spec]
        + [pair_spec] * 3
        + [ANY] * len(more),
        [array(queries.shape)] + [array((2 * rows, pairs_own.shape[1]))] * 2,
        [query_spec, half_spec, half_spec],
        40 * rows * rows * width,
        (counts,),
        {9: 0} if more else None,
        grid=(steps,),
        scratch=[pltpu.VMEM((width // steps, rows), F32)],
    )


def leave_kernel(x_ref, o_ref, gain_ref, w0, w1, w2, middle_ref, normed_ref):
    out = o_ref[...]
    added = jnp.concatenate([dot_nn(out, w[...]) for w in (w0, w1, w2)], axis=1)
    middle = x_ref[...].astype(F32) + added
    middle_ref[...] = middle
    normed_ref[...] = (middle * row_scale_of(middle) * gain_ref[...]).astype(BF16)


def leave(b, x_rows, attended, gain, weights):
    rows, width = x_rows.shape[0] // 2, x_rows.shape[1]
    here = block((rows, width), (b, 0))
    return call(
        leave_kernel,
        "leave",
        (x_rows, attended, gain, weights, weights, weights),
        [here, here, block(gain.shape)] + chunk_specs(width, OUT_CHUNKS),
        [array((rows, width), F32), array((rows, width))],
        [block((rows, width))] * 2,
        2 * rows * width * width,
    )


def enter_kernel(
    count, part_ref, near_ref, far_ref, middle_ref, cot_ref, gain_ref, w0, w1, w2, *rest
):
    grad_middle_ref, branch_ref, out_ref, gain_grad_ref = rest[-4:]
    rows, width = middle_ref.shape
    third = width // 3
    middle = middle_ref[...]
    grad_normed = part_ref[...] + near_ref[...].astype(F32) + far_ref[...].astype(F32)
    scale = row_scale_of(middle)
    row = lax.broadcasted_iota(jnp.int32, (rows, width), 0)
    grad_row = jnp.where(row < count[0], cot_ref[...].astype(F32), 0.0)
    gain_grad = jnp.sum(grad_normed * middle * scale, axis=0, keepdims=True)
    gain_grad_ref[...] = jnp.broadcast_to(gain_grad, gain_grad_ref.shape)
    inner = grad_normed * gain_ref[...]
    grad_middle = grad_row + (
        scale * inner - middle * scale**3 * jnp.mean(inner * middle, axis=-1, keepdims=True)
    )
    grad_middle_ref[...] = grad_middle
    branch = grad_middle.astype(BF16)
    branch_ref[...] = branch
    weights = (w0, w1, w2)
    out = dot_nt(branch[:, :third], w0[...])
    for c in range(1, 3):
        out = out + dot_nt(branch[:, c * third : (c + 1) * third], weights[c][...])
    out_ref[...] = out.astype(BF16)


def enter(b, count, part, near_part, far_part, middle, cot_rows, gain, weights, earlier):
    rows, width = middle.shape
    full, here = block((rows, width)), block((rows, width), (b, 0))
    more = [] if earlier is None else [earlier]
    return call(
        enter_kernel,
        "enter",
        (part, near_part, far_part, middle, cot_rows, gain, weights, weights, weights, *more),
        [full, full, full, full, here, block(gain.shape)]
        + chunk_specs(width, OUT_CHUNKS)
        + [ANY] * len(more),
        [
            array((rows, width), F32),
            array((2 * rows, width)),
            array((rows, width)),
            array((8, width), F32),
        ],
        [full, here, full, block((8, width))],
        2 * rows * width * width,
        (count,),
        {10: 1} if more else None,
    )


def pairs_back_kernel(kept_ref, near_ref, far_ref, cosine_ref, sine_ref, *rest):
    pair_ref = rest[-1]
    width = pair_ref.shape[1] // 2
    for i in range(width // 128):
        lanes = slice(256 * i, 256 * (i + 1))
        total = (
            kept_ref[:, lanes].astype(F32)
            + near_ref[:, lanes].astype(F32)
            + far_ref[:, lanes].astype(F32)
        )
        turned = turn(total[:, :128], cosine_ref[...], -sine_ref[...])
        pair_ref[:, 128 * i : 128 * (i + 1)] = turned.astype(BF16)
        pair_ref[:, width + 128 * i : width + 128 * (i + 1)] = total[:, 128:].astype(BF16)


def pairs_back(b, kept, near_part, far_part, cosine, sine, earlier):
    rows, width = far_part.shape
    first = block((rows, width))
    table = block((rows, 128))
    more = [] if earlier is None else [earlier]
    return call(
        pairs_back_kernel,
        "pairs_back",
        (kept, near_part, far_part, cosine, sine, *more),
        [first, first, first, table, table] + [ANY] * len(more),
        array((2 * rows, width)),
        block((rows, width), (b, 0)),
        aliases={5: 0} if more else None,
    )


def finish_kernel(
    x_ref, query_ref, pair_ref, middle_ref, gain_ref, wk, wv, w0, w1, w2, grad_ref, gain_grad_ref
):
    third = x_ref.shape[1] // 3
    grads = [pair_ref[:, :third], pair_ref[:, third:]]
    grads += [query_ref[:, c * third : (c + 1) * third] for c in range(3)]
    grad_normed = dot_nt(grads[0], wk[...])
    for grad, w in zip(grads[1:], (wv, w0, w1, w2)):
        grad_normed = grad_normed + dot_nt(grad, w[...])
    values = x_ref[...].astype(F32)
    scale = row_scale_of(values)
    gain_grad = jnp.sum(grad_normed * values * scale, axis=0, keepdims=True)
    gain_grad_ref[...] = jnp.broadcast_to(gain_grad, gain_grad_ref.shape)
    inner = grad_normed * gain_ref[...]
    grad_ref[...] = (
        middle_ref[...]
        + scale * inner
        - values * scale**3 * jnp.mean(inner * values, axis=-1, keepdims=True)
    ).astype(BF16)


def finish(b, x_rows, query_grads, pair_grads, grad_middle, gain, weights):
    rows, width = grad_middle.shape
    here = block((rows, width), (b, 0))
    return call(
        finish_kernel,
        "finish",
        (x_rows, query_grads, pair_grads, grad_middle, gain, *([weights] * 5)),
        [here, here, block((rows, pair_grads.shape[1]), (b, 0)), block((rows, width))]
        + [block(gain.shape)]
        + chunk_specs(width, PAIR_CHUNKS + QUERY_CHUNKS),
        [array((rows, width)), array((8, width), F32)],
        [block((rows, width)), block((8, width))],
        10 * rows * width * width // 3,
    )


def row_major(value):
    return with_layout_constraint(value, Layout(major_to_minor=tuple(range(value.ndim))))


def pick(flag, first, second):
    return jnp.where(flag, first, second)


def sum_over_data(part_a, part_b, extra):
    data_count = lax.axis_size("dp")
    data_index = lax.axis_index("dp")
    columns = part_a[0].shape[1]

    def split(value):
        return value.reshape(data_count, -1, columns)

    if data_count != 8:
        total = part_a[0] + far(part_a[1].astype(BF16)).astype(F32)
        other = part_b[0] + far(part_b[1].astype(BF16)).astype(F32)
        rows = jnp.concatenate([split(total), split(other), extra], axis=1).astype(BF16)
        rows = lax.psum_scatter(rows, "dp", scatter_dimension=0, tiled=True)[0].astype(F32)
        share = total.shape[0] // data_count
        return rows[:share], rows[share : 2 * share], rows[2 * share :]

    groups = data_count // 2
    odd = (data_index & 1) == 1
    group = data_index // 2

    def beside(value):
        even_rows, odd_rows = value[..., 0, :, :], value[..., 1, :, :]
        sent = pick(odd, even_rows, odd_rows).astype(BF16)
        came = lax.ppermute(sent, "dp", [(i, i ^ 1) for i in range(data_count)])
        return pick(odd, odd_rows, even_rows).astype(F32) + came.astype(F32)

    def along(value):
        low = value.astype(BF16)
        total = lax.dynamic_index_in_dim(value, group, 0, keepdims=False)
        for step in range(1, groups):
            sent = lax.dynamic_index_in_dim(low, (group + step) % groups, 0, keepdims=False)
            moves = [(i, (i + 2 * step) % data_count) for i in range(data_count)]
            total = total + lax.ppermute(sent, "dp", moves).astype(F32)
        return total

    second = jnp.stack([split(p) for p in part_b], axis=0)
    second = beside(second.reshape(2, groups, 2, -1, columns))
    first = split(part_a[0] + far(part_a[1].astype(BF16)).astype(F32))
    first = jnp.concatenate([first, extra], axis=1).reshape(groups, 2, -1, columns)
    first = beside(first)
    second = along(jnp.moveaxis(second, 1, 0))
    first = along(first)
    second = second[0] + far(second[1].astype(BF16)).astype(F32)
    share = second.shape[0]
    return first[:share], second, first[share:]


def shards(
    inputs,
    lengths,
    gain_attn,
    gain_mlp,
    w_query,
    key_weight,
    value_weight,
    w_gate,
    w_up,
    w_out,
    w_down,
    cotangent,
):
    micro = inputs.shape[0]
    row_share = inputs.shape[2]
    width = inputs.shape[3]
    tensor_count = lax.axis_size("tensor")
    tensor_index = lax.axis_index("tensor")
    hidden_share = w_gate.shape[1]

    third = width // 3

    out_parts = [w_out[:, c * third : (c + 1) * third] for c in range(3)]
    query_parts = [w_query[:, c * third : (c + 1) * third] for c in range(3)]
    attn_quarter = lax.select_n(
        tensor_index,
        jnp.concatenate([key_weight, query_parts[0]], axis=1),
        jnp.concatenate([value_weight, query_parts[1]], axis=1),
        jnp.concatenate([out_parts[1], query_parts[2]], axis=1),
        jnp.concatenate([out_parts[2], out_parts[0]], axis=1),
    )
    attn_w = lax.all_gather(attn_quarter, ("tensor", "dp"), axis=0, tiled=True)
    mlp_local = jnp.concatenate([w_gate, w_up, w_down.T], axis=1)
    mlp_full = lax.all_gather(mlp_local, "dp", axis=0, tiled=True)
    gains = lax.all_gather(jnp.stack([gain_attn, gain_mlp]), "dp", axis=1, tiled=True).astype(F32)
    gain_one, gain_two = gains[0:1], gains[1:2]

    query_pos = tensor_index * row_share + jnp.arange(row_share, dtype=jnp.int32)
    exponent = jnp.arange(HEAD_SIZE // 2, dtype=F32) * (2.0 / HEAD_SIZE)
    angles = query_pos.astype(F32)[:, None] * (ROPE_BASE ** (-exponent))[None, :]
    cosine, sine = jnp.cos(angles), jnp.sin(angles)
    cosine_t, sine_t = cosine.T, sine.T
    cosine = jnp.concatenate([cosine] * 4, axis=1)
    sine = jnp.concatenate([-sine, sine, -sine, sine], axis=1)

    def counts_of(b):
        counts = []
        for x in BLOCK_XOR:
            block = tensor_index ^ x
            count = jnp.clip(lengths[b, 0] - block * row_share, 0, row_share)
            counts.append(jnp.where(block <= tensor_index, count, 0))
        return jnp.stack(counts).astype(jnp.int32)

    counts = [counts_of(b) for b in range(micro)]
    valid_rows = [
        jnp.clip(lengths[b, 0] - tensor_index * row_share, 0, row_share).astype(jnp.int32)
        for b in range(micro)
    ]
    valids = [
        (jnp.arange(row_share, dtype=jnp.int32) < valid_rows[b])[:, None] for b in range(micro)
    ]

    grad_own = jnp.stack(
        [jnp.where(valids[b], cotangent[b, 0], jnp.zeros((), BF16)) for b in range(micro)]
    )
    grad_far = far(grad_own)
    grad_near = near(jnp.stack([grad_own, grad_far]))
    grad_ffn = [
        jnp.concatenate([grad_own[b], grad_far[b], grad_near[0, b], grad_near[1, b]], axis=0)
        for b in range(micro)
    ]

    x_rows = inputs[:, 0].reshape(micro * row_share, width)
    cot_rows = cotangent[:, 0].reshape(micro * row_share, width)
    cosine_all = jnp.concatenate([cosine] * micro, axis=0)
    sine_all = jnp.concatenate([sine] * micro, axis=0)
    pairs_own, normed = project_pairs(x_rows, gain_one, cosine_all, sine_all, attn_w)
    queries = project_queries(normed, cosine_all, sine_all, attn_w)
    kept = []
    attended = None
    for b in range(micro):
        own = pairs_own[b * row_share : (b + 1) * row_share]
        across = far(own)
        others = [across, near(own), near(across)]
        attended = attend(b, counts[b], queries, pairs_own, others, attended)
        middle, hidden_own = leave(b, x_rows, attended, gain_two, attn_w)
        across = far(hidden_own)
        half = jnp.concatenate([hidden_own, across], axis=0)
        hidden = jnp.concatenate([half, near(half)], axis=0)
        kept.append(dict(others=others, middle=middle, hidden=hidden))
        if b == micro - 1:
            mlp_full, _ = lax.optimization_barrier((mlp_full, across))

    full_gate = mlp_full[:, :hidden_share]
    full_up = mlp_full[:, hidden_share : 2 * hidden_share]
    full_down_t = mlp_full[:, 2 * hidden_share :]
    for b in range(micro):
        k = kept[b]
        gate_proj = dot(k["hidden"], full_gate)
        up_proj = dot(k["hidden"], full_up)
        grad_act = dot(grad_ffn[b], full_down_t)
        sigmoid_gate = jax.nn.sigmoid(gate_proj)
        k["activated"] = (gate_proj * sigmoid_gate * up_proj).astype(BF16)
        k["grad_gate"] = (
            grad_act * up_proj * sigmoid_gate * (1.0 + gate_proj * (1.0 - sigmoid_gate))
        ).astype(BF16)
        k["grad_up"] = (grad_act * gate_proj * sigmoid_gate).astype(BF16)
        k["part"] = contract_last(k["grad_gate"], full_gate) + contract_last(k["grad_up"], full_up)
        k["near_part"] = near(k["part"][2 * row_share :].astype(BF16))
        k["far_part"] = far(
            (
                k["part"][row_share : 2 * row_share] + k["near_part"][row_share:].astype(F32)
            ).astype(BF16)
        )

    def total(left_side, right_side):
        parts = [contract_rows(left_side(b), right_side(b)) for b in range(micro)]
        return row_major(sum(parts[1:], parts[0]).astype(BF16))

    grad_mlp_w = row_major(
        jnp.concatenate(
            [
                total(lambda b: kept[b]["hidden"], lambda b: kept[b]["grad_gate"]),
                total(lambda b: kept[b]["hidden"], lambda b: kept[b]["grad_up"]),
                total(lambda b: grad_ffn[b], lambda b: kept[b]["activated"]),
            ],
            axis=1,
        )
    )
    grad_mlp_w, kept[0]["middle"] = lax.optimization_barrier((grad_mlp_w, kept[0]["middle"]))

    gain_two_grads = []
    branch = query_grads = pair_grads = None

    def backward(b, branch, query_grads):
        k = kept[b]
        k["grad_middle"], branch, grad_att, gain_two_grad = enter(
            b,
            valid_rows[b][None],
            k["part"],
            k["near_part"],
            k["far_part"],
            k["middle"],
            cot_rows,
            gain_two,
            attn_w,
            branch,
        )
        gain_two_grads.append(gain_two_grad[0:1])
        query_grads, k["pair_kept"], k["pair_sent"] = attend_back(
            b, counts[b], queries, grad_att, cosine_t, sine_t, pairs_own, k["others"], query_grads
        )
        return branch, query_grads

    grad_mlp_w = lax.psum_scatter(grad_mlp_w, "dp", scatter_dimension=0, tiled=True)
    for b in range(micro):
        branch, query_grads = backward(b, branch, query_grads)
    for b in range(micro):
        k = kept[b]
        near_pair = near(k["pair_sent"])
        far_pair = far(
            (k["pair_kept"][row_share:].astype(F32) + near_pair[row_share:].astype(F32)).astype(
                BF16
            )
        )
        pair_grads = pairs_back(b, k["pair_kept"], near_pair, far_pair, cosine, sine, pair_grads)

    outputs, input_grads, gain_one_grads = [], [], []
    for b in range(micro):
        k = kept[b]
        input_grad, gain_one_grad = finish(
            b, x_rows, query_grads, pair_grads, k["grad_middle"], gain_one, attn_w
        )
        gain_one_grads.append(gain_one_grad[0:1])
        input_grads.append(input_grad)
        ffn_out = scatter_rows(contract_last(k["activated"], full_down_t))
        outputs.append(jnp.where(valids[b], k["middle"] + ffn_out, 0.0).astype(BF16))

    odd = (tensor_index & 1) == 1
    high = (tensor_index & 2) == 2
    query_grad = [query_grads[:, c * third : (c + 1) * third] for c in range(3)]
    branch_grad = [branch[:, c * third : (c + 1) * third] for c in range(3)]
    key_grad, value_grad = pair_grads[:, :third], pair_grads[:, third:]

    def traded(left_even, right_even, left_odd, right_odd):
        def product(flag):
            left = left_even if left_even is left_odd else pick(flag, left_odd, left_even)
            return contract_rows(left, pick(flag, right_odd, right_even))

        sent = row_major(product(jnp.logical_not(odd)).astype(BF16))
        return row_major(product(odd)) + near(sent).astype(F32)

    query_low = traded(normed, query_grad[0], normed, query_grad[1])
    query_high = traded(normed, query_grad[2], attended, branch_grad[0])
    pair_low = traded(normed, key_grad, normed, value_grad)
    pair_high = traded(attended, branch_grad[1], attended, branch_grad[2])
    data_count = lax.axis_size("dp")
    gain_part = jnp.stack([sum(gain_one_grads), sum(gain_two_grads)])[:, 0]
    gain_part = jnp.moveaxis(gain_part.reshape(2, data_count, -1), 1, 0)
    gain_share = gain_part.shape[2]
    gain_part = jnp.pad(gain_part, ((0, 0), (0, 14), (0, third - gain_share)))
    first, second, gain_rows = sum_over_data(
        (pick(high, pair_high, pair_low), pick(high, pair_low, pair_high)),
        (pick(high, query_high, query_low), pick(high, query_low, query_high)),
        gain_part,
    )
    quarter = jnp.concatenate([first, second, gain_rows], axis=0).astype(BF16)
    other = far(quarter)
    pair = jnp.stack([pick(high, other, quarter), pick(high, quarter, other)])
    other = near(pair)
    even_pair, odd_pair = pick(odd, other, pair).astype(F32), pick(odd, pair, other).astype(F32)
    share = first.shape[0]
    chunks = [even_pair[0], odd_pair[0], even_pair[1], odd_pair[1]]
    gain_sum = sum(c[2 * share :] for c in chunks)
    first_of = [c[:share] for c in chunks]
    second_of = [c[share : 2 * share] for c in chunks]
    grad_mlp_w = grad_mlp_w.astype(F32)
    return (
        jnp.stack(outputs)[:, None],
        jnp.stack(input_grads)[:, None],
        gain_sum[0, :gain_share],
        gain_sum[1, :gain_share],
        jnp.concatenate(second_of[:3], axis=1),
        first_of[0],
        first_of[1],
        grad_mlp_w[:, :hidden_share],
        grad_mlp_w[:, hidden_share : 2 * hidden_share],
        jnp.concatenate([second_of[3], first_of[2], first_of[3]], axis=1),
        grad_mlp_w[:, 2 * hidden_share :].T,
    )


def solution(mesh):
    in_specs = (
        P(None, "dp", "tensor", None),
        P(None, "dp"),
        P("dp"),
        P("dp"),
        P("dp", None),
        P("dp", None),
        P("dp", None),
        P("dp", "tensor"),
        P("dp", "tensor"),
        P("dp", None),
        P("tensor", "dp"),
        P(None, "dp", "tensor", None),
    )
    out_specs = (
        P(None, "dp", "tensor", None),
        P(None, "dp", "tensor", None),
        P("dp"),
        P("dp"),
        P("dp", None),
        P("dp", None),
        P("dp", None),
        P("dp", "tensor"),
        P("dp", "tensor"),
        P("dp", None),
        P("tensor", "dp"),
    )
    return jax.shard_map(shards, mesh=mesh, in_specs=in_specs, out_specs=out_specs, check_vma=False)
```

```python
import functools

import jax
import jax.numpy as jnp
from jax import lax
from jax.experimental import pallas as pl
from jax.experimental.layout import Layout, with_layout_constraint
from jax.experimental.pallas import tpu as pltpu
from jax.sharding import PartitionSpec as P

HEAD_SIZE = 64
EPSILON = 1e-05
ROPE_BASE = 10000.0
MASKED = -1e30
BF16 = jnp.bfloat16
F32 = jnp.float32

BLOCK_XOR = (0, 2, 1, 3)


def near(value):
    count = lax.axis_size("tensor")
    return lax.ppermute(value, "tensor", [(i, i ^ 1) for i in range(count)])


def far(value):
    count = lax.axis_size("tensor")
    return lax.ppermute(value, "tensor", [(i, i ^ 2) for i in range(count)])


def dot(left_side, right_side):
    return jnp.dot(left_side, right_side, preferred_element_type=F32)


def contract_rows(left_side, right_side):
    return lax.dot_general(
        left_side, right_side, (((0,), (0,)), ((), ())), preferred_element_type=F32
    )


def contract_last(left_side, right_side):
    return lax.dot_general(
        left_side, right_side, (((1,), (1,)), ((), ())), preferred_element_type=F32
    )


def dot_nt(left_side, right_side):
    return lax.dot_general(
        left_side, right_side, (((1,), (1,)), ((), ())), preferred_element_type=F32
    )


def dot_nn(left_side, right_side):
    return lax.dot_general(
        left_side, right_side, (((1,), (0,)), ((), ())), preferred_element_type=F32
    )


def head_of(ref, index):
    return ref[:, index * HEAD_SIZE : (index + 1) * HEAD_SIZE]


def row_scale_of(values):
    return lax.rsqrt(jnp.mean(values * values, axis=-1, keepdims=True) + EPSILON)


def turn(values, cosine, sine):
    lane = lax.broadcasted_iota(jnp.int32, (values.shape[0], 128), 1)
    first_half = lane % HEAD_SIZE < HEAD_SIZE // 2
    parts = []
    for start in range(0, values.shape[1], 128):
        part = values[:, start : start + 128]
        later = pltpu.roll(part, 128 - HEAD_SIZE // 2, 1)
        earlier = pltpu.roll(part, HEAD_SIZE // 2, 1)
        parts.append(part * cosine + jnp.where(first_half, later, earlier) * sine)
    return jnp.concatenate(parts, axis=1)


PAIR_CHUNKS = ((0, 0), (1, 0))
QUERY_CHUNKS = ((0, 1), (1, 1), (2, 1))
OUT_CHUNKS = ((3, 1), (2, 0), (3, 0))


def call(kernel, name, arrays, specs, outs, out_specs, flops=0, scalars=(), aliases=None, **more):
    moved = sum(x.size * x.dtype.itemsize for x in (*arrays, *jax.tree.leaves(outs)))
    return pl.pallas_call(
        kernel,
        grid_spec=pltpu.PrefetchScalarGridSpec(
            num_scalar_prefetch=len(scalars),
            grid=more.get("grid", (1,)),
            in_specs=specs,
            out_specs=out_specs,
            scratch_shapes=more.get("scratch", ()),
        ),
        out_shape=outs,
        input_output_aliases=aliases or {},
        compiler_params=pltpu.CompilerParams(vmem_limit_bytes=VMEM_MIB[name] << 20),
        cost_estimate=pl.CostEstimate(flops=1, transcendentals=0, bytes_accessed=1),
        name=name,
    )(*scalars, *arrays)


def block(shape, at=(0, 0)):
    return pl.BlockSpec(shape, lambda *_: at)


def chunk_specs(width, chunks):
    return [block((width, width // 3), c) for c in chunks]


def array(shape, kind=BF16):
    return jax.ShapeDtypeStruct(shape, kind)


ANY = pl.BlockSpec(memory_space=pl.ANY)
VMEM_MIB = {
    "project_pairs": 24,
    "project_queries": 24,
    "attend": 28,
    "leave": 20,
    "feed": 40,
    "enter": 24,
    "attend_back": 36,
    "pairs_back": 12,
    "finish": 28,
}


def project_pairs_kernel(x_ref, gain_ref, cosine_ref, sine_ref, wk, wv, pair_ref, normed_ref):
    values = x_ref[...].astype(F32)
    normed = (values * row_scale_of(values) * gain_ref[...]).astype(BF16)
    normed_ref[...] = normed
    keys = turn(dot_nn(normed, wk[...]), cosine_ref[...], sine_ref[...]).astype(BF16)
    values = dot_nn(normed, wv[...]).astype(BF16)
    for i in range(keys.shape[1] // 128):
        pair_ref[:, 256 * i : 256 * i + 128] = keys[:, 128 * i : 128 * (i + 1)]
        pair_ref[:, 256 * i + 128 : 256 * (i + 1)] = values[:, 128 * i : 128 * (i + 1)]


def project_pairs(x_rows, gain, cosine, sine, weights):
    rows, width = x_rows.shape
    pair_width = 2 * (width // 3)
    return call(
        project_pairs_kernel,
        "project_pairs",
        (x_rows, gain, cosine, sine, weights, weights),
        [block(x.shape) for x in (x_rows, gain, cosine, sine)] + chunk_specs(width, PAIR_CHUNKS),
        [array((rows, pair_width)), array((rows, width))],
        [block((rows, pair_width)), block((rows, width))],
        2 * rows * width * pair_width,
    )


def project_queries_kernel(normed_ref, cosine_ref, sine_ref, w0, w1, w2, query_ref):
    third = w0.shape[1]
    for i, w in enumerate((w0, w1, w2)):
        turned = turn(dot_nn(normed_ref[...], w[...]), cosine_ref[...], sine_ref[...])
        query_ref[:, i * third : (i + 1) * third] = (turned * HEAD_SIZE ** (-0.5)).astype(BF16)


def project_queries(normed, cosine, sine, weights):
    rows, width = normed.shape
    return call(
        project_queries_kernel,
        "project_queries",
        (normed, cosine, sine, weights, weights, weights),
        [block(x.shape) for x in (normed, cosine, sine)] + chunk_specs(width, QUERY_CHUNKS),
        array((rows, width)),
        block((rows, width)),
        2 * rows * width * width,
    )


def attend_kernel(group, counts, q_ref, p0, p1, p2, p3, *rest):
    o_ref = rest[-1]
    rows = q_ref.shape[0]
    refs = (p0, p1, p2, p3)
    row = lax.broadcasted_iota(jnp.int32, (rows, rows), 0)
    col = lax.broadcasted_iota(jnp.int32, (rows, rows), 1)
    allowed = [jnp.logical_and(col <= row, col < counts[0])]
    allowed += [col < counts[j] for j in range(1, 4)]
    allowed = [jnp.concatenate([a] * group, axis=0) for a in allowed]
    for pair in range(2):
        queries = jnp.concatenate([head_of(q_ref, pair * group + i) for i in range(group)], axis=0)
        scores = [
            jnp.where(allowed[j], dot_nt(queries, head_of(refs[j], pair)), MASKED)
            for j in range(4)
        ]
        top = functools.reduce(jnp.maximum, [jnp.max(s, axis=1, keepdims=True) for s in scores])
        soft = [jnp.exp(s - top) for s in scores]
        total = functools.reduce(jnp.add, [jnp.sum(s, axis=1, keepdims=True) for s in soft])
        out = functools.reduce(
            jnp.add, [dot_nn(soft[j].astype(BF16), head_of(refs[j], 2 + pair)) for j in range(4)]
        )
        out = (out / total).astype(BF16)
        for i in range(group):
            start = (pair * group + i) * HEAD_SIZE
            o_ref[:, start : start + HEAD_SIZE] = out[i * rows : (i + 1) * rows]


def attention_sizes(queries, pairs_own):
    rows = queries.shape[0] // 2
    steps = pairs_own.shape[1] // (4 * HEAD_SIZE)
    group = queries.shape[1] // (2 * HEAD_SIZE * steps)
    return rows, steps, group


def attend(b, counts, queries, pairs_own, others, earlier):
    rows, steps, group = attention_sizes(queries, pairs_own)
    width = queries.shape[1]
    query_spec = pl.BlockSpec((rows, width // steps), lambda i, c: (b, i))
    own_spec = pl.BlockSpec((rows, 4 * HEAD_SIZE), lambda i, c: (b, i))
    pair_spec = pl.BlockSpec((rows, 4 * HEAD_SIZE), lambda i, c: (0, i))
    more = [] if earlier is None else [earlier]
    return call(
        functools.partial(attend_kernel, group),
        "attend",
        (queries, pairs_own, *others, *more),
        [query_spec, own_spec] + [pair_spec] * 3 + [ANY] * len(more),
        array(queries.shape),
        query_spec,
        16 * rows * rows * width,
        (counts,),
        {6: 0} if more else None,
        grid=(steps,),
    )


def attend_back_kernel(group, counts, q_ref, g_ref, cos_ref, sin_ref, p0, p1, p2, p3, *rest):
    dq_ref, kept_ref, sent_ref, turned_ref = rest[-4:]
    rows = q_ref.shape[0]
    half = HEAD_SIZE // 2
    both = jnp.concatenate([p0[...], p1[...], p2[...], p3[...]], axis=0)
    keys, values = both[:, :128], both[:, 128:]
    keys_t = keys.T
    row = lax.broadcasted_iota(jnp.int32, (rows, rows), 0)
    col = lax.broadcasted_iota(jnp.int32, (rows, rows), 1)
    allowed = [jnp.logical_and(row <= col, row < counts[0])]
    allowed += [row < counts[j] for j in range(1, 4)]
    allowed = jnp.concatenate([jnp.concatenate([a] * group, axis=1) for a in allowed], axis=0)
    key_grads, value_grads = [], []
    for pair in range(2):
        lanes = slice(pair * HEAD_SIZE, (pair + 1) * HEAD_SIZE)
        key, value = keys[:, lanes], values[:, lanes]
        queries = jnp.concatenate([head_of(q_ref, pair * group + i) for i in range(group)], axis=0)
        grads = jnp.concatenate([head_of(g_ref, pair * group + i) for i in range(group)], axis=0)
        scores = jnp.where(allowed, dot_nt(key, queries), MASKED)
        soft = jnp.exp(scores - jnp.max(scores, axis=0, keepdims=True))
        soft = soft * (1.0 / jnp.sum(soft, axis=0, keepdims=True))
        grad_soft = dot_nt(value, grads)
        scaled = soft * grad_soft
        grad_scores = (scaled - soft * jnp.sum(scaled, axis=0, keepdims=True)).astype(BF16)
        value_grads.append(dot_nn(soft.astype(BF16), grads))
        key_grads.append(dot_nn(grad_scores, queries))
        query_grad = dot_nn(keys_t[lanes, :], grad_scores) * HEAD_SIZE ** (-0.5)
        for i in range(group):
            part = query_grad[:, i * rows : (i + 1) * rows]
            first, second = part[:half], part[half:]
            start = (pair * group + i) * HEAD_SIZE
            turned_ref[start : start + half, :] = first * cos_ref[...] + second * sin_ref[...]
            turned_ref[start + half : start + HEAD_SIZE, :] = (
                second * cos_ref[...] - first * sin_ref[...]
            )
    grads = jnp.concatenate(key_grads + value_grads, axis=1).astype(BF16)
    kept_ref[...] = grads[: 2 * rows]
    sent_ref[...] = grads[2 * rows :]
    dq_ref[...] = turned_ref[...].T.astype(BF16)


def attend_back(b, counts, queries, grads, cosine_t, sine_t, pairs_own, others, earlier):
    rows, steps, group = attention_sizes(queries, pairs_own)
    width = queries.shape[1]
    query_spec = pl.BlockSpec((rows, width // steps), lambda i, c: (b, i))
    grad_spec = pl.BlockSpec((rows, width // steps), lambda i, c: (0, i))
    own_spec = pl.BlockSpec((rows, 4 * HEAD_SIZE), lambda i, c: (b, i))
    pair_spec = pl.BlockSpec((rows, 4 * HEAD_SIZE), lambda i, c: (0, i))
    half_spec = pl.BlockSpec((2 * rows, 4 * HEAD_SIZE), lambda i, c: (0, i))
    more = [] if earlier is None else [earlier]
    return call(
        functools.partial(attend_back_kernel, group),
        "attend_back",
        (queries, grads, cosine_t, sine_t, pairs_own, *others, *more),
        [query_spec, grad_spec, block(cosine_t.shape), block(sine_t.shape), own_spec]
        + [pair_spec] * 3
        + [ANY] * len(more),
        [array(queries.shape)] + [array((2 * rows, pairs_own.shape[1]))] * 2,
        [query_spec, half_spec, half_spec],
        40 * rows * rows * width,
        (counts,),
        {9: 0} if more else None,
        grid=(steps,),
        scratch=[pltpu.VMEM((width // steps, rows), F32)],
    )


def leave_kernel(x_ref, o_ref, gain_ref, w0, w1, w2, middle_ref, normed_ref):
    out = o_ref[...]
    added = jnp.concatenate([dot_nn(out, w[...]) for w in (w0, w1, w2)], axis=1)
    middle = x_ref[...].astype(F32) + added
    middle_ref[...] = middle
    normed_ref[...] = (middle * row_scale_of(middle) * gain_ref[...]).astype(BF16)


def leave(b, x_rows, attended, gain, weights):
    rows, width = x_rows.shape[0] // 2, x_rows.shape[1]
    here = block((rows, width), (b, 0))
    return call(
        leave_kernel,
        "leave",
        (x_rows, attended, gain, weights, weights, weights),
        [here, here, block(gain.shape)] + chunk_specs(width, OUT_CHUNKS),
        [array((rows, width), F32), array((rows, width))],
        [block((rows, width))] * 2,
        2 * rows * width * width,
    )


def feed_kernel(steps, low_ref, high_ref, grad_ref, weight_ref, *rest):
    rows_ref, act_ref, inner_ref, out_low, out_high, back_low, back_high = rest[-7:]
    step = pl.program_id(0)
    share = weight_ref.shape[1] // 3
    gate, up, down_t = (slice(i * share, (i + 1) * share) for i in range(3))

    @pl.when(step < steps // 2)
    def _():
        rows_ref[...] = low_ref[...]

    @pl.when(step >= steps // 2)
    def _():
        rows_ref[...] = high_ref[...]

    rows = rows_ref[...]
    gate_proj = dot_nn(rows, weight_ref[:, gate])
    up_proj = dot_nn(rows, weight_ref[:, up])
    grad_act = dot_nn(grad_ref[...], weight_ref[:, down_t])
    sigma = 1.0 / (1.0 + jnp.exp(-gate_proj))
    silu = gate_proj * sigma
    act = (silu * up_proj).astype(BF16)
    act_ref[...] = act
    grad_gate = (grad_act * up_proj * sigma * (1.0 + gate_proj * (1.0 - sigma))).astype(BF16)
    grad_up = (grad_act * silu).astype(BF16)
    inner_ref[:, gate] = grad_gate
    inner_ref[:, up] = grad_up
    back = dot_nt(grad_gate, weight_ref[:, gate]) + dot_nt(grad_up, weight_ref[:, up])
    out = dot_nt(act, weight_ref[:, down_t])

    @pl.when(step < steps // 2)
    def _():
        out_low[...] = out.astype(BF16)
        back_low[...] = back.astype(BF16)

    @pl.when(step >= steps // 2)
    def _():
        out_high[...] = out.astype(BF16)
        back_high[...] = back.astype(BF16)


def feed(b, low, high, grads, weights, earlier):
    half, width = low.shape
    share = weights.shape[1] // 3
    steps = 4
    rows = 2 * half // steps
    first = pl.BlockSpec((rows, width), lambda i: (jnp.minimum(i, steps // 2 - 1), 0))
    second = pl.BlockSpec((rows, width), lambda i: (jnp.maximum(i - steps // 2, 0), 0))

    def here(columns):
        return pl.BlockSpec((rows, columns), lambda i: (b * steps + i, 0))

    more = [] if earlier is None else list(earlier)
    return call(
        functools.partial(feed_kernel, steps),
        "feed",
        (low, high, grads, weights, *more),
        [
            first,
            second,
            here(width),
            pl.BlockSpec(weights.shape, lambda i: (0, 0), pipeline_mode=pl.Buffered(1)),
        ]
        + [ANY] * len(more),
        [array((4 * half, width)), array((4 * half, share)), array((4 * half, 2 * share))]
        + [array((half, width))] * 4,
        [here(width), here(share), here(2 * share), first, second, first, second],
        24 * half * width * share,
        aliases={4: 0, 5: 1, 6: 2} if more else None,
        grid=(steps,),
    )


def enter_kernel(
    count, part_ref, near_ref, far_ref, middle_ref, cot_ref, gain_ref, w0, w1, w2, *rest
):
    grad_middle_ref, branch_ref, out_ref, gain_grad_ref = rest[-4:]
    rows, width = middle_ref.shape
    third = width // 3
    middle = middle_ref[...]
    grad_normed = (
        part_ref[...].astype(F32) + near_ref[...].astype(F32) + far_ref[...].astype(F32)
    )
    scale = row_scale_of(middle)
    row = lax.broadcasted_iota(jnp.int32, (rows, width), 0)
    grad_row = jnp.where(row < count[0], cot_ref[...].astype(F32), 0.0)
    gain_grad = jnp.sum(grad_normed * middle * scale, axis=0, keepdims=True)
    gain_grad_ref[...] = jnp.broadcast_to(gain_grad, gain_grad_ref.shape)
    inner = grad_normed * gain_ref[...]
    grad_middle = grad_row + (
        scale * inner - middle * scale**3 * jnp.mean(inner * middle, axis=-1, keepdims=True)
    )
    grad_middle_ref[...] = grad_middle
    branch = grad_middle.astype(BF16)
    branch_ref[...] = branch
    weights = (w0, w1, w2)
    out = dot_nt(branch[:, :third], w0[...])
    for c in range(1, 3):
        out = out + dot_nt(branch[:, c * third : (c + 1) * third], weights[c][...])
    out_ref[...] = out.astype(BF16)


def enter(b, count, part, near_part, far_part, middle, cot_rows, gain, weights, earlier):
    rows, width = middle.shape
    full, here = block((rows, width)), block((rows, width), (b, 0))
    more = [] if earlier is None else [earlier]
    return call(
        enter_kernel,
        "enter",
        (part, near_part, far_part, middle, cot_rows, gain, weights, weights, weights, *more),
        [full, full, full, full, here, block(gain.shape)]
        + chunk_specs(width, OUT_CHUNKS)
        + [ANY] * len(more),
        [
            array((rows, width), F32),
            array((2 * rows, width)),
            array((rows, width)),
            array((8, width), F32),
        ],
        [full, here, full, block((8, width))],
        2 * rows * width * width,
        (count,),
        {10: 1} if more else None,
    )


def pairs_back_kernel(kept_ref, near_ref, far_ref, cosine_ref, sine_ref, *rest):
    pair_ref = rest[-1]
    width = pair_ref.shape[1] // 2
    for i in range(width // 128):
        lanes = slice(256 * i, 256 * (i + 1))
        total = (
            kept_ref[:, lanes].astype(F32)
            + near_ref[:, lanes].astype(F32)
            + far_ref[:, lanes].astype(F32)
        )
        turned = turn(total[:, :128], cosine_ref[...], -sine_ref[...])
        pair_ref[:, 128 * i : 128 * (i + 1)] = turned.astype(BF16)
        pair_ref[:, width + 128 * i : width + 128 * (i + 1)] = total[:, 128:].astype(BF16)


def pairs_back(b, kept, near_part, far_part, cosine, sine, earlier):
    rows, width = far_part.shape
    first = block((rows, width))
    table = block((rows, 128))
    more = [] if earlier is None else [earlier]
    return call(
        pairs_back_kernel,
        "pairs_back",
        (kept, near_part, far_part, cosine, sine, *more),
        [first, first, first, table, table] + [ANY] * len(more),
        array((2 * rows, width)),
        block((rows, width), (b, 0)),
        aliases={5: 0} if more else None,
    )


def finish_kernel(
    x_ref, query_ref, pair_ref, middle_ref, gain_ref, wk, wv, w0, w1, w2, grad_ref, gain_grad_ref
):
    third = x_ref.shape[1] // 3
    grads = [pair_ref[:, :third], pair_ref[:, third:]]
    grads += [query_ref[:, c * third : (c + 1) * third] for c in range(3)]
    grad_normed = dot_nt(grads[0], wk[...])
    for grad, w in zip(grads[1:], (wv, w0, w1, w2)):
        grad_normed = grad_normed + dot_nt(grad, w[...])
    values = x_ref[...].astype(F32)
    scale = row_scale_of(values)
    gain_grad = jnp.sum(grad_normed * values * scale, axis=0, keepdims=True)
    gain_grad_ref[...] = jnp.broadcast_to(gain_grad, gain_grad_ref.shape)
    inner = grad_normed * gain_ref[...]
    grad_ref[...] = (
        middle_ref[...]
        + scale * inner
        - values * scale**3 * jnp.mean(inner * values, axis=-1, keepdims=True)
    ).astype(BF16)


def finish(b, x_rows, query_grads, pair_grads, grad_middle, gain, weights):
    rows, width = grad_middle.shape
    here = block((rows, width), (b, 0))
    return call(
        finish_kernel,
        "finish",
        (x_rows, query_grads, pair_grads, grad_middle, gain, *([weights] * 5)),
        [here, here, block((rows, pair_grads.shape[1]), (b, 0)), block((rows, width))]
        + [block(gain.shape)]
        + chunk_specs(width, PAIR_CHUNKS + QUERY_CHUNKS),
        [array((rows, width)), array((8, width), F32)],
        [block((rows, width)), block((8, width))],
        10 * rows * width * width // 3,
    )


def row_major(value):
    return with_layout_constraint(value, Layout(major_to_minor=tuple(range(value.ndim))))


def added(first, second):
    return (first.astype(F32) + second.astype(F32)).astype(BF16)


def pick(flag, first, second):
    return jnp.where(flag, first, second)


def sum_over_data(part_a, part_b, extra, earlier):
    data_count = lax.axis_size("dp")
    data_index = lax.axis_index("dp")
    columns = part_a[0].shape[1]

    def split(value):
        return value.reshape(data_count, -1, columns)

    if data_count != 8:
        total = part_a[0] + far(part_a[1].astype(BF16)).astype(F32)
        other = part_b[0] + far(part_b[1].astype(BF16)).astype(F32)
        rows = jnp.concatenate([split(total), split(other), extra], axis=1).astype(BF16)
        rows = lax.psum_scatter(rows, "dp", scatter_dimension=0, tiled=True)[0].astype(F32)
        share = total.shape[0] // data_count
        return rows[:share], rows[share : 2 * share], rows[2 * share :], earlier

    groups = data_count // 2
    odd = (data_index & 1) == 1
    group = data_index // 2

    def beside(value):
        even_rows, odd_rows = value[..., 0, :, :], value[..., 1, :, :]
        sent = pick(odd, even_rows, odd_rows).astype(BF16)
        came = lax.ppermute(sent, "dp", [(i, i ^ 1) for i in range(data_count)])
        return pick(odd, odd_rows, even_rows).astype(F32) + came.astype(F32)

    def along(value):
        low = value.astype(BF16)
        total = lax.dynamic_index_in_dim(value, group, 0, keepdims=False)
        for step in range(1, groups):
            sent = lax.dynamic_index_in_dim(low, (group + step) % groups, 0, keepdims=False)
            moves = [(i, (i + 2 * step) % data_count) for i in range(data_count)]
            total = total + lax.ppermute(sent, "dp", moves).astype(F32)
        return total

    second = jnp.stack([split(p) for p in part_b], axis=0)
    second = beside(second.reshape(2, groups, 2, -1, columns))
    first = split(part_a[0] + far(part_a[1].astype(BF16)).astype(F32))
    first = jnp.concatenate([first, extra], axis=1).reshape(groups, 2, -1, columns)
    first, earlier = lax.optimization_barrier((beside(first), earlier))
    second = along(jnp.moveaxis(second, 1, 0))
    first = along(first)
    second = second[0] + far(second[1].astype(BF16)).astype(F32)
    share = second.shape[0]
    return first[:share], second, first[share:], earlier


def shards(
    inputs,
    lengths,
    gain_attn,
    gain_mlp,
    w_query,
    key_weight,
    value_weight,
    w_gate,
    w_up,
    w_out,
    w_down,
    cotangent,
):
    micro = inputs.shape[0]
    row_share = inputs.shape[2]
    width = inputs.shape[3]
    tensor_count = lax.axis_size("tensor")
    tensor_index = lax.axis_index("tensor")
    hidden_share = w_gate.shape[1]

    third = width // 3

    out_parts = [w_out[:, c * third : (c + 1) * third] for c in range(3)]
    query_parts = [w_query[:, c * third : (c + 1) * third] for c in range(3)]
    attn_quarter = lax.select_n(
        tensor_index,
        jnp.concatenate([key_weight, query_parts[0]], axis=1),
        jnp.concatenate([value_weight, query_parts[1]], axis=1),
        jnp.concatenate([out_parts[1], query_parts[2]], axis=1),
        jnp.concatenate([out_parts[2], out_parts[0]], axis=1),
    )
    attn_w = lax.all_gather(attn_quarter, ("tensor", "dp"), axis=0, tiled=True)
    mlp_local = jnp.concatenate([w_gate, w_up, w_down.T], axis=1)
    mlp_full = lax.all_gather(mlp_local, "dp", axis=0, tiled=True)
    gains = lax.all_gather(jnp.stack([gain_attn, gain_mlp]), "dp", axis=1, tiled=True).astype(F32)
    gain_one, gain_two = gains[0:1], gains[1:2]

    query_pos = tensor_index * row_share + jnp.arange(row_share, dtype=jnp.int32)
    exponent = jnp.arange(HEAD_SIZE // 2, dtype=F32) * (2.0 / HEAD_SIZE)
    angles = query_pos.astype(F32)[:, None] * (ROPE_BASE ** (-exponent))[None, :]
    cosine, sine = jnp.cos(angles), jnp.sin(angles)
    cosine_t, sine_t = cosine.T, sine.T
    cosine = jnp.concatenate([cosine] * 4, axis=1)
    sine = jnp.concatenate([-sine, sine, -sine, sine], axis=1)

    def counts_of(b):
        counts = []
        for x in BLOCK_XOR:
            block = tensor_index ^ x
            count = jnp.clip(lengths[b, 0] - block * row_share, 0, row_share)
            counts.append(jnp.where(block <= tensor_index, count, 0))
        return jnp.stack(counts).astype(jnp.int32)

    counts = [counts_of(b) for b in range(micro)]
    valid_rows = [
        jnp.clip(lengths[b, 0] - tensor_index * row_share, 0, row_share).astype(jnp.int32)
        for b in range(micro)
    ]
    valids = [
        (jnp.arange(row_share, dtype=jnp.int32) < valid_rows[b])[:, None] for b in range(micro)
    ]

    grad_own = jnp.stack(
        [jnp.where(valids[b], cotangent[b, 0], jnp.zeros((), BF16)) for b in range(micro)]
    )
    grad_far = far(grad_own)
    grad_near = near(jnp.stack([grad_own, grad_far]))
    grad_ffn = jnp.concatenate(
        [p[b] for b in range(micro) for p in (grad_own, grad_far, grad_near[0], grad_near[1])],
        axis=0,
    )

    x_rows = inputs[:, 0].reshape(micro * row_share, width)
    cot_rows = cotangent[:, 0].reshape(micro * row_share, width)
    cosine_all = jnp.concatenate([cosine] * micro, axis=0)
    sine_all = jnp.concatenate([sine] * micro, axis=0)
    pairs_own, normed = project_pairs(x_rows, gain_one, cosine_all, sine_all, attn_w)
    queries = project_queries(normed, cosine_all, sine_all, attn_w)
    kept = []
    attended = None
    for b in range(micro):
        own = pairs_own[b * row_share : (b + 1) * row_share]
        if b > 0:
            own, queries = lax.optimization_barrier((own, queries))
        across = far(own)
        if b == 0:
            across, queries = lax.optimization_barrier((across, queries))
        others = [across, near(own), near(across)]
        attended = attend(b, counts[b], queries, pairs_own, others, attended)
        middle, hidden_own = leave(b, x_rows, attended, gain_two, attn_w)
        across = far(hidden_own)
        low = jnp.concatenate([hidden_own, across], axis=0)
        kept.append(dict(others=others, middle=middle, low=low, high=near(low)))
        if b == micro - 1:
            mlp_full, _ = lax.optimization_barrier((mlp_full, across))

    shared = None
    for b in range(micro):
        k = kept[b]
        *shared, k["out_low"], k["out_high"], k["part"], back_high = feed(
            b, k["low"], k["high"], grad_ffn, mlp_full, shared
        )
        k["near_part"] = near(back_high)
        k["far_part"] = far(added(k["part"][row_share:], k["near_part"][row_share:]))
    hidden_rows, activated, inner_grads = shared
    grad_mlp_w = row_major(
        jnp.concatenate(
            [
                row_major(contract_rows(hidden_rows, inner_grads).astype(BF16)),
                row_major(contract_rows(grad_ffn, activated).astype(BF16)),
            ],
            axis=1,
        )
    )
    grad_mlp_w, kept[0]["middle"] = lax.optimization_barrier((grad_mlp_w, kept[0]["middle"]))

    gain_two_grads = []
    branch = query_grads = pair_grads = None

    grad_mlp_w = lax.psum_scatter(grad_mlp_w, "dp", scatter_dimension=0, tiled=True)
    for b in range(micro):
        k = kept[b]
        k["grad_middle"], branch, grad_att, gain_two_grad = enter(
            b,
            valid_rows[b][None],
            k["part"],
            k["near_part"],
            k["far_part"],
            k["middle"],
            cot_rows,
            gain_two,
            attn_w,
            branch,
        )
        gain_two_grads.append(gain_two_grad[0:1])
        if b > 0:
            near_pair, grad_att = lax.optimization_barrier((kept[b - 1]["near_pair"], grad_att))
            kept[b - 1]["near_pair"] = near_pair
        query_grads, k["pair_kept"], pair_sent = attend_back(
            b, counts[b], queries, grad_att, cosine_t, sine_t, pairs_own, k["others"], query_grads
        )
        k["near_pair"] = near(pair_sent)
    for b in range(micro):
        k = kept[b]
        far_pair = far(added(k["pair_kept"][row_share:], k["near_pair"][row_share:]))
        pair_grads = pairs_back(
            b, k["pair_kept"], k["near_pair"], far_pair, cosine, sine, pair_grads
        )

    outputs, input_grads, gain_one_grads = [], [], []
    for b in range(micro):
        k = kept[b]
        input_grad, gain_one_grad = finish(
            b, x_rows, query_grads, pair_grads, k["grad_middle"], gain_one, attn_w
        )
        gain_one_grads.append(gain_one_grad[0:1])
        input_grads.append(input_grad)
        out_near = near(k["out_high"])
        out_far = far(added(k["out_low"][row_share:], out_near[row_share:]))
        ffn_out = (
            k["out_low"][:row_share].astype(F32)
            + out_near[:row_share].astype(F32)
            + out_far.astype(F32)
        )
        outputs.append(jnp.where(valids[b], k["middle"] + ffn_out, 0.0).astype(BF16))

    odd = (tensor_index & 1) == 1
    high = (tensor_index & 2) == 2
    query_grad = [query_grads[:, c * third : (c + 1) * third] for c in range(3)]
    branch_grad = [branch[:, c * third : (c + 1) * third] for c in range(3)]
    key_grad, value_grad = pair_grads[:, :third], pair_grads[:, third:]

    def traded(left_even, right_even, left_odd, right_odd):
        def product(flag):
            left = left_even if left_even is left_odd else pick(flag, left_odd, left_even)
            return contract_rows(left, pick(flag, right_odd, right_even))

        sent = row_major(product(jnp.logical_not(odd)).astype(BF16))
        return row_major(product(odd)) + near(sent).astype(F32)

    query_low = traded(normed, query_grad[0], normed, query_grad[1])
    query_high = traded(normed, query_grad[2], attended, branch_grad[0])
    pair_low = traded(normed, key_grad, normed, value_grad)
    pair_high = traded(attended, branch_grad[1], attended, branch_grad[2])
    data_count = lax.axis_size("dp")
    gain_part = jnp.stack([sum(gain_one_grads), sum(gain_two_grads)])[:, 0]
    gain_part = jnp.moveaxis(gain_part.reshape(2, data_count, -1), 1, 0)
    gain_share = gain_part.shape[2]
    gain_part = jnp.pad(gain_part, ((0, 0), (0, 14), (0, third - gain_share)))
    first, second, gain_rows, grad_mlp_w = sum_over_data(
        (pick(high, pair_high, pair_low), pick(high, pair_low, pair_high)),
        (pick(high, query_high, query_low), pick(high, query_low, query_high)),
        gain_part,
        grad_mlp_w,
    )
    quarter = jnp.concatenate([first, second, gain_rows], axis=0).astype(BF16)
    other = far(quarter)
    pair = jnp.stack([pick(high, other, quarter), pick(high, quarter, other)])
    other = near(pair)
    even_pair, odd_pair = pick(odd, other, pair).astype(F32), pick(odd, pair, other).astype(F32)
    share = first.shape[0]
    chunks = [even_pair[0], odd_pair[0], even_pair[1], odd_pair[1]]
    gain_sum = sum(c[2 * share :] for c in chunks)
    first_of = [c[:share] for c in chunks]
    second_of = [c[share : 2 * share] for c in chunks]
    grad_mlp_w = grad_mlp_w.astype(F32)
    return (
        jnp.stack(outputs)[:, None],
        jnp.stack(input_grads)[:, None],
        gain_sum[0, :gain_share],
        gain_sum[1, :gain_share],
        jnp.concatenate(second_of[:3], axis=1),
        first_of[0],
        first_of[1],
        grad_mlp_w[:, :hidden_share],
        grad_mlp_w[:, hidden_share : 2 * hidden_share],
        jnp.concatenate([second_of[3], first_of[2], first_of[3]], axis=1),
        grad_mlp_w[:, 2 * hidden_share :].T,
    )


def solution(mesh):
    in_specs = (
        P(None, "dp", "tensor", None),
        P(None, "dp"),
        P("dp"),
        P("dp"),
        P("dp", None),
        P("dp", None),
        P("dp", None),
        P("dp", "tensor"),
        P("dp", "tensor"),
        P("dp", None),
        P("tensor", "dp"),
        P(None, "dp", "tensor", None),
    )
    out_specs = (
        P(None, "dp", "tensor", None),
        P(None, "dp", "tensor", None),
        P("dp"),
        P("dp"),
        P("dp", None),
        P("dp", None),
        P("dp", None),
        P("dp", "tensor"),
        P("dp", "tensor"),
        P("dp", None),
        P("tensor", "dp"),
    )
    return jax.shard_map(shards, mesh=mesh, in_specs=in_specs, out_specs=out_specs, check_vma=False)
```

```python
import functools

import jax
import jax.numpy as jnp
from jax import lax
from jax.experimental import pallas as pl
from jax.experimental.layout import Layout, with_layout_constraint
from jax.experimental.pallas import tpu as pltpu
from jax.sharding import PartitionSpec as P

HEAD_SIZE = 64
EPSILON = 1e-05
ROPE_BASE = 10000.0
MASKED = -1e30
BF16 = jnp.bfloat16
F32 = jnp.float32

BLOCK_XOR = (0, 2, 1, 3)


def near(value):
    count = lax.axis_size("tensor")
    return lax.ppermute(value, "tensor", [(i, i ^ 1) for i in range(count)])


def far(value):
    count = lax.axis_size("tensor")
    return lax.ppermute(value, "tensor", [(i, i ^ 2) for i in range(count)])


def dot(left_side, right_side):
    return jnp.dot(left_side, right_side, preferred_element_type=F32)


def contract_rows(left_side, right_side):
    return lax.dot_general(
        left_side, right_side, (((0,), (0,)), ((), ())), preferred_element_type=F32
    )


def dot_nt(left_side, right_side):
    return lax.dot_general(
        left_side, right_side, (((1,), (1,)), ((), ())), preferred_element_type=F32
    )


def dot_nn(left_side, right_side):
    return lax.dot_general(
        left_side, right_side, (((1,), (0,)), ((), ())), preferred_element_type=F32
    )


def head_of(ref, index):
    return ref[:, index * HEAD_SIZE : (index + 1) * HEAD_SIZE]


def row_scale_of(values):
    return lax.rsqrt(jnp.mean(values * values, axis=-1, keepdims=True) + EPSILON)


def turn(values, cosine, sine):
    lane = lax.broadcasted_iota(jnp.int32, (values.shape[0], 128), 1)
    first_half = lane % HEAD_SIZE < HEAD_SIZE // 2
    parts = []
    for start in range(0, values.shape[1], 128):
        part = values[:, start : start + 128]
        later = pltpu.roll(part, 128 - HEAD_SIZE // 2, 1)
        earlier = pltpu.roll(part, HEAD_SIZE // 2, 1)
        parts.append(part * cosine + jnp.where(first_half, later, earlier) * sine)
    return jnp.concatenate(parts, axis=1)


PAIR_CHUNKS = ((0, 0), (1, 0))
QUERY_CHUNKS = ((0, 1), (1, 1), (2, 1))
OUT_CHUNKS = ((3, 1), (2, 0), (3, 0))


def call(kernel, name, arrays, specs, outs, out_specs, flops=0, scalars=(), aliases=None, **more):
    moved = sum(x.size * x.dtype.itemsize for x in (*arrays, *jax.tree.leaves(outs)))
    return pl.pallas_call(
        kernel,
        grid_spec=pltpu.PrefetchScalarGridSpec(
            num_scalar_prefetch=len(scalars),
            grid=more.get("grid", (1,)),
            in_specs=specs,
            out_specs=out_specs,
            scratch_shapes=more.get("scratch", ()),
        ),
        out_shape=outs,
        input_output_aliases=aliases or {},
        compiler_params=pltpu.CompilerParams(vmem_limit_bytes=VMEM_MIB[name] << 20),
        cost_estimate=pl.CostEstimate(flops=1, transcendentals=0, bytes_accessed=1),
        name=name,
    )(*scalars, *arrays)


def block(shape, at=(0, 0)):
    return pl.BlockSpec(shape, lambda *_: at)


def chunk_specs(width, chunks):
    return [block((width, width // 3), c) for c in chunks]


def array(shape, kind=BF16):
    return jax.ShapeDtypeStruct(shape, kind)


ANY = pl.BlockSpec(memory_space=pl.ANY)
VMEM_MIB = {
    "project_pairs": 24,
    "project_queries": 24,
    "attend": 28,
    "leave": 20,
    "feed": 40,
    "enter": 24,
    "attend_back": 36,
    "pairs_back": 12,
    "finish": 28,
}


def project_pairs_kernel(x_ref, gain_ref, cosine_ref, sine_ref, wk, wv, pair_ref, normed_ref):
    values = x_ref[...].astype(F32)
    normed = (values * row_scale_of(values) * gain_ref[...]).astype(BF16)
    normed_ref[...] = normed
    keys = turn(dot_nn(normed, wk[...]), cosine_ref[...], sine_ref[...]).astype(BF16)
    values = dot_nn(normed, wv[...]).astype(BF16)
    for i in range(keys.shape[1] // 128):
        pair_ref[:, 256 * i : 256 * i + 128] = keys[:, 128 * i : 128 * (i + 1)]
        pair_ref[:, 256 * i + 128 : 256 * (i + 1)] = values[:, 128 * i : 128 * (i + 1)]


def project_pairs(x_rows, gain, cosine, sine, weights):
    rows, width = x_rows.shape
    pair_width = 2 * (width // 3)
    return call(
        project_pairs_kernel,
        "project_pairs",
        (x_rows, gain, cosine, sine, weights, weights),
        [block(x.shape) for x in (x_rows, gain, cosine, sine)] + chunk_specs(width, PAIR_CHUNKS),
        [array((rows, pair_width)), array((rows, width))],
        [block((rows, pair_width)), block((rows, width))],
        2 * rows * width * pair_width,
    )


def project_queries_kernel(normed_ref, cosine_ref, sine_ref, w0, w1, w2, query_ref):
    third = w0.shape[1]
    for i, w in enumerate((w0, w1, w2)):
        turned = turn(dot_nn(normed_ref[...], w[...]), cosine_ref[...], sine_ref[...])
        query_ref[:, i * third : (i + 1) * third] = (turned * HEAD_SIZE ** (-0.5)).astype(BF16)


def project_queries(normed, cosine, sine, weights):
    rows, width = normed.shape
    return call(
        project_queries_kernel,
        "project_queries",
        (normed, cosine, sine, weights, weights, weights),
        [block(x.shape) for x in (normed, cosine, sine)] + chunk_specs(width, QUERY_CHUNKS),
        array((rows, width)),
        block((rows, width)),
        2 * rows * width * width,
    )


def attend_kernel(group, counts, q_ref, p0, p1, p2, p3, *rest):
    o_ref = rest[-1]
    rows = q_ref.shape[0]
    refs = (p0, p1, p2, p3)
    row = lax.broadcasted_iota(jnp.int32, (rows, rows), 0)
    col = lax.broadcasted_iota(jnp.int32, (rows, rows), 1)
    allowed = [jnp.logical_and(col <= row, col < counts[0])]
    allowed += [col < counts[j] for j in range(1, 4)]
    allowed = [jnp.concatenate([a] * group, axis=0) for a in allowed]
    for pair in range(2):
        queries = jnp.concatenate([head_of(q_ref, pair * group + i) for i in range(group)], axis=0)
        scores = [
            jnp.where(allowed[j], dot_nt(queries, head_of(refs[j], pair)), MASKED)
            for j in range(4)
        ]
        top = functools.reduce(jnp.maximum, [jnp.max(s, axis=1, keepdims=True) for s in scores])
        soft = [jnp.exp(s - top) for s in scores]
        total = functools.reduce(jnp.add, [jnp.sum(s, axis=1, keepdims=True) for s in soft])
        out = functools.reduce(
            jnp.add, [dot_nn(soft[j].astype(BF16), head_of(refs[j], 2 + pair)) for j in range(4)]
        )
        out = (out / total).astype(BF16)
        for i in range(group):
            start = (pair * group + i) * HEAD_SIZE
            o_ref[:, start : start + HEAD_SIZE] = out[i * rows : (i + 1) * rows]


def attention_sizes(queries, pairs_own):
    rows = queries.shape[0] // 2
    steps = pairs_own.shape[1] // (4 * HEAD_SIZE)
    group = queries.shape[1] // (2 * HEAD_SIZE * steps)
    return rows, steps, group


def attend(b, counts, queries, pairs_own, others, earlier):
    rows, steps, group = attention_sizes(queries, pairs_own)
    width = queries.shape[1]
    query_spec = pl.BlockSpec((rows, width // steps), lambda i, c: (b, i))
    own_spec = pl.BlockSpec((rows, 4 * HEAD_SIZE), lambda i, c: (b, i))
    pair_spec = pl.BlockSpec((rows, 4 * HEAD_SIZE), lambda i, c: (0, i))
    more = [] if earlier is None else [earlier]
    return call(
        functools.partial(attend_kernel, group),
        "attend",
        (queries, pairs_own, *others, *more),
        [query_spec, own_spec] + [pair_spec] * 3 + [ANY] * len(more),
        array(queries.shape),
        query_spec,
        16 * rows * rows * width,
        (counts,),
        {6: 0} if more else None,
        grid=(steps,),
    )


def attend_back_kernel(group, counts, q_ref, g_ref, cos_ref, sin_ref, p0, p1, p2, p3, *rest):
    dq_ref, kept_ref, sent_ref, turned_ref = rest[-4:]
    rows = q_ref.shape[0]
    half = HEAD_SIZE // 2
    both = jnp.concatenate([p0[...], p1[...], p2[...], p3[...]], axis=0)
    keys, values = both[:, :128], both[:, 128:]
    keys_t = keys.T
    row = lax.broadcasted_iota(jnp.int32, (rows, rows), 0)
    col = lax.broadcasted_iota(jnp.int32, (rows, rows), 1)
    allowed = [jnp.logical_and(row <= col, row < counts[0])]
    allowed += [row < counts[j] for j in range(1, 4)]
    allowed = jnp.concatenate([jnp.concatenate([a] * group, axis=1) for a in allowed], axis=0)
    key_grads, value_grads = [], []
    for pair in range(2):
        lanes = slice(pair * HEAD_SIZE, (pair + 1) * HEAD_SIZE)
        key, value = keys[:, lanes], values[:, lanes]
        queries = jnp.concatenate([head_of(q_ref, pair * group + i) for i in range(group)], axis=0)
        grads = jnp.concatenate([head_of(g_ref, pair * group + i) for i in range(group)], axis=0)
        scores = jnp.where(allowed, dot_nt(key, queries), MASKED)
        soft = jnp.exp(scores - jnp.max(scores, axis=0, keepdims=True))
        soft = soft * (1.0 / jnp.sum(soft, axis=0, keepdims=True))
        grad_soft = dot_nt(value, grads)
        scaled = soft * grad_soft
        grad_scores = (scaled - soft * jnp.sum(scaled, axis=0, keepdims=True)).astype(BF16)
        value_grads.append(dot_nn(soft.astype(BF16), grads))
        key_grads.append(dot_nn(grad_scores, queries))
        query_grad = dot_nn(keys_t[lanes, :], grad_scores) * HEAD_SIZE ** (-0.5)
        for i in range(group):
            part = query_grad[:, i * rows : (i + 1) * rows]
            first, second = part[:half], part[half:]
            start = (pair * group + i) * HEAD_SIZE
            turned_ref[start : start + half, :] = first * cos_ref[...] + second * sin_ref[...]
            turned_ref[start + half : start + HEAD_SIZE, :] = (
                second * cos_ref[...] - first * sin_ref[...]
            )
    grads = jnp.concatenate(key_grads + value_grads, axis=1).astype(BF16)
    kept_ref[...] = grads[: 2 * rows]
    sent_ref[...] = grads[2 * rows :]
    dq_ref[...] = turned_ref[...].T.astype(BF16)


def attend_back(b, counts, queries, grads, cosine_t, sine_t, pairs_own, others, earlier):
    rows, steps, group = attention_sizes(queries, pairs_own)
    width = queries.shape[1]
    query_spec = pl.BlockSpec((rows, width // steps), lambda i, c: (b, i))
    grad_spec = pl.BlockSpec((rows, width // steps), lambda i, c: (0, i))
    own_spec = pl.BlockSpec((rows, 4 * HEAD_SIZE), lambda i, c: (b, i))
    pair_spec = pl.BlockSpec((rows, 4 * HEAD_SIZE), lambda i, c: (0, i))
    half_spec = pl.BlockSpec((2 * rows, 4 * HEAD_SIZE), lambda i, c: (0, i))
    more = [] if earlier is None else [earlier]
    return call(
        functools.partial(attend_back_kernel, group),
        "attend_back",
        (queries, grads, cosine_t, sine_t, pairs_own, *others, *more),
        [query_spec, grad_spec, block(cosine_t.shape), block(sine_t.shape), own_spec]
        + [pair_spec] * 3
        + [ANY] * len(more),
        [array(queries.shape)] + [array((2 * rows, pairs_own.shape[1]))] * 2,
        [query_spec, half_spec, half_spec],
        40 * rows * rows * width,
        (counts,),
        {9: 0} if more else None,
        grid=(steps,),
        scratch=[pltpu.VMEM((width // steps, rows), F32)],
    )


def leave_kernel(x_ref, o_ref, gain_ref, w0, w1, w2, middle_ref, normed_ref):
    out = o_ref[...]
    added = jnp.concatenate([dot_nn(out, w[...]) for w in (w0, w1, w2)], axis=1)
    middle = x_ref[...].astype(F32) + added
    middle_ref[...] = middle
    normed_ref[...] = (middle * row_scale_of(middle) * gain_ref[...]).astype(BF16)


def leave(b, x_rows, attended, gain, weights):
    rows, width = x_rows.shape[0] // 2, x_rows.shape[1]
    here = block((rows, width), (b, 0))
    return call(
        leave_kernel,
        "leave",
        (x_rows, attended, gain, weights, weights, weights),
        [here, here, block(gain.shape)] + chunk_specs(width, OUT_CHUNKS),
        [array((rows, width), F32), array((rows, width))],
        [block((rows, width))] * 2,
        2 * rows * width * width,
    )


def feed_kernel(steps, low_ref, high_ref, grad_ref, weight_ref, *rest):
    rows_ref, act_ref, inner_ref, out_low, out_high, back_low, back_high = rest[-7:]
    step = pl.program_id(0)
    share = weight_ref.shape[1] // 3
    gate, up, down_t = (slice(i * share, (i + 1) * share) for i in range(3))

    @pl.when(step < steps // 2)
    def _():
        rows_ref[...] = low_ref[...]

    @pl.when(step >= steps // 2)
    def _():
        rows_ref[...] = high_ref[...]

    rows = rows_ref[...]
    gate_proj = dot_nn(rows, weight_ref[:, gate])
    up_proj = dot_nn(rows, weight_ref[:, up])
    grad_act = dot_nn(grad_ref[...], weight_ref[:, down_t])
    sigma = 1.0 / (1.0 + jnp.exp(-gate_proj))
    silu = gate_proj * sigma
    act = (silu * up_proj).astype(BF16)
    act_ref[...] = act
    grad_gate = (grad_act * up_proj * sigma * (1.0 + gate_proj * (1.0 - sigma))).astype(BF16)
    grad_up = (grad_act * silu).astype(BF16)
    inner_ref[:, gate] = grad_gate
    inner_ref[:, up] = grad_up
    back = dot_nt(grad_gate, weight_ref[:, gate]) + dot_nt(grad_up, weight_ref[:, up])
    out = dot_nt(act, weight_ref[:, down_t])

    @pl.when(step < steps // 2)
    def _():
        out_low[...] = out.astype(BF16)
        back_low[...] = back.astype(BF16)

    @pl.when(step >= steps // 2)
    def _():
        out_high[...] = out.astype(BF16)
        back_high[...] = back.astype(BF16)


def feed(b, low, high, grads, weights, earlier):
    half, width = low.shape
    share = weights.shape[1] // 3
    steps = 4
    rows = 2 * half // steps
    first = pl.BlockSpec((rows, width), lambda i: (jnp.minimum(i, steps // 2 - 1), 0))
    second = pl.BlockSpec((rows, width), lambda i: (jnp.maximum(i - steps // 2, 0), 0))

    def here(columns):
        return pl.BlockSpec((rows, columns), lambda i: (b * steps + i, 0))

    more = [] if earlier is None else list(earlier)
    return call(
        functools.partial(feed_kernel, steps),
        "feed",
        (low, high, grads, weights, *more),
        [
            first,
            second,
            here(width),
            pl.BlockSpec(weights.shape, lambda i: (0, 0), pipeline_mode=pl.Buffered(1)),
        ]
        + [ANY] * len(more),
        [array((4 * half, width)), array((4 * half, share)), array((4 * half, 2 * share))]
        + [array((half, width))] * 4,
        [here(width), here(share), here(2 * share), first, second, first, second],
        24 * half * width * share,
        aliases={4: 0, 5: 1, 6: 2} if more else None,
        grid=(steps,),
    )


def enter_kernel(
    count, part_ref, near_ref, far_ref, middle_ref, cot_ref, gain_ref, w0, w1, w2, *rest
):
    grad_middle_ref, branch_ref, out_ref, gain_grad_ref = rest[-4:]
    rows, width = middle_ref.shape
    third = width // 3
    middle = middle_ref[...]
    grad_normed = (
        part_ref[...].astype(F32) + near_ref[...].astype(F32) + far_ref[...].astype(F32)
    )
    scale = row_scale_of(middle)
    row = lax.broadcasted_iota(jnp.int32, (rows, width), 0)
    grad_row = jnp.where(row < count[0], cot_ref[...].astype(F32), 0.0)
    gain_grad = jnp.sum(grad_normed * middle * scale, axis=0, keepdims=True)
    gain_grad_ref[...] = jnp.broadcast_to(gain_grad, gain_grad_ref.shape)
    inner = grad_normed * gain_ref[...]
    grad_middle = grad_row + (
        scale * inner - middle * scale**3 * jnp.mean(inner * middle, axis=-1, keepdims=True)
    )
    grad_middle_ref[...] = grad_middle
    branch = grad_middle.astype(BF16)
    branch_ref[...] = branch
    weights = (w0, w1, w2)
    out = dot_nt(branch[:, :third], w0[...])
    for c in range(1, 3):
        out = out + dot_nt(branch[:, c * third : (c + 1) * third], weights[c][...])
    out_ref[...] = out.astype(BF16)


def enter(b, count, part, near_part, far_part, middle, cot_rows, gain, weights, earlier):
    rows, width = middle.shape
    full, here = block((rows, width)), block((rows, width), (b, 0))
    more = [] if earlier is None else [earlier]
    return call(
        enter_kernel,
        "enter",
        (part, near_part, far_part, middle, cot_rows, gain, weights, weights, weights, *more),
        [full, full, full, full, here, block(gain.shape)]
        + chunk_specs(width, OUT_CHUNKS)
        + [ANY] * len(more),
        [
            array((rows, width), F32),
            array((2 * rows, width)),
            array((rows, width)),
            array((8, width), F32),
        ],
        [full, here, full, block((8, width))],
        2 * rows * width * width,
        (count,),
        {10: 1} if more else None,
    )


def pairs_back_kernel(kept_ref, near_ref, far_ref, cosine_ref, sine_ref, *rest):
    pair_ref = rest[-1]
    width = pair_ref.shape[1] // 2
    for i in range(width // 128):
        lanes = slice(256 * i, 256 * (i + 1))
        total = (
            kept_ref[:, lanes].astype(F32)
            + near_ref[:, lanes].astype(F32)
            + far_ref[:, lanes].astype(F32)
        )
        turned = turn(total[:, :128], cosine_ref[...], -sine_ref[...])
        pair_ref[:, 128 * i : 128 * (i + 1)] = turned.astype(BF16)
        pair_ref[:, width + 128 * i : width + 128 * (i + 1)] = total[:, 128:].astype(BF16)


def pairs_back(b, kept, near_part, far_part, cosine, sine, earlier):
    rows, width = far_part.shape
    first = block((rows, width))
    table = block((rows, 128))
    more = [] if earlier is None else [earlier]
    return call(
        pairs_back_kernel,
        "pairs_back",
        (kept, near_part, far_part, cosine, sine, *more),
        [first, first, first, table, table] + [ANY] * len(more),
        array((2 * rows, width)),
        block((rows, width), (b, 0)),
        aliases={5: 0} if more else None,
    )


def finish_kernel(
    x_ref, query_ref, pair_ref, middle_ref, gain_ref, wk, wv, w0, w1, w2, grad_ref, gain_grad_ref
):
    third = x_ref.shape[1] // 3
    grads = [pair_ref[:, :third], pair_ref[:, third:]]
    grads += [query_ref[:, c * third : (c + 1) * third] for c in range(3)]
    grad_normed = dot_nt(grads[0], wk[...])
    for grad, w in zip(grads[1:], (wv, w0, w1, w2)):
        grad_normed = grad_normed + dot_nt(grad, w[...])
    values = x_ref[...].astype(F32)
    scale = row_scale_of(values)
    gain_grad = jnp.sum(grad_normed * values * scale, axis=0, keepdims=True)
    gain_grad_ref[...] = jnp.broadcast_to(gain_grad, gain_grad_ref.shape)
    inner = grad_normed * gain_ref[...]
    grad_ref[...] = (
        middle_ref[...]
        + scale * inner
        - values * scale**3 * jnp.mean(inner * values, axis=-1, keepdims=True)
    ).astype(BF16)


def finish(b, x_rows, query_grads, pair_grads, grad_middle, gain, weights):
    rows, width = grad_middle.shape
    here = block((rows, width), (b, 0))
    return call(
        finish_kernel,
        "finish",
        (x_rows, query_grads, pair_grads, grad_middle, gain, *([weights] * 5)),
        [here, here, block((rows, pair_grads.shape[1]), (b, 0)), block((rows, width))]
        + [block(gain.shape)]
        + chunk_specs(width, PAIR_CHUNKS + QUERY_CHUNKS),
        [array((rows, width)), array((8, width), F32)],
        [block((rows, width)), block((8, width))],
        10 * rows * width * width // 3,
    )


def row_major(value):
    return with_layout_constraint(value, Layout(major_to_minor=tuple(range(value.ndim))))


def added(first, second):
    return (first.astype(F32) + second.astype(F32)).astype(BF16)


def pick(flag, first, second):
    return jnp.where(flag, first, second)


def sum_over_data(part_a, part_b, extra, earlier):
    data_count = lax.axis_size("dp")
    data_index = lax.axis_index("dp")
    columns = part_a[0].shape[1]

    def split(value):
        return value.reshape(data_count, -1, columns)

    if data_count != 8:
        total = part_a[0] + far(part_a[1].astype(BF16)).astype(F32)
        other = part_b[0] + far(part_b[1].astype(BF16)).astype(F32)
        rows = jnp.concatenate([split(total), split(other), extra], axis=1).astype(BF16)
        rows = lax.psum_scatter(rows, "dp", scatter_dimension=0, tiled=True)[0].astype(F32)
        share = total.shape[0] // data_count
        return rows[:share], rows[share : 2 * share], rows[2 * share :], earlier

    groups = data_count // 2
    odd = (data_index & 1) == 1
    group = data_index // 2

    def beside(value):
        even_rows, odd_rows = value[..., 0, :, :], value[..., 1, :, :]
        sent = pick(odd, even_rows, odd_rows).astype(BF16)
        came = lax.ppermute(sent, "dp", [(i, i ^ 1) for i in range(data_count)])
        return pick(odd, odd_rows, even_rows).astype(F32) + came.astype(F32)

    def along(value):
        low = value.astype(BF16)
        total = lax.dynamic_index_in_dim(value, group, 0, keepdims=False)
        for step in range(1, groups):
            sent = lax.dynamic_index_in_dim(low, (group + step) % groups, 0, keepdims=False)
            moves = [(i, (i + 2 * step) % data_count) for i in range(data_count)]
            total = total + lax.ppermute(sent, "dp", moves).astype(F32)
        return total

    second = jnp.stack([split(p) for p in part_b], axis=0)
    second = beside(second.reshape(2, groups, 2, -1, columns))
    first = split(part_a[0] + far(part_a[1].astype(BF16)).astype(F32))
    first = jnp.concatenate([first, extra], axis=1).reshape(groups, 2, -1, columns)
    first, earlier = lax.optimization_barrier((beside(first), earlier))
    second = along(jnp.moveaxis(second, 1, 0))
    first = along(first)
    second = second[0] + far(second[1].astype(BF16)).astype(F32)
    share = second.shape[0]
    return first[:share], second, first[share:], earlier


def shards(
    inputs,
    lengths,
    gain_attn,
    gain_mlp,
    w_query,
    key_weight,
    value_weight,
    w_gate,
    w_up,
    w_out,
    w_down,
    cotangent,
):
    micro = inputs.shape[0]
    row_share = inputs.shape[2]
    width = inputs.shape[3]
    tensor_count = lax.axis_size("tensor")
    tensor_index = lax.axis_index("tensor")
    hidden_share = w_gate.shape[1]

    third = width // 3

    out_parts = [w_out[:, c * third : (c + 1) * third] for c in range(3)]
    query_parts = [w_query[:, c * third : (c + 1) * third] for c in range(3)]
    attn_quarter = lax.select_n(
        tensor_index,
        jnp.concatenate([key_weight, query_parts[0]], axis=1),
        jnp.concatenate([value_weight, query_parts[1]], axis=1),
        jnp.concatenate([out_parts[1], query_parts[2]], axis=1),
        jnp.concatenate([out_parts[2], out_parts[0]], axis=1),
    )
    attn_w = lax.all_gather(attn_quarter, ("tensor", "dp"), axis=0, tiled=True)
    mlp_local = jnp.concatenate([w_gate, w_up, w_down.T], axis=1)
    mlp_full = lax.all_gather(mlp_local, "dp", axis=0, tiled=True)
    gains = lax.all_gather(jnp.stack([gain_attn, gain_mlp]), "dp", axis=1, tiled=True).astype(F32)
    gain_one, gain_two = gains[0:1], gains[1:2]

    query_pos = tensor_index * row_share + jnp.arange(row_share, dtype=jnp.int32)
    exponent = jnp.arange(HEAD_SIZE // 2, dtype=F32) * (2.0 / HEAD_SIZE)
    angles = query_pos.astype(F32)[:, None] * (ROPE_BASE ** (-exponent))[None, :]
    cosine, sine = jnp.cos(angles), jnp.sin(angles)
    cosine_t, sine_t = cosine.T, sine.T
    cosine = jnp.concatenate([cosine] * 4, axis=1)
    sine = jnp.concatenate([-sine, sine, -sine, sine], axis=1)

    def counts_of(b):
        counts = []
        for x in BLOCK_XOR:
            block = tensor_index ^ x
            count = jnp.clip(lengths[b, 0] - block * row_share, 0, row_share)
            counts.append(jnp.where(block <= tensor_index, count, 0))
        return jnp.stack(counts).astype(jnp.int32)

    counts = [counts_of(b) for b in range(micro)]
    valid_rows = [
        jnp.clip(lengths[b, 0] - tensor_index * row_share, 0, row_share).astype(jnp.int32)
        for b in range(micro)
    ]
    valids = [
        (jnp.arange(row_share, dtype=jnp.int32) < valid_rows[b])[:, None] for b in range(micro)
    ]

    grad_own = jnp.stack(
        [jnp.where(valids[b], cotangent[b, 0], jnp.zeros((), BF16)) for b in range(micro)]
    )
    grad_far = far(grad_own)
    grad_near = near(jnp.stack([grad_own, grad_far]))
    grad_ffn = jnp.concatenate(
        [p[b] for b in range(micro) for p in (grad_own, grad_far, grad_near[0], grad_near[1])],
        axis=0,
    )

    x_rows = inputs[:, 0].reshape(micro * row_share, width)
    cot_rows = cotangent[:, 0].reshape(micro * row_share, width)
    cosine_all = jnp.concatenate([cosine] * micro, axis=0)
    sine_all = jnp.concatenate([sine] * micro, axis=0)
    pairs_own, normed = project_pairs(x_rows, gain_one, cosine_all, sine_all, attn_w)
    queries = project_queries(normed, cosine_all, sine_all, attn_w)
    kept = []
    attended = None
    for b in range(micro):
        own = pairs_own[b * row_share : (b + 1) * row_share]
        if b > 0:
            own, queries = lax.optimization_barrier((own, queries))
        across = far(own)
        if b == 0:
            across, queries = lax.optimization_barrier((across, queries))
        else:
            across, _ = lax.optimization_barrier((across, attended))
        others = [across, near(own), near(across)]
        attended = attend(b, counts[b], queries, pairs_own, others, attended)
        middle, hidden_own = leave(b, x_rows, attended, gain_two, attn_w)
        across = far(hidden_own)
        low = jnp.concatenate([hidden_own, across], axis=0)
        kept.append(dict(others=others, middle=middle, low=low, high=near(low)))
        if b == micro - 1:
            mlp_full, _ = lax.optimization_barrier((mlp_full, across))

    shared = None
    for b in range(micro):
        k = kept[b]
        if b > 0:
            k["low"], kept[b - 1]["far_sent"] = lax.optimization_barrier(
                (k["low"], kept[b - 1]["far_sent"])
            )
        *shared, k["out_low"], k["out_high"], k["part"], back_high = feed(
            b, k["low"], k["high"], grad_ffn, mlp_full, shared
        )
        k["near_part"] = near(back_high)
        k["far_sent"] = added(k["part"][row_share:], k["near_part"][row_share:])
    shared[0], kept[-1]["far_sent"] = lax.optimization_barrier((shared[0], kept[-1]["far_sent"]))
    hidden_rows, activated, inner_grads = shared
    grad_mlp_w = row_major(
        jnp.concatenate(
            [
                row_major(contract_rows(hidden_rows, inner_grads).astype(BF16)),
                row_major(contract_rows(grad_ffn, activated).astype(BF16)),
            ],
            axis=1,
        )
    )
    grad_mlp_w, kept[0]["middle"] = lax.optimization_barrier((grad_mlp_w, kept[0]["middle"]))

    gain_two_grads = []
    branch = query_grads = pair_grads = None

    grad_mlp_w = lax.psum_scatter(grad_mlp_w, "dp", scatter_dimension=0, tiled=True)
    for b in range(micro):
        k = kept[b]
        k["grad_middle"], branch, grad_att, gain_two_grad = enter(
            b,
            valid_rows[b][None],
            k["part"],
            k["near_part"],
            far(k["far_sent"]),
            k["middle"],
            cot_rows,
            gain_two,
            attn_w,
            branch,
        )
        gain_two_grads.append(gain_two_grad[0:1])
        k["out_high"], grad_att = lax.optimization_barrier((k["out_high"], grad_att))
        if b > 0:
            kept[b - 1]["pair_far"], grad_att = lax.optimization_barrier(
                (kept[b - 1]["pair_far"], grad_att)
            )
        query_grads, k["pair_kept"], pair_sent = attend_back(
            b, counts[b], queries, grad_att, cosine_t, sine_t, pairs_own, k["others"], query_grads
        )
        k["near_pair"] = near(pair_sent)
        k["pair_far"] = added(k["pair_kept"][row_share:], k["near_pair"][row_share:])
    for b in range(micro):
        k = kept[b]
        pair_grads = pairs_back(
            b, k["pair_kept"], k["near_pair"], far(k["pair_far"]), cosine, sine, pair_grads
        )

    outputs, input_grads, gain_one_grads = [], [], []
    for b in range(micro):
        k = kept[b]
        input_grad, gain_one_grad = finish(
            b, x_rows, query_grads, pair_grads, k["grad_middle"], gain_one, attn_w
        )
        gain_one_grads.append(gain_one_grad[0:1])
        input_grads.append(input_grad)
        out_near = near(k["out_high"])
        out_far = far(added(k["out_low"][row_share:], out_near[row_share:]))
        ffn_out = (
            k["out_low"][:row_share].astype(F32)
            + out_near[:row_share].astype(F32)
            + out_far.astype(F32)
        )
        outputs.append(jnp.where(valids[b], k["middle"] + ffn_out, 0.0).astype(BF16))

    odd = (tensor_index & 1) == 1
    high = (tensor_index & 2) == 2
    query_grad = [query_grads[:, c * third : (c + 1) * third] for c in range(3)]
    branch_grad = [branch[:, c * third : (c + 1) * third] for c in range(3)]
    key_grad, value_grad = pair_grads[:, :third], pair_grads[:, third:]

    def traded(left_even, right_even, left_odd, right_odd):
        def product(flag):
            left = left_even if left_even is left_odd else pick(flag, left_odd, left_even)
            return contract_rows(left, pick(flag, right_odd, right_even))

        sent = row_major(product(jnp.logical_not(odd)).astype(BF16))
        return row_major(product(odd)) + near(sent).astype(F32)

    query_low = traded(normed, query_grad[0], normed, query_grad[1])
    query_high = traded(normed, query_grad[2], attended, branch_grad[0])
    pair_low = traded(normed, key_grad, normed, value_grad)
    pair_high = traded(attended, branch_grad[1], attended, branch_grad[2])
    data_count = lax.axis_size("dp")
    gain_part = jnp.stack([sum(gain_one_grads), sum(gain_two_grads)])[:, 0]
    gain_part = jnp.moveaxis(gain_part.reshape(2, data_count, -1), 1, 0)
    gain_share = gain_part.shape[2]
    gain_part = jnp.pad(gain_part, ((0, 0), (0, 14), (0, third - gain_share)))
    first, second, gain_rows, grad_mlp_w = sum_over_data(
        (pick(high, pair_high, pair_low), pick(high, pair_low, pair_high)),
        (pick(high, query_high, query_low), pick(high, query_low, query_high)),
        gain_part,
        grad_mlp_w,
    )
    quarter = jnp.concatenate([first, second, gain_rows], axis=0).astype(BF16)
    other = far(quarter)
    pair = jnp.stack([pick(high, other, quarter), pick(high, quarter, other)])
    other = near(pair)
    even_pair, odd_pair = pick(odd, other, pair).astype(F32), pick(odd, pair, other).astype(F32)
    share = first.shape[0]
    chunks = [even_pair[0], odd_pair[0], even_pair[1], odd_pair[1]]
    gain_sum = sum(c[2 * share :] for c in chunks)
    first_of = [c[:share] for c in chunks]
    second_of = [c[share : 2 * share] for c in chunks]
    grad_mlp_w = grad_mlp_w.astype(F32)
    return (
        jnp.stack(outputs)[:, None],
        jnp.stack(input_grads)[:, None],
        gain_sum[0, :gain_share],
        gain_sum[1, :gain_share],
        jnp.concatenate(second_of[:3], axis=1),
        first_of[0],
        first_of[1],
        grad_mlp_w[:, :hidden_share],
        grad_mlp_w[:, hidden_share : 2 * hidden_share],
        jnp.concatenate([second_of[3], first_of[2], first_of[3]], axis=1),
        grad_mlp_w[:, 2 * hidden_share :].T,
    )


def solution(mesh):
    in_specs = (
        P(None, "dp", "tensor", None),
        P(None, "dp"),
        P("dp"),
        P("dp"),
        P("dp", None),
        P("dp", None),
        P("dp", None),
        P("dp", "tensor"),
        P("dp", "tensor"),
        P("dp", None),
        P("tensor", "dp"),
        P(None, "dp", "tensor", None),
    )
    out_specs = (
        P(None, "dp", "tensor", None),
        P(None, "dp", "tensor", None),
        P("dp"),
        P("dp"),
        P("dp", None),
        P("dp", None),
        P("dp", None),
        P("dp", "tensor"),
        P("dp", "tensor"),
        P("dp", None),
        P("tensor", "dp"),
    )
    return jax.shard_map(shards, mesh=mesh, in_specs=in_specs, out_specs=out_specs, check_vma=False)
```

```python
import functools

import jax
import jax.numpy as jnp
from jax import lax
from jax.experimental import pallas as pl
from jax.experimental.layout import Layout, with_layout_constraint
from jax.experimental.pallas import tpu as pltpu
from jax.sharding import PartitionSpec as P

HEAD_SIZE = 64
EPSILON = 1e-05
ROPE_BASE = 10000.0
MASKED = -1e30
BF16 = jnp.bfloat16
F32 = jnp.float32

BLOCK_XOR = (0, 2, 1, 3)


def near(value):
    count = lax.axis_size("tensor")
    return lax.ppermute(value, "tensor", [(i, i ^ 1) for i in range(count)])


def far(value):
    count = lax.axis_size("tensor")
    return lax.ppermute(value, "tensor", [(i, i ^ 2) for i in range(count)])


def dot(left_side, right_side):
    return jnp.dot(left_side, right_side, preferred_element_type=F32)


def contract_rows(left_side, right_side):
    return lax.dot_general(
        left_side, right_side, (((0,), (0,)), ((), ())), preferred_element_type=F32
    )


def dot_nt(left_side, right_side):
    return lax.dot_general(
        left_side, right_side, (((1,), (1,)), ((), ())), preferred_element_type=F32
    )


def dot_nn(left_side, right_side):
    return lax.dot_general(
        left_side, right_side, (((1,), (0,)), ((), ())), preferred_element_type=F32
    )


def head_of(ref, index):
    return ref[:, index * HEAD_SIZE : (index + 1) * HEAD_SIZE]


def row_scale_of(values):
    return lax.rsqrt(jnp.mean(values * values, axis=-1, keepdims=True) + EPSILON)


def turn(values, cosine, sine):
    lane = lax.broadcasted_iota(jnp.int32, (values.shape[0], 128), 1)
    first_half = lane % HEAD_SIZE < HEAD_SIZE // 2
    parts = []
    for start in range(0, values.shape[1], 128):
        part = values[:, start : start + 128]
        later = pltpu.roll(part, 128 - HEAD_SIZE // 2, 1)
        earlier = pltpu.roll(part, HEAD_SIZE // 2, 1)
        parts.append(part * cosine + jnp.where(first_half, later, earlier) * sine)
    return jnp.concatenate(parts, axis=1)


PAIR_CHUNKS = ((0, 0), (1, 0))
QUERY_CHUNKS = ((0, 1), (1, 1), (2, 1))
OUT_CHUNKS = ((3, 1), (2, 0), (3, 0))


def call(kernel, name, arrays, specs, outs, out_specs, scalars=(), aliases=None, **more):
    return pl.pallas_call(
        kernel,
        grid_spec=pltpu.PrefetchScalarGridSpec(
            num_scalar_prefetch=len(scalars),
            grid=more.get("grid", (1,)),
            in_specs=specs,
            out_specs=out_specs,
            scratch_shapes=more.get("scratch", ()),
        ),
        out_shape=outs,
        input_output_aliases=aliases or {},
        compiler_params=pltpu.CompilerParams(vmem_limit_bytes=KERNELS[name][0] << 20),
        cost_estimate=pl.CostEstimate(
            flops=int(KERNELS[name][1] * FLOPS_PER_MICROSECOND), transcendentals=0, bytes_accessed=1
        ),
        name=name,
    )(*scalars, *arrays)


def block(shape, at=(0, 0)):
    return pl.BlockSpec(shape, lambda *_: at)


def chunk_specs(width, chunks):
    return [block((width, width // 3), c) for c in chunks]


def array(shape, kind=BF16):
    return jax.ShapeDtypeStruct(shape, kind)


ANY = pl.BlockSpec(memory_space=pl.ANY)
KERNELS = {
    "project_pairs": (24, 1.8),
    "project_queries": (24, 2.6),
    "attend": (28, 11.3),
    "leave": (20, 1.4),
    "feed": (40, 18.5),
    "feed_grads": (32, 17.0),
    "enter": (24, 2.5),
    "attend_back": (36, 17.3),
    "pairs_back": (12, 0.8),
    "finish": (28, 2.2),
}
FLOPS_PER_MICROSECOND = 1.15e9


def project_pairs_kernel(x_ref, gain_ref, cosine_ref, sine_ref, wk, wv, pair_ref, normed_ref):
    values = x_ref[...].astype(F32)
    normed = (values * row_scale_of(values) * gain_ref[...]).astype(BF16)
    normed_ref[...] = normed
    keys = turn(dot_nn(normed, wk[...]), cosine_ref[...], sine_ref[...]).astype(BF16)
    values = dot_nn(normed, wv[...]).astype(BF16)
    for i in range(keys.shape[1] // 128):
        pair_ref[:, 256 * i : 256 * i + 128] = keys[:, 128 * i : 128 * (i + 1)]
        pair_ref[:, 256 * i + 128 : 256 * (i + 1)] = values[:, 128 * i : 128 * (i + 1)]


def project_pairs(x_rows, gain, cosine, sine, weights):
    rows, width = x_rows.shape
    pair_width = 2 * (width // 3)
    return call(
        project_pairs_kernel,
        "project_pairs",
        (x_rows, gain, cosine, sine, weights, weights),
        [block(x.shape) for x in (x_rows, gain, cosine, sine)] + chunk_specs(width, PAIR_CHUNKS),
        [array((rows, pair_width)), array((rows, width))],
        [block((rows, pair_width)), block((rows, width))],
    )


def project_queries_kernel(normed_ref, cosine_ref, sine_ref, w0, w1, w2, query_ref):
    third = w0.shape[1]
    for i, w in enumerate((w0, w1, w2)):
        turned = turn(dot_nn(normed_ref[...], w[...]), cosine_ref[...], sine_ref[...])
        query_ref[:, i * third : (i + 1) * third] = (turned * HEAD_SIZE ** (-0.5)).astype(BF16)


def project_queries(normed, cosine, sine, weights):
    rows, width = normed.shape
    return call(
        project_queries_kernel,
        "project_queries",
        (normed, cosine, sine, weights, weights, weights),
        [block(x.shape) for x in (normed, cosine, sine)] + chunk_specs(width, QUERY_CHUNKS),
        array((rows, width)),
        block((rows, width)),
    )


def attend_kernel(group, counts, q_ref, p0, p1, p2, p3, *rest):
    o_ref = rest[-1]
    rows = q_ref.shape[0]
    refs = (p0, p1, p2, p3)
    row = lax.broadcasted_iota(jnp.int32, (rows, rows), 0)
    col = lax.broadcasted_iota(jnp.int32, (rows, rows), 1)
    allowed = [jnp.logical_and(col <= row, col < counts[0])]
    allowed += [col < counts[j] for j in range(1, 4)]
    allowed = [jnp.concatenate([a] * group, axis=0) for a in allowed]
    for pair in range(2):
        queries = jnp.concatenate([head_of(q_ref, pair * group + i) for i in range(group)], axis=0)
        scores = [
            jnp.where(allowed[j], dot_nt(queries, head_of(refs[j], pair)), MASKED)
            for j in range(4)
        ]
        top = functools.reduce(jnp.maximum, [jnp.max(s, axis=1, keepdims=True) for s in scores])
        soft = [jnp.exp(s - top) for s in scores]
        total = functools.reduce(jnp.add, [jnp.sum(s, axis=1, keepdims=True) for s in soft])
        out = functools.reduce(
            jnp.add, [dot_nn(soft[j].astype(BF16), head_of(refs[j], 2 + pair)) for j in range(4)]
        )
        out = (out / total).astype(BF16)
        for i in range(group):
            start = (pair * group + i) * HEAD_SIZE
            o_ref[:, start : start + HEAD_SIZE] = out[i * rows : (i + 1) * rows]


def attention_sizes(queries, pairs_own):
    rows = queries.shape[0] // 2
    steps = pairs_own.shape[1] // (4 * HEAD_SIZE)
    group = queries.shape[1] // (2 * HEAD_SIZE * steps)
    return rows, steps, group


def attend(b, counts, queries, pairs_own, others, earlier):
    rows, steps, group = attention_sizes(queries, pairs_own)
    width = queries.shape[1]
    query_spec = pl.BlockSpec((rows, width // steps), lambda i, c: (b, i))
    own_spec = pl.BlockSpec((rows, 4 * HEAD_SIZE), lambda i, c: (b, i))
    pair_spec = pl.BlockSpec((rows, 4 * HEAD_SIZE), lambda i, c: (0, i))
    more = [] if earlier is None else [earlier]
    return call(
        functools.partial(attend_kernel, group),
        "attend",
        (queries, pairs_own, *others, *more),
        [query_spec, own_spec] + [pair_spec] * 3 + [ANY] * len(more),
        array(queries.shape),
        query_spec,
        (counts,),
        {6: 0} if more else None,
        grid=(steps,),
    )


def attend_back_kernel(group, counts, q_ref, g_ref, cos_ref, sin_ref, p0, p1, p2, p3, *rest):
    dq_ref, kept_ref, sent_ref, turned_ref = rest[-4:]
    rows = q_ref.shape[0]
    half = HEAD_SIZE // 2
    both = jnp.concatenate([p0[...], p1[...], p2[...], p3[...]], axis=0)
    keys, values = both[:, :128], both[:, 128:]
    keys_t = keys.T
    row = lax.broadcasted_iota(jnp.int32, (rows, rows), 0)
    col = lax.broadcasted_iota(jnp.int32, (rows, rows), 1)
    allowed = [jnp.logical_and(row <= col, row < counts[0])]
    allowed += [row < counts[j] for j in range(1, 4)]
    allowed = jnp.concatenate([jnp.concatenate([a] * group, axis=1) for a in allowed], axis=0)
    key_grads, value_grads = [], []
    for pair in range(2):
        lanes = slice(pair * HEAD_SIZE, (pair + 1) * HEAD_SIZE)
        key, value = keys[:, lanes], values[:, lanes]
        queries = jnp.concatenate([head_of(q_ref, pair * group + i) for i in range(group)], axis=0)
        grads = jnp.concatenate([head_of(g_ref, pair * group + i) for i in range(group)], axis=0)
        scores = jnp.where(allowed, dot_nt(key, queries), MASKED)
        soft = jnp.exp(scores - jnp.max(scores, axis=0, keepdims=True))
        soft = soft * (1.0 / jnp.sum(soft, axis=0, keepdims=True))
        grad_soft = dot_nt(value, grads)
        scaled = soft * grad_soft
        grad_scores = (scaled - soft * jnp.sum(scaled, axis=0, keepdims=True)).astype(BF16)
        value_grads.append(dot_nn(soft.astype(BF16), grads))
        key_grads.append(dot_nn(grad_scores, queries))
        query_grad = dot_nn(keys_t[lanes, :], grad_scores) * HEAD_SIZE ** (-0.5)
        for i in range(group):
            part = query_grad[:, i * rows : (i + 1) * rows]
            first, second = part[:half], part[half:]
            start = (pair * group + i) * HEAD_SIZE
            turned_ref[start : start + half, :] = first * cos_ref[...] + second * sin_ref[...]
            turned_ref[start + half : start + HEAD_SIZE, :] = (
                second * cos_ref[...] - first * sin_ref[...]
            )
    grads = jnp.concatenate(key_grads + value_grads, axis=1).astype(BF16)
    kept_ref[...] = grads[: 2 * rows]
    sent_ref[...] = grads[2 * rows :]
    dq_ref[...] = turned_ref[...].T.astype(BF16)


def attend_back(b, counts, queries, grads, cosine_t, sine_t, pairs_own, others, earlier):
    rows, steps, group = attention_sizes(queries, pairs_own)
    width = queries.shape[1]
    query_spec = pl.BlockSpec((rows, width // steps), lambda i, c: (b, i))
    grad_spec = pl.BlockSpec((rows, width // steps), lambda i, c: (0, i))
    own_spec = pl.BlockSpec((rows, 4 * HEAD_SIZE), lambda i, c: (b, i))
    pair_spec = pl.BlockSpec((rows, 4 * HEAD_SIZE), lambda i, c: (0, i))
    half_spec = pl.BlockSpec((2 * rows, 4 * HEAD_SIZE), lambda i, c: (0, i))
    more = [] if earlier is None else [earlier]
    return call(
        functools.partial(attend_back_kernel, group),
        "attend_back",
        (queries, grads, cosine_t, sine_t, pairs_own, *others, *more),
        [query_spec, grad_spec, block(cosine_t.shape), block(sine_t.shape), own_spec]
        + [pair_spec] * 3
        + [ANY] * len(more),
        [array(queries.shape)] + [array((2 * rows, pairs_own.shape[1]))] * 2,
        [query_spec, half_spec, half_spec],
        (counts,),
        {9: 0} if more else None,
        grid=(steps,),
        scratch=[pltpu.VMEM((width // steps, rows), F32)],
    )


def leave_kernel(x_ref, o_ref, gain_ref, w0, w1, w2, middle_ref, normed_ref):
    out = o_ref[...]
    added = jnp.concatenate([dot_nn(out, w[...]) for w in (w0, w1, w2)], axis=1)
    middle = x_ref[...].astype(F32) + added
    middle_ref[...] = middle
    normed_ref[...] = (middle * row_scale_of(middle) * gain_ref[...]).astype(BF16)


def leave(b, x_rows, attended, gain, weights):
    rows, width = x_rows.shape[0] // 2, x_rows.shape[1]
    here = block((rows, width), (b, 0))
    return call(
        leave_kernel,
        "leave",
        (x_rows, attended, gain, weights, weights, weights),
        [here, here, block(gain.shape)] + chunk_specs(width, OUT_CHUNKS),
        [array((rows, width), F32), array((rows, width))],
        [block((rows, width))] * 2,
    )


def feed_kernel(steps, places, low_ref, high_ref, grad_ref, weight_ref, *rest):
    rows_ref, act_ref, inner_ref, out_ref, back_low, back_high = rest[-6:]
    step = pl.program_id(0)
    share = weight_ref.shape[1] // 3
    gate, up, down_t = (slice(i * share, (i + 1) * share) for i in range(3))

    @pl.when(step < steps // 2)
    def _():
        rows_ref[...] = low_ref[...]

    @pl.when(step >= steps // 2)
    def _():
        rows_ref[...] = high_ref[...]

    rows = rows_ref[...]
    gate_proj = dot_nn(rows, weight_ref[:, gate])
    up_proj = dot_nn(rows, weight_ref[:, up])
    grad_act = dot_nn(grad_ref[...], weight_ref[:, down_t])
    sigma = 1.0 / (1.0 + jnp.exp(-gate_proj))
    silu = gate_proj * sigma
    act = (silu * up_proj).astype(BF16)
    act_ref[...] = act
    grad_gate = (grad_act * up_proj * sigma * (1.0 + gate_proj * (1.0 - sigma))).astype(BF16)
    grad_up = (grad_act * silu).astype(BF16)
    inner_ref[:, gate] = grad_gate
    inner_ref[:, up] = grad_up
    back = dot_nt(grad_gate, weight_ref[:, gate]) + dot_nt(grad_up, weight_ref[:, up])
    out_ref[...] = dot_nt(act, weight_ref[:, down_t]).astype(BF16)

    @pl.when(step < steps // 2)
    def _():
        back_low[...] = back.astype(BF16)

    @pl.when(step >= steps // 2)
    def _():
        back_high[...] = back.astype(BF16)


def feed(b, places, low, high, grads, weights, earlier):
    half, width = low.shape
    share = weights.shape[1] // 3
    steps = 4
    rows = 2 * half // steps
    first = pl.BlockSpec((rows, width), lambda i, p: (jnp.minimum(i, steps // 2 - 1), 0))
    second = pl.BlockSpec((rows, width), lambda i, p: (jnp.maximum(i - steps // 2, 0), 0))

    def here(columns):
        return pl.BlockSpec((rows, columns), lambda i, p: (b * steps + i, 0))

    more = [] if earlier is None else list(earlier)
    return call(
        functools.partial(feed_kernel, steps),
        "feed",
        (low, high, grads, weights, *more),
        [
            first,
            second,
            here(width),
            pl.BlockSpec(weights.shape, lambda i, p: (0, 0), pipeline_mode=pl.Buffered(1)),
        ]
        + [ANY] * len(more),
        [array((4 * half, width)), array((4 * half, share)), array((4 * half, 2 * share))]
        + [array((2 * half, width))]
        + [array((half, width))] * 2,
        [here(width), here(share), here(2 * share)]
        + [pl.BlockSpec((rows, width), lambda i, p: (p[i], 0)), first, second],
        (places,),
        aliases={5: 0, 6: 1, 7: 2} if more else None,
        grid=(steps,),
    )


def feed_grads_kernel(rows_ref, grad_ref, inner_ref, act_ref, out_ref):
    share = act_ref.shape[1]
    out_ref[:, : 2 * share] = dot_nn(rows_ref[...].T, inner_ref[...]).astype(BF16)
    out_ref[:, 2 * share :] = dot_nn(grad_ref[...].T, act_ref[...]).astype(BF16)


def feed_grads(rows, grads, inner_grads, activated):
    count, width = rows.shape
    share = activated.shape[1]
    steps = 3
    left = pl.BlockSpec((count, width // steps), lambda i: (0, i))

    def held(columns):
        return pl.BlockSpec((count, columns), lambda i: (0, 0), pipeline_mode=pl.Buffered(1))

    return call(
        feed_grads_kernel,
        "feed_grads",
        (rows, grads, inner_grads, activated),
        [left, left, held(2 * share), held(share)],
        array((width, 3 * share)),
        pl.BlockSpec((width // steps, 3 * share), lambda i: (i, 0)),
        grid=(steps,),
    )


def enter_kernel(
    count, part_ref, near_ref, far_ref, middle_ref, cot_ref, gain_ref, w0, w1, w2, *rest
):
    grad_middle_ref, branch_ref, out_ref, gain_grad_ref = rest[-4:]
    rows, width = middle_ref.shape
    third = width // 3
    middle = middle_ref[...]
    grad_normed = (
        part_ref[...].astype(F32) + near_ref[...].astype(F32) + far_ref[...].astype(F32)
    )
    scale = row_scale_of(middle)
    row = lax.broadcasted_iota(jnp.int32, (rows, width), 0)
    grad_row = jnp.where(row < count[0], cot_ref[...].astype(F32), 0.0)
    gain_grad = jnp.sum(grad_normed * middle * scale, axis=0, keepdims=True)
    gain_grad_ref[...] = jnp.broadcast_to(gain_grad, gain_grad_ref.shape)
    inner = grad_normed * gain_ref[...]
    grad_middle = grad_row + (
        scale * inner - middle * scale**3 * jnp.mean(inner * middle, axis=-1, keepdims=True)
    )
    grad_middle_ref[...] = grad_middle
    branch = grad_middle.astype(BF16)
    branch_ref[...] = branch
    weights = (w0, w1, w2)
    out = dot_nt(branch[:, :third], w0[...])
    for c in range(1, 3):
        out = out + dot_nt(branch[:, c * third : (c + 1) * third], weights[c][...])
    out_ref[...] = out.astype(BF16)


def enter(b, count, part, near_part, far_part, middle, cot_rows, gain, weights, earlier):
    rows, width = middle.shape
    full, here = block((rows, width)), block((rows, width), (b, 0))
    more = [] if earlier is None else [earlier]
    return call(
        enter_kernel,
        "enter",
        (part, near_part, far_part, middle, cot_rows, gain, weights, weights, weights, *more),
        [full, full, full, full, here, block(gain.shape)]
        + chunk_specs(width, OUT_CHUNKS)
        + [ANY] * len(more),
        [
            array((rows, width), F32),
            array((2 * rows, width)),
            array((rows, width)),
            array((8, width), F32),
        ],
        [full, here, full, block((8, width))],
        (count,),
        {10: 1} if more else None,
    )


def pairs_back_kernel(kept_ref, near_ref, far_ref, cosine_ref, sine_ref, *rest):
    pair_ref = rest[-1]
    width = pair_ref.shape[1] // 2
    for i in range(width // 128):
        lanes = slice(256 * i, 256 * (i + 1))
        total = (
            kept_ref[:, lanes].astype(F32)
            + near_ref[:, lanes].astype(F32)
            + far_ref[:, lanes].astype(F32)
        )
        turned = turn(total[:, :128], cosine_ref[...], -sine_ref[...])
        pair_ref[:, 128 * i : 128 * (i + 1)] = turned.astype(BF16)
        pair_ref[:, width + 128 * i : width + 128 * (i + 1)] = total[:, 128:].astype(BF16)


def pairs_back(b, kept, near_part, far_part, cosine, sine, earlier):
    rows, width = far_part.shape
    first = block((rows, width))
    table = block((rows, 128))
    more = [] if earlier is None else [earlier]
    return call(
        pairs_back_kernel,
        "pairs_back",
        (kept, near_part, far_part, cosine, sine, *more),
        [first, first, first, table, table] + [ANY] * len(more),
        array((2 * rows, width)),
        block((rows, width), (b, 0)),
        aliases={5: 0} if more else None,
    )


def finish_kernel(
    x_ref, query_ref, pair_ref, middle_ref, gain_ref, wk, wv, w0, w1, w2, grad_ref, gain_grad_ref
):
    third = x_ref.shape[1] // 3
    grads = [pair_ref[:, :third], pair_ref[:, third:]]
    grads += [query_ref[:, c * third : (c + 1) * third] for c in range(3)]
    grad_normed = dot_nt(grads[0], wk[...])
    for grad, w in zip(grads[1:], (wv, w0, w1, w2)):
        grad_normed = grad_normed + dot_nt(grad, w[...])
    values = x_ref[...].astype(F32)
    scale = row_scale_of(values)
    gain_grad = jnp.sum(grad_normed * values * scale, axis=0, keepdims=True)
    gain_grad_ref[...] = jnp.broadcast_to(gain_grad, gain_grad_ref.shape)
    inner = grad_normed * gain_ref[...]
    grad_ref[...] = (
        middle_ref[...]
        + scale * inner
        - values * scale**3 * jnp.mean(inner * values, axis=-1, keepdims=True)
    ).astype(BF16)


def finish(b, x_rows, query_grads, pair_grads, grad_middle, gain, weights):
    rows, width = grad_middle.shape
    here = block((rows, width), (b, 0))
    return call(
        finish_kernel,
        "finish",
        (x_rows, query_grads, pair_grads, grad_middle, gain, *([weights] * 5)),
        [here, here, block((rows, pair_grads.shape[1]), (b, 0)), block((rows, width))]
        + [block(gain.shape)]
        + chunk_specs(width, PAIR_CHUNKS + QUERY_CHUNKS),
        [array((rows, width)), array((8, width), F32)],
        [block((rows, width)), block((8, width))],
    )


def row_major(value):
    return with_layout_constraint(value, Layout(major_to_minor=tuple(range(value.ndim))))


def added(first, second):
    return (first.astype(F32) + second.astype(F32)).astype(BF16)


def pick(flag, first, second):
    return jnp.where(flag, first, second)


def sum_over_data(part_a, part_b, extra, earlier):
    data_count = lax.axis_size("dp")
    data_index = lax.axis_index("dp")
    columns = part_a[0].shape[1]

    def split(value):
        return value.reshape(data_count, -1, columns)

    if data_count != 8:
        total = part_a[0] + far(part_a[1].astype(BF16)).astype(F32)
        other = part_b[0] + far(part_b[1].astype(BF16)).astype(F32)
        rows = jnp.concatenate([split(total), split(other), extra], axis=1).astype(BF16)
        rows = lax.psum_scatter(rows, "dp", scatter_dimension=0, tiled=True)[0].astype(F32)
        share = total.shape[0] // data_count
        return rows[:share], rows[share : 2 * share], rows[2 * share :], earlier

    groups = data_count // 2
    odd = (data_index & 1) == 1
    group = lax.shift_right_logical(data_index, 1)

    def beside(value):
        even_rows, odd_rows = value[..., 0, :, :], value[..., 1, :, :]
        sent = pick(odd, even_rows, odd_rows).astype(BF16)
        came = lax.ppermute(sent, "dp", [(i, i ^ 1) for i in range(data_count)])
        return pick(odd, odd_rows, even_rows).astype(F32) + came.astype(F32)

    def along(value):
        low = value.astype(BF16)
        total = lax.dynamic_index_in_dim(
            value, group, 0, keepdims=False, allow_negative_indices=False
        )
        for step in range(1, groups):
            sent = lax.dynamic_index_in_dim(
                low, (group + step) & (groups - 1), 0, keepdims=False, allow_negative_indices=False
            )
            moves = [(i, (i + 2 * step) % data_count) for i in range(data_count)]
            total = total + lax.ppermute(sent, "dp", moves).astype(F32)
        return total

    second = jnp.stack([split(p) for p in part_b], axis=0)
    second = beside(second.reshape(2, groups, 2, -1, columns))
    first = split(part_a[0] + far(part_a[1].astype(BF16)).astype(F32))
    first = jnp.concatenate([first, extra], axis=1).reshape(groups, 2, -1, columns)
    first, earlier = lax.optimization_barrier((beside(first), earlier))
    second = along(jnp.moveaxis(second, 1, 0))
    first = along(first)
    second = second[0] + far(second[1].astype(BF16)).astype(F32)
    share = second.shape[0]
    return first[:share], second, first[share:], earlier


def shards(
    inputs,
    lengths,
    gain_attn,
    gain_mlp,
    w_query,
    key_weight,
    value_weight,
    w_gate,
    w_up,
    w_out,
    w_down,
    cotangent,
):
    micro = inputs.shape[0]
    row_share = inputs.shape[2]
    width = inputs.shape[3]
    tensor_count = lax.axis_size("tensor")
    tensor_index = lax.axis_index("tensor")
    hidden_share = w_gate.shape[1]

    third = width // 3

    out_parts = [w_out[:, c * third : (c + 1) * third] for c in range(3)]
    query_parts = [w_query[:, c * third : (c + 1) * third] for c in range(3)]
    attn_quarter = lax.select_n(
        tensor_index,
        jnp.concatenate([key_weight, query_parts[0]], axis=1),
        jnp.concatenate([value_weight, query_parts[1]], axis=1),
        jnp.concatenate([out_parts[1], query_parts[2]], axis=1),
        jnp.concatenate([out_parts[2], out_parts[0]], axis=1),
    )
    attn_w = lax.all_gather(attn_quarter, ("tensor", "dp"), axis=0, tiled=True)
    mlp_local = jnp.concatenate([w_gate, w_up, w_down.T], axis=1)
    mlp_full = lax.all_gather(mlp_local, "dp", axis=0, tiled=True)
    gains = lax.all_gather(jnp.stack([gain_attn, gain_mlp]), "dp", axis=1, tiled=True).astype(F32)
    gain_one, gain_two = gains[0:1], gains[1:2]

    query_pos = tensor_index * row_share + jnp.arange(row_share, dtype=jnp.int32)
    exponent = jnp.arange(HEAD_SIZE // 2, dtype=F32) * (2.0 / HEAD_SIZE)
    angles = query_pos.astype(F32)[:, None] * (ROPE_BASE ** (-exponent))[None, :]
    cosine, sine = jnp.cos(angles), jnp.sin(angles)
    cosine_t, sine_t = cosine.T, sine.T
    cosine = jnp.concatenate([cosine] * 4, axis=1)
    sine = jnp.concatenate([-sine, sine, -sine, sine], axis=1)

    def counts_of(b):
        counts = []
        for x in BLOCK_XOR:
            block = tensor_index ^ x
            count = jnp.clip(lengths[b, 0] - block * row_share, 0, row_share)
            counts.append(jnp.where(block <= tensor_index, count, 0))
        return jnp.stack(counts).astype(jnp.int32)

    counts = [counts_of(b) for b in range(micro)]
    valid_rows = [
        jnp.clip(lengths[b, 0] - tensor_index * row_share, 0, row_share).astype(jnp.int32)
        for b in range(micro)
    ]
    valids = [
        (jnp.arange(row_share, dtype=jnp.int32) < valid_rows[b])[:, None] for b in range(micro)
    ]

    grad_own = jnp.stack(
        [jnp.where(valids[b], cotangent[b, 0], jnp.zeros((), BF16)) for b in range(micro)]
    )
    grad_far = far(grad_own)
    grad_near = near(jnp.stack([grad_own, grad_far]))
    grad_ffn = jnp.concatenate(
        [p[b] for b in range(micro) for p in (grad_own, grad_far, grad_near[0], grad_near[1])],
        axis=0,
    )

    x_rows = inputs[:, 0].reshape(micro * row_share, width)
    cot_rows = cotangent[:, 0].reshape(micro * row_share, width)
    cosine_all = jnp.concatenate([cosine] * micro, axis=0)
    sine_all = jnp.concatenate([sine] * micro, axis=0)
    pairs_own, normed = project_pairs(x_rows, gain_one, cosine_all, sine_all, attn_w)
    queries = project_queries(normed, cosine_all, sine_all, attn_w)
    kept = []
    attended = None
    for b in range(micro):
        own = pairs_own[b * row_share : (b + 1) * row_share]
        if b > 0:
            own, queries = lax.optimization_barrier((own, queries))
        across = far(own)
        if b == 0:
            across, queries = lax.optimization_barrier((across, queries))
        else:
            across, _ = lax.optimization_barrier((across, attended))
        others = [across, near(own), near(across)]
        attended = attend(b, counts[b], queries, pairs_own, others, attended)
        middle, hidden_own = leave(b, x_rows, attended, gain_two, attn_w)
        across = far(hidden_own)
        low = jnp.concatenate([hidden_own, across], axis=0)
        kept.append(dict(others=others, middle=middle, low=low, high=near(low)))
        if b == micro - 1:
            mlp_full, _ = lax.optimization_barrier((mlp_full, across))

    places = jnp.stack([tensor_index ^ x for x in BLOCK_XOR]).astype(jnp.int32)
    shared = None
    for b in range(micro):
        k = kept[b]
        *shared, k["out"], k["part"], back_high = feed(
            b, places, k["low"], k["high"], grad_ffn, mlp_full, shared
        )
        if b > 0:
            back_high, kept[b - 1]["far_part"] = lax.optimization_barrier(
                (back_high, far(kept[b - 1]["far_part"]))
            )
        k["near_part"] = near(back_high)
        k["far_part"] = added(k["part"][row_share:], k["near_part"][row_share:])
    hidden_rows, activated, inner_grads = shared
    hidden_rows, kept[-1]["far_part"] = lax.optimization_barrier(
        (hidden_rows, kept[-1]["far_part"])
    )
    kept[-1]["far_part"] = far(kept[-1]["far_part"])
    grad_mlp_w = feed_grads(hidden_rows, grad_ffn, inner_grads, activated)
    grad_mlp_w, kept[0]["middle"], kept[-1]["far_part"] = lax.optimization_barrier(
        (grad_mlp_w, kept[0]["middle"], kept[-1]["far_part"])
    )

    gain_two_grads = []
    branch = query_grads = pair_grads = None

    grad_mlp_w = lax.psum_scatter(grad_mlp_w, "dp", scatter_dimension=0, tiled=True)
    def summed_out(b):
        return lax.psum_scatter(kept[b]["out"], "tensor", scatter_dimension=0, tiled=True)

    kept[0]["out"] = summed_out(0)
    for b in range(micro):
        k = kept[b]
        k["grad_middle"], branch, grad_att, gain_two_grad = enter(
            b,
            valid_rows[b][None],
            k["part"],
            k["near_part"],
            k["far_part"],
            k["middle"],
            cot_rows,
            gain_two,
            attn_w,
            branch,
        )
        gain_two_grads.append(gain_two_grad[0:1])
        if b > 0:
            k["out"], grad_att = lax.optimization_barrier((k["out"], grad_att))
            k["out"] = summed_out(b)
            kept[b - 1]["pair_far"], grad_att = lax.optimization_barrier(
                (kept[b - 1]["pair_far"], grad_att)
            )
        query_grads, k["pair_kept"], pair_sent = attend_back(
            b, counts[b], queries, grad_att, cosine_t, sine_t, pairs_own, k["others"], query_grads
        )
        k["near_pair"] = near(pair_sent)
        k["pair_far"] = added(k["pair_kept"][row_share:], k["near_pair"][row_share:])
    for b in range(micro):
        k = kept[b]
        pair_grads = pairs_back(
            b, k["pair_kept"], k["near_pair"], far(k["pair_far"]), cosine, sine, pair_grads
        )

    input_grads, gain_one_grads = [], []
    for b in range(micro):
        k = kept[b]
        input_grad, gain_one_grad = finish(
            b, x_rows, query_grads, pair_grads, k["grad_middle"], gain_one, attn_w
        )
        gain_one_grads.append(gain_one_grad[0:1])
        input_grads.append(input_grad)

    odd = (tensor_index & 1) == 1
    high = (tensor_index & 2) == 2
    query_grad = [query_grads[:, c * third : (c + 1) * third] for c in range(3)]
    branch_grad = [branch[:, c * third : (c + 1) * third] for c in range(3)]
    key_grad, value_grad = pair_grads[:, :third], pair_grads[:, third:]

    def traded(left_even, right_even, left_odd, right_odd):
        def product(flag):
            left = left_even if left_even is left_odd else pick(flag, left_odd, left_even)
            return contract_rows(left, pick(flag, right_odd, right_even))

        sent = row_major(product(jnp.logical_not(odd)).astype(BF16))
        return row_major(product(odd)) + near(sent).astype(F32)

    query_low = traded(normed, query_grad[0], normed, query_grad[1])
    query_high = traded(normed, query_grad[2], attended, branch_grad[0])
    pair_low = traded(normed, key_grad, normed, value_grad)
    pair_high = traded(attended, branch_grad[1], attended, branch_grad[2])
    data_count = lax.axis_size("dp")
    gain_part = jnp.stack([sum(gain_one_grads), sum(gain_two_grads)])[:, 0]
    gain_part = jnp.moveaxis(gain_part.reshape(2, data_count, -1), 1, 0)
    gain_share = gain_part.shape[2]
    gain_part = jnp.pad(gain_part, ((0, 0), (0, 14), (0, third - gain_share)))
    first, second, gain_rows, grad_mlp_w = sum_over_data(
        (pick(high, pair_high, pair_low), pick(high, pair_low, pair_high)),
        (pick(high, query_high, query_low), pick(high, query_low, query_high)),
        gain_part,
        grad_mlp_w,
    )
    outputs = []
    for b in range(micro):
        k = kept[b]
        ffn_out = k["out"].astype(F32)
        outputs.append(jnp.where(valids[b], k["middle"] + ffn_out, 0.0).astype(BF16))
    quarter = jnp.concatenate([first, second, gain_rows], axis=0).astype(BF16)
    other = far(quarter)
    pair = jnp.stack([pick(high, other, quarter), pick(high, quarter, other)])
    other = near(pair)
    even_pair, odd_pair = pick(odd, other, pair).astype(F32), pick(odd, pair, other).astype(F32)
    share = first.shape[0]
    chunks = [even_pair[0], odd_pair[0], even_pair[1], odd_pair[1]]
    gain_sum = sum(c[2 * share :] for c in chunks)
    first_of = [c[:share] for c in chunks]
    second_of = [c[share : 2 * share] for c in chunks]
    grad_mlp_w = grad_mlp_w.astype(F32)
    return (
        jnp.stack(outputs)[:, None],
        jnp.stack(input_grads)[:, None],
        gain_sum[0, :gain_share],
        gain_sum[1, :gain_share],
        jnp.concatenate(second_of[:3], axis=1),
        first_of[0],
        first_of[1],
        grad_mlp_w[:, :hidden_share],
        grad_mlp_w[:, hidden_share : 2 * hidden_share],
        jnp.concatenate([second_of[3], first_of[2], first_of[3]], axis=1),
        grad_mlp_w[:, 2 * hidden_share :].T,
    )


def solution(mesh):
    in_specs = (
        P(None, "dp", "tensor", None),
        P(None, "dp"),
        P("dp"),
        P("dp"),
        P("dp", None),
        P("dp", None),
        P("dp", None),
        P("dp", "tensor"),
        P("dp", "tensor"),
        P("dp", None),
        P("tensor", "dp"),
        P(None, "dp", "tensor", None),
    )
    out_specs = (
        P(None, "dp", "tensor", None),
        P(None, "dp", "tensor", None),
        P("dp"),
        P("dp"),
        P("dp", None),
        P("dp", None),
        P("dp", None),
        P("dp", "tensor"),
        P("dp", "tensor"),
        P("dp", None),
        P("tensor", "dp"),
    )
    return jax.shard_map(shards, mesh=mesh, in_specs=in_specs, out_specs=out_specs, check_vma=False)
```

```python
import functools

import jax
import jax.numpy as jnp
from jax import lax
from jax.experimental import pallas as pl
from jax.experimental.layout import Layout, with_layout_constraint
from jax.experimental.pallas import tpu as pltpu
from jax.sharding import PartitionSpec as P

HEAD_SIZE = 64
EPSILON = 1e-05
ROPE_BASE = 10000.0
MASKED = -1e30
BF16 = jnp.bfloat16
F32 = jnp.float32

BLOCK_XOR = (0, 2, 1, 3)


def near(value):
    count = lax.axis_size("tensor")
    return lax.ppermute(value, "tensor", [(i, i ^ 1) for i in range(count)])


def far(value):
    count = lax.axis_size("tensor")
    return lax.ppermute(value, "tensor", [(i, i ^ 2) for i in range(count)])


def dot(left_side, right_side):
    return jnp.dot(left_side, right_side, preferred_element_type=F32)


def contract_rows(left_side, right_side):
    return lax.dot_general(
        left_side, right_side, (((0,), (0,)), ((), ())), preferred_element_type=F32
    )


def spread(own, came):
    index = lax.axis_index("tensor")
    odd, high = (index & 1) == 1, (index & 2) == 2
    pair = jnp.stack([jnp.where(high, came, own), jnp.where(high, own, came)])
    other = near(pair)
    rows = jnp.stack([jnp.where(odd, other, pair), jnp.where(odd, pair, other)], axis=1)
    return rows.reshape(-1, own.shape[1])


def dot_nt(left_side, right_side):
    return lax.dot_general(
        left_side, right_side, (((1,), (1,)), ((), ())), preferred_element_type=F32
    )


def dot_nn(left_side, right_side):
    return lax.dot_general(
        left_side, right_side, (((1,), (0,)), ((), ())), preferred_element_type=F32
    )


def head_of(ref, index):
    return ref[:, index * HEAD_SIZE : (index + 1) * HEAD_SIZE]


def row_scale_of(values):
    return lax.rsqrt(jnp.mean(values * values, axis=-1, keepdims=True) + EPSILON)


def turn(values, cosine, sine):
    lane = lax.broadcasted_iota(jnp.int32, (values.shape[0], 128), 1)
    first_half = lane % HEAD_SIZE < HEAD_SIZE // 2
    parts = []
    for start in range(0, values.shape[1], 128):
        part = values[:, start : start + 128]
        later = pltpu.roll(part, 128 - HEAD_SIZE // 2, 1)
        earlier = pltpu.roll(part, HEAD_SIZE // 2, 1)
        parts.append(part * cosine + jnp.where(first_half, later, earlier) * sine)
    return jnp.concatenate(parts, axis=1)


PAIR_CHUNKS = ((0, 0), (1, 0))
QUERY_CHUNKS = ((0, 1), (1, 1), (2, 1))
OUT_CHUNKS = ((3, 1), (2, 0), (3, 0))


def call(kernel, name, arrays, specs, outs, out_specs, scalars=(), aliases=None, **more):
    return pl.pallas_call(
        kernel,
        grid_spec=pltpu.PrefetchScalarGridSpec(
            num_scalar_prefetch=len(scalars),
            grid=more.get("grid", (1,)),
            in_specs=specs,
            out_specs=out_specs,
            scratch_shapes=more.get("scratch", ()),
        ),
        out_shape=outs,
        input_output_aliases=aliases or {},
        compiler_params=pltpu.CompilerParams(vmem_limit_bytes=KERNELS[name][0] << 20),
        cost_estimate=pl.CostEstimate(
            flops=int(KERNELS[name][1] * FLOPS_PER_MICROSECOND), transcendentals=0, bytes_accessed=1
        ),
        name=name,
    )(*scalars, *arrays)


def block(shape, at=(0, 0)):
    return pl.BlockSpec(shape, lambda *_: at)


def chunk_specs(width, chunks):
    return [block((width, width // 3), (owner, 0)) for owner, _ in chunks]


def chunk_arrays(weights, chunks):
    return [weights[half] for _, half in chunks]


def array(shape, kind=BF16):
    return jax.ShapeDtypeStruct(shape, kind)


ANY = pl.BlockSpec(memory_space=pl.ANY)
KERNELS = {
    "project_pairs": (24, 1.8),
    "project_queries": (24, 2.6),
    "attend": (28, 11.3),
    "leave": (20, 1.4),
    "feed": (58, 18.5),
    "feed_grads": (58, 17.0),
    "enter": (58, 2.5),
    "attend_back": (58, 17.3),
    "pairs_back": (12, 0.8),
    "finish": (28, 2.2),
}
FLOPS_PER_MICROSECOND = 1.15e9


def project_pairs_kernel(x_ref, gain_ref, cosine_ref, sine_ref, wk, wv, pair_ref, normed_ref):
    values = x_ref[...].astype(F32)
    normed = (values * row_scale_of(values) * gain_ref[...]).astype(BF16)
    normed_ref[...] = normed
    keys = turn(dot_nn(normed, wk[...]), cosine_ref[...], sine_ref[...]).astype(BF16)
    values = dot_nn(normed, wv[...]).astype(BF16)
    for i in range(keys.shape[1] // 128):
        pair_ref[:, 256 * i : 256 * i + 128] = keys[:, 128 * i : 128 * (i + 1)]
        pair_ref[:, 256 * i + 128 : 256 * (i + 1)] = values[:, 128 * i : 128 * (i + 1)]


def project_pairs(x_rows, gain, cosine, sine, weights):
    rows, width = x_rows.shape
    pair_width = 2 * (width // 3)
    return call(
        project_pairs_kernel,
        "project_pairs",
        (x_rows, gain, cosine, sine, *chunk_arrays(weights, PAIR_CHUNKS)),
        [block(x.shape) for x in (x_rows, gain, cosine, sine)] + chunk_specs(width, PAIR_CHUNKS),
        [array((rows, pair_width)), array((rows, width))],
        [block((rows, pair_width)), block((rows, width))],
    )


def project_queries_kernel(normed_ref, cosine_ref, sine_ref, w0, w1, w2, query_ref):
    third = w0.shape[1]
    for i, w in enumerate((w0, w1, w2)):
        turned = turn(dot_nn(normed_ref[...], w[...]), cosine_ref[...], sine_ref[...])
        query_ref[:, i * third : (i + 1) * third] = (turned * HEAD_SIZE ** (-0.5)).astype(BF16)


def project_queries(normed, cosine, sine, weights):
    rows, width = normed.shape
    return call(
        project_queries_kernel,
        "project_queries",
        (normed, cosine, sine, *chunk_arrays(weights, QUERY_CHUNKS)),
        [block(x.shape) for x in (normed, cosine, sine)] + chunk_specs(width, QUERY_CHUNKS),
        array((rows, width)),
        block((rows, width)),
    )


def attend_kernel(group, counts, q_ref, p0, p1, p2, p3, *rest):
    o_ref = rest[-1]
    rows = q_ref.shape[0]
    refs = (p0, p1, p2, p3)
    row = lax.broadcasted_iota(jnp.int32, (rows, rows), 0)
    col = lax.broadcasted_iota(jnp.int32, (rows, rows), 1)
    allowed = [jnp.logical_and(col <= row, col < counts[0])]
    allowed += [col < counts[j] for j in range(1, 4)]
    allowed = [jnp.concatenate([a] * group, axis=0) for a in allowed]
    for pair in range(2):
        queries = jnp.concatenate([head_of(q_ref, pair * group + i) for i in range(group)], axis=0)
        scores = [
            jnp.where(allowed[j], dot_nt(queries, head_of(refs[j], pair)), MASKED)
            for j in range(4)
        ]
        top = functools.reduce(jnp.maximum, [jnp.max(s, axis=1, keepdims=True) for s in scores])
        soft = [jnp.exp(s - top) for s in scores]
        total = functools.reduce(jnp.add, [jnp.sum(s, axis=1, keepdims=True) for s in soft])
        out = functools.reduce(
            jnp.add, [dot_nn(soft[j].astype(BF16), head_of(refs[j], 2 + pair)) for j in range(4)]
        )
        out = (out / total).astype(BF16)
        for i in range(group):
            start = (pair * group + i) * HEAD_SIZE
            o_ref[:, start : start + HEAD_SIZE] = out[i * rows : (i + 1) * rows]


def attention_sizes(queries, pairs_own):
    rows = queries.shape[0] // 2
    steps = pairs_own.shape[1] // (4 * HEAD_SIZE)
    group = queries.shape[1] // (2 * HEAD_SIZE * steps)
    return rows, steps, group


def attend(b, counts, queries, pairs_own, others, earlier):
    rows, steps, group = attention_sizes(queries, pairs_own)
    width = queries.shape[1]
    query_spec = pl.BlockSpec((rows, width // steps), lambda i, c: (b, i))
    own_spec = pl.BlockSpec((rows, 4 * HEAD_SIZE), lambda i, c: (b, i))
    pair_spec = pl.BlockSpec((rows, 4 * HEAD_SIZE), lambda i, c: (0, i))
    more = [] if earlier is None else [earlier]
    return call(
        functools.partial(attend_kernel, group),
        "attend",
        (queries, pairs_own, *others, *more),
        [query_spec, own_spec] + [pair_spec] * 3 + [ANY] * len(more),
        array(queries.shape),
        query_spec,
        (counts,),
        {6: 0} if more else None,
        grid=(steps,),
    )


def attend_back_kernel(group, counts, q_ref, g_ref, cos_ref, sin_ref, p0, p1, p2, p3, *rest):
    dq_ref, kept_ref, sent_ref, turned_ref = rest[-4:]
    rows = q_ref.shape[0]
    half = HEAD_SIZE // 2
    both = jnp.concatenate([p0[...], p1[...], p2[...], p3[...]], axis=0)
    keys, values = both[:, :128], both[:, 128:]
    keys_t = keys.T
    row = lax.broadcasted_iota(jnp.int32, (rows, rows), 0)
    col = lax.broadcasted_iota(jnp.int32, (rows, rows), 1)
    allowed = [jnp.logical_and(row <= col, row < counts[0])]
    allowed += [row < counts[j] for j in range(1, 4)]
    allowed = jnp.concatenate([jnp.concatenate([a] * group, axis=1) for a in allowed], axis=0)
    key_grads, value_grads = [], []
    for pair in range(2):
        lanes = slice(pair * HEAD_SIZE, (pair + 1) * HEAD_SIZE)
        key, value = keys[:, lanes], values[:, lanes]
        queries = jnp.concatenate([head_of(q_ref, pair * group + i) for i in range(group)], axis=0)
        grads = jnp.concatenate([head_of(g_ref, pair * group + i) for i in range(group)], axis=0)
        scores = jnp.where(allowed, dot_nt(key, queries), MASKED)
        soft = jnp.exp(scores - jnp.max(scores, axis=0, keepdims=True))
        soft = soft * (1.0 / jnp.sum(soft, axis=0, keepdims=True))
        grad_soft = dot_nt(value, grads)
        scaled = soft * grad_soft
        grad_scores = (scaled - soft * jnp.sum(scaled, axis=0, keepdims=True)).astype(BF16)
        value_grads.append(dot_nn(soft.astype(BF16), grads))
        key_grads.append(dot_nn(grad_scores, queries))
        query_grad = dot_nn(keys_t[lanes, :], grad_scores) * HEAD_SIZE ** (-0.5)
        for i in range(group):
            part = query_grad[:, i * rows : (i + 1) * rows]
            first, second = part[:half], part[half:]
            start = (pair * group + i) * HEAD_SIZE
            turned_ref[start : start + half, :] = first * cos_ref[...] + second * sin_ref[...]
            turned_ref[start + half : start + HEAD_SIZE, :] = (
                second * cos_ref[...] - first * sin_ref[...]
            )
    grads = jnp.concatenate(key_grads + value_grads, axis=1).astype(BF16)
    kept_ref[...] = grads[: 2 * rows]
    sent_ref[...] = grads[2 * rows :]
    dq_ref[...] = turned_ref[...].T.astype(BF16)


def attend_back(b, counts, queries, grads, cosine_t, sine_t, pairs_own, others, earlier):
    rows, steps, group = attention_sizes(queries, pairs_own)
    width = queries.shape[1]
    query_spec = pl.BlockSpec((rows, width // steps), lambda i, c: (b, i))
    grad_spec = pl.BlockSpec((rows, width // steps), lambda i, c: (0, i))
    own_spec = pl.BlockSpec((rows, 4 * HEAD_SIZE), lambda i, c: (b, i))
    pair_spec = pl.BlockSpec((rows, 4 * HEAD_SIZE), lambda i, c: (0, i))
    half_spec = pl.BlockSpec((2 * rows, 4 * HEAD_SIZE), lambda i, c: (0, i))
    more = [] if earlier is None else [earlier]
    return call(
        functools.partial(attend_back_kernel, group),
        "attend_back",
        (queries, grads, cosine_t, sine_t, pairs_own, *others, *more),
        [query_spec, grad_spec, block(cosine_t.shape), block(sine_t.shape), own_spec]
        + [pair_spec] * 3
        + [ANY] * len(more),
        [array(queries.shape)] + [array((2 * rows, pairs_own.shape[1]))] * 2,
        [query_spec, half_spec, half_spec],
        (counts,),
        {9: 0} if more else None,
        grid=(steps,),
        scratch=[pltpu.VMEM((width // steps, rows), F32)],
    )


def leave_kernel(x_ref, o_ref, gain_ref, w0, w1, w2, middle_ref, normed_ref):
    out = o_ref[...]
    added = jnp.concatenate([dot_nn(out, w[...]) for w in (w0, w1, w2)], axis=1)
    middle = x_ref[...].astype(F32) + added
    middle_ref[...] = middle
    normed_ref[...] = (middle * row_scale_of(middle) * gain_ref[...]).astype(BF16)


def leave(b, x_rows, attended, gain, weights):
    rows, width = x_rows.shape[0] // 2, x_rows.shape[1]
    here = block((rows, width), (b, 0))
    return call(
        leave_kernel,
        "leave",
        (x_rows, attended, gain, *chunk_arrays(weights, OUT_CHUNKS)),
        [here, here, block(gain.shape)] + chunk_specs(width, OUT_CHUNKS),
        [array((rows, width), F32), array((rows, width))],
        [block((rows, width))] * 2,
    )


def feed_kernel(steps, places, low_ref, high_ref, grad_ref, weight_ref, *rest):
    rows_ref, act_ref, inner_ref, out_ref, back_low, back_high = rest[-6:]
    step = pl.program_id(0)
    share = weight_ref.shape[1] // 3
    gate, up, down_t = (slice(i * share, (i + 1) * share) for i in range(3))

    @pl.when(step < steps // 2)
    def _():
        rows_ref[...] = low_ref[...]

    @pl.when(step >= steps // 2)
    def _():
        rows_ref[...] = high_ref[...]

    rows = rows_ref[...]
    gate_proj = dot_nn(rows, weight_ref[:, gate])
    up_proj = dot_nn(rows, weight_ref[:, up])
    grad_act = dot_nn(grad_ref[...], weight_ref[:, down_t])
    sigma = 1.0 / (1.0 + jnp.exp(-gate_proj))
    silu = gate_proj * sigma
    act = (silu * up_proj).astype(BF16)
    act_ref[...] = act
    grad_gate = (grad_act * up_proj * sigma * (1.0 + gate_proj * (1.0 - sigma))).astype(BF16)
    grad_up = (grad_act * silu).astype(BF16)
    inner_ref[:, gate] = grad_gate
    inner_ref[:, up] = grad_up
    back = dot_nt(grad_gate, weight_ref[:, gate]) + dot_nt(grad_up, weight_ref[:, up])
    out_ref[...] = dot_nt(act, weight_ref[:, down_t]).astype(BF16)

    @pl.when(step < steps // 2)
    def _():
        back_low[...] = back.astype(BF16)

    @pl.when(step >= steps // 2)
    def _():
        back_high[...] = back.astype(BF16)


def feed(b, places, low, high, grads, weights, earlier):
    half, width = low.shape
    share = weights.shape[1] // 3
    steps = 4
    rows = 2 * half // steps
    first = pl.BlockSpec((rows, width), lambda i, p: (jnp.minimum(i, steps // 2 - 1), 0))
    second = pl.BlockSpec((rows, width), lambda i, p: (jnp.maximum(i - steps // 2, 0), 0))

    def here(columns):
        return pl.BlockSpec((rows, columns), lambda i, p: (b * steps + i, 0))

    more = [] if earlier is None else list(earlier)
    return call(
        functools.partial(feed_kernel, steps),
        "feed",
        (low, high, grads, weights, *more),
        [
            first,
            second,
            here(width),
            pl.BlockSpec(weights.shape, lambda i, p: (0, 0), pipeline_mode=pl.Buffered(1)),
        ]
        + [ANY] * len(more),
        [array((4 * half, width)), array((4 * half, share)), array((4 * half, 2 * share))]
        + [array((2 * half, width))]
        + [array((half, width))] * 2,
        [here(width), here(share), here(2 * share)]
        + [pl.BlockSpec((rows, width), lambda i, p: (p[i], 0)), first, second],
        (places,),
        aliases={5: 0, 6: 1, 7: 2} if more else None,
        grid=(steps,),
    )


def feed_grads_kernel(rows_ref, grad_ref, inner_ref, act_ref, out_ref):
    share = act_ref.shape[1]
    out_ref[:, : 2 * share] = dot_nn(rows_ref[...].T, inner_ref[...]).astype(BF16)
    out_ref[:, 2 * share :] = dot_nn(grad_ref[...].T, act_ref[...]).astype(BF16)


def feed_grads(rows, grads, inner_grads, activated):
    count, width = rows.shape
    share = activated.shape[1]
    steps = 3
    left = pl.BlockSpec((count, width // steps), lambda i: (0, i))

    def held(columns):
        return pl.BlockSpec((count, columns), lambda i: (0, 0), pipeline_mode=pl.Buffered(1))

    return call(
        feed_grads_kernel,
        "feed_grads",
        (rows, grads, inner_grads, activated),
        [left, left, held(2 * share), held(share)],
        array((width, 3 * share)),
        pl.BlockSpec((width // steps, 3 * share), lambda i: (i, 0)),
        grid=(steps,),
    )


def enter_kernel(
    count, part_ref, near_ref, far_ref, middle_ref, cot_ref, gain_ref, w0, w1, w2, *rest
):
    grad_middle_ref, branch_ref, out_ref, gain_grad_ref = rest[-4:]
    rows, width = middle_ref.shape
    third = width // 3
    middle = middle_ref[...]
    grad_normed = (
        part_ref[...].astype(F32) + near_ref[...].astype(F32) + far_ref[...].astype(F32)
    )
    scale = row_scale_of(middle)
    row = lax.broadcasted_iota(jnp.int32, (rows, width), 0)
    grad_row = jnp.where(row < count[0], cot_ref[...].astype(F32), 0.0)
    gain_grad = jnp.sum(grad_normed * middle * scale, axis=0, keepdims=True)
    gain_grad_ref[...] = jnp.broadcast_to(gain_grad, gain_grad_ref.shape)
    inner = grad_normed * gain_ref[...]
    grad_middle = grad_row + (
        scale * inner - middle * scale**3 * jnp.mean(inner * middle, axis=-1, keepdims=True)
    )
    grad_middle_ref[...] = grad_middle
    branch = grad_middle.astype(BF16)
    branch_ref[...] = branch
    weights = (w0, w1, w2)
    out = dot_nt(branch[:, :third], w0[...])
    for c in range(1, 3):
        out = out + dot_nt(branch[:, c * third : (c + 1) * third], weights[c][...])
    out_ref[...] = out.astype(BF16)


def enter(b, count, part, near_part, far_part, middle, cot_rows, gain, weights, earlier):
    rows, width = middle.shape
    full, here = block((rows, width)), block((rows, width), (b, 0))
    more = [] if earlier is None else [earlier]
    return call(
        enter_kernel,
        "enter",
        (part, near_part, far_part, middle, cot_rows, gain)
        + (*chunk_arrays(weights, OUT_CHUNKS), *more),
        [full, full, full, full, here, block(gain.shape)]
        + chunk_specs(width, OUT_CHUNKS)
        + [ANY] * len(more),
        [
            array((rows, width), F32),
            array((2 * rows, width)),
            array((rows, width)),
            array((8, width), F32),
        ],
        [full, here, full, block((8, width))],
        (count,),
        {10: 1} if more else None,
    )


def pairs_back_kernel(kept_ref, near_ref, far_ref, cosine_ref, sine_ref, *rest):
    pair_ref = rest[-1]
    width = pair_ref.shape[1] // 2
    for i in range(width // 128):
        lanes = slice(256 * i, 256 * (i + 1))
        total = (
            kept_ref[:, lanes].astype(F32)
            + near_ref[:, lanes].astype(F32)
            + far_ref[:, lanes].astype(F32)
        )
        turned = turn(total[:, :128], cosine_ref[...], -sine_ref[...])
        pair_ref[:, 128 * i : 128 * (i + 1)] = turned.astype(BF16)
        pair_ref[:, width + 128 * i : width + 128 * (i + 1)] = total[:, 128:].astype(BF16)


def pairs_back(b, kept, near_part, far_part, cosine, sine, earlier):
    rows, width = far_part.shape
    first = block((rows, width))
    table = block((rows, 128))
    more = [] if earlier is None else [earlier]
    return call(
        pairs_back_kernel,
        "pairs_back",
        (kept, near_part, far_part, cosine, sine, *more),
        [first, first, first, table, table] + [ANY] * len(more),
        array((2 * rows, width)),
        block((rows, width), (b, 0)),
        aliases={5: 0} if more else None,
    )


def finish_kernel(
    x_ref, query_ref, pair_ref, middle_ref, gain_ref, wk, wv, w0, w1, w2, grad_ref, gain_grad_ref
):
    third = x_ref.shape[1] // 3
    grads = [pair_ref[:, :third], pair_ref[:, third:]]
    grads += [query_ref[:, c * third : (c + 1) * third] for c in range(3)]
    grad_normed = dot_nt(grads[0], wk[...])
    for grad, w in zip(grads[1:], (wv, w0, w1, w2)):
        grad_normed = grad_normed + dot_nt(grad, w[...])
    values = x_ref[...].astype(F32)
    scale = row_scale_of(values)
    gain_grad = jnp.sum(grad_normed * values * scale, axis=0, keepdims=True)
    gain_grad_ref[...] = jnp.broadcast_to(gain_grad, gain_grad_ref.shape)
    inner = grad_normed * gain_ref[...]
    grad_ref[...] = (
        middle_ref[...]
        + scale * inner
        - values * scale**3 * jnp.mean(inner * values, axis=-1, keepdims=True)
    ).astype(BF16)


def finish(b, x_rows, query_grads, pair_grads, grad_middle, gain, weights):
    rows, width = grad_middle.shape
    here = block((rows, width), (b, 0))
    return call(
        finish_kernel,
        "finish",
        (x_rows, query_grads, pair_grads, grad_middle, gain)
        + (*chunk_arrays(weights, PAIR_CHUNKS + QUERY_CHUNKS),),
        [here, here, block((rows, pair_grads.shape[1]), (b, 0)), block((rows, width))]
        + [block(gain.shape)]
        + chunk_specs(width, PAIR_CHUNKS + QUERY_CHUNKS),
        [array((rows, width)), array((8, width), F32)],
        [block((rows, width)), block((8, width))],
    )


def row_major(value):
    return with_layout_constraint(value, Layout(major_to_minor=tuple(range(value.ndim))))


def added(first, second):
    return (first.astype(F32) + second.astype(F32)).astype(BF16)


def pick(flag, first, second):
    return jnp.where(flag, first, second)


def sum_over_data(part_a, part_b, extra, earlier):
    data_count = lax.axis_size("dp")
    data_index = lax.axis_index("dp")
    columns = part_a[0].shape[1]

    def split(value):
        return value.reshape(data_count, -1, columns)

    if data_count != 8:
        total = part_a[0] + far(part_a[1].astype(BF16)).astype(F32)
        other = part_b[0] + far(part_b[1].astype(BF16)).astype(F32)
        rows = jnp.concatenate([split(total), split(other), extra], axis=1).astype(BF16)
        rows = lax.psum_scatter(rows, "dp", scatter_dimension=0, tiled=True)[0].astype(F32)
        share = total.shape[0] // data_count
        return rows[:share], rows[share : 2 * share], rows[2 * share :], earlier

    groups = data_count // 2
    odd = (data_index & 1) == 1
    group = lax.shift_right_logical(data_index, 1)

    def beside(value):
        even_rows, odd_rows = value[..., 0, :, :], value[..., 1, :, :]
        sent = pick(odd, even_rows, odd_rows).astype(BF16)
        came = lax.ppermute(sent, "dp", [(i, i ^ 1) for i in range(data_count)])
        return pick(odd, odd_rows, even_rows).astype(F32) + came.astype(F32)

    def along(value):
        low = value.astype(BF16)
        total = lax.dynamic_index_in_dim(
            value, group, 0, keepdims=False, allow_negative_indices=False
        )
        for step in range(1, groups):
            sent = lax.dynamic_index_in_dim(
                low, (group + step) & (groups - 1), 0, keepdims=False, allow_negative_indices=False
            )
            moves = [(i, (i + 2 * step) % data_count) for i in range(data_count)]
            total = total + lax.ppermute(sent, "dp", moves).astype(F32)
        return total

    second = jnp.stack([split(p) for p in part_b], axis=0)
    second = beside(second.reshape(2, groups, 2, -1, columns))
    first = split(part_a[0] + far(part_a[1].astype(BF16)).astype(F32))
    first = jnp.concatenate([first, extra], axis=1).reshape(groups, 2, -1, columns)
    first, earlier = lax.optimization_barrier((beside(first), earlier))
    second = along(jnp.moveaxis(second, 1, 0))
    first = along(first)
    second = second[0] + far(second[1].astype(BF16)).astype(F32)
    share = second.shape[0]
    return first[:share], second, first[share:], earlier


def shards(
    inputs,
    lengths,
    gain_attn,
    gain_mlp,
    w_query,
    key_weight,
    value_weight,
    w_gate,
    w_up,
    w_out,
    w_down,
    cotangent,
):
    micro = inputs.shape[0]
    row_share = inputs.shape[2]
    width = inputs.shape[3]
    tensor_count = lax.axis_size("tensor")
    tensor_index = lax.axis_index("tensor")
    hidden_share = w_gate.shape[1]

    third = width // 3

    out_parts = [w_out[:, c * third : (c + 1) * third] for c in range(3)]
    query_parts = [w_query[:, c * third : (c + 1) * third] for c in range(3)]
    attn_quarter = lax.select_n(
        tensor_index,
        jnp.concatenate([key_weight, query_parts[0]], axis=1),
        jnp.concatenate([value_weight, query_parts[1]], axis=1),
        jnp.concatenate([out_parts[1], query_parts[2]], axis=1),
        jnp.concatenate([out_parts[2], out_parts[0]], axis=1),
    )
    attn_own = lax.all_gather(attn_quarter, "dp", axis=0, tiled=True)
    mlp_local = jnp.concatenate([w_gate, w_up, w_down.T], axis=1)
    mlp_full = lax.all_gather(mlp_local, "dp", axis=0, tiled=True)
    gains = lax.all_gather(jnp.stack([gain_attn, gain_mlp]), "dp", axis=1, tiled=True).astype(F32)
    gain_one, gain_two = gains[0:1], gains[1:2]

    query_pos = tensor_index * row_share + jnp.arange(row_share, dtype=jnp.int32)
    exponent = jnp.arange(HEAD_SIZE // 2, dtype=F32) * (2.0 / HEAD_SIZE)
    angles = query_pos.astype(F32)[:, None] * (ROPE_BASE ** (-exponent))[None, :]
    cosine, sine = jnp.cos(angles), jnp.sin(angles)
    cosine_t, sine_t = cosine.T, sine.T
    cosine = jnp.concatenate([cosine] * 4, axis=1)
    sine = jnp.concatenate([-sine, sine, -sine, sine], axis=1)

    def counts_of(b):
        counts = []
        for x in BLOCK_XOR:
            block = tensor_index ^ x
            count = jnp.clip(lengths[b, 0] - block * row_share, 0, row_share)
            counts.append(jnp.where(block <= tensor_index, count, 0))
        return jnp.stack(counts).astype(jnp.int32)

    counts = [counts_of(b) for b in range(micro)]
    valid_rows = [
        jnp.clip(lengths[b, 0] - tensor_index * row_share, 0, row_share).astype(jnp.int32)
        for b in range(micro)
    ]
    valids = [
        (jnp.arange(row_share, dtype=jnp.int32) < valid_rows[b])[:, None] for b in range(micro)
    ]

    grad_own = jnp.stack(
        [jnp.where(valids[b], cotangent[b, 0], jnp.zeros((), BF16)) for b in range(micro)]
    )
    grad_far = far(grad_own)
    grad_near = near(jnp.stack([grad_own, grad_far]))
    grad_ffn = jnp.concatenate(
        [p[b] for b in range(micro) for p in (grad_own, grad_far, grad_near[0], grad_near[1])],
        axis=0,
    )

    low, high_own = attn_own[:, :third], attn_own[:, third:]
    came, high_own = lax.optimization_barrier((far(low), high_own))
    attn_w = (spread(low, came), spread(high_own, far(high_own)))
    x_rows = inputs[:, 0].reshape(micro * row_share, width)
    cot_rows = cotangent[:, 0].reshape(micro * row_share, width)
    cosine_all = jnp.concatenate([cosine] * micro, axis=0)
    sine_all = jnp.concatenate([sine] * micro, axis=0)
    pairs_own, normed = project_pairs(x_rows, gain_one, cosine_all, sine_all, attn_w)
    queries = project_queries(normed, cosine_all, sine_all, attn_w)
    kept = []
    attended = None
    for b in range(micro):
        own = pairs_own[b * row_share : (b + 1) * row_share]
        if b > 0:
            own, queries = lax.optimization_barrier((own, queries))
        across = far(own)
        if b == 0:
            across, queries = lax.optimization_barrier((across, queries))
        else:
            across, _ = lax.optimization_barrier((across, attended))
        others = [across, near(own), near(across)]
        attended = attend(b, counts[b], queries, pairs_own, others, attended)
        middle, hidden_own = leave(b, x_rows, attended, gain_two, attn_w)
        kept.append(dict(others=others, middle=middle, own=hidden_own, across=far(hidden_own)))
    mlp_full, _ = lax.optimization_barrier((mlp_full, kept[-1]["own"]))
    kept[0]["across"], _ = lax.optimization_barrier((kept[0]["across"], attended))
    for k in kept:
        k["low"] = jnp.concatenate([k["own"], k["across"]], axis=0)
        k["high"] = near(k["low"])

    places = jnp.stack([tensor_index ^ x for x in BLOCK_XOR]).astype(jnp.int32)
    shared = None
    for b in range(micro):
        k = kept[b]
        *shared, k["out"], k["part"], back_high = feed(
            b, places, k["low"], k["high"], grad_ffn, mlp_full, shared
        )
        if b > 0:
            back_high, kept[b - 1]["far_part"] = lax.optimization_barrier(
                (back_high, far(kept[b - 1]["far_part"]))
            )
        k["near_part"] = near(back_high)
        k["far_part"] = added(k["part"][row_share:], k["near_part"][row_share:])
    hidden_rows, activated, inner_grads = shared
    hidden_rows, kept[-1]["far_part"] = lax.optimization_barrier(
        (hidden_rows, kept[-1]["far_part"])
    )
    kept[-1]["far_part"] = far(kept[-1]["far_part"])
    grad_mlp_w = feed_grads(hidden_rows, grad_ffn, inner_grads, activated)
    grad_mlp_w, kept[0]["middle"], kept[-1]["far_part"] = lax.optimization_barrier(
        (grad_mlp_w, kept[0]["middle"], kept[-1]["far_part"])
    )

    gain_two_grads = []
    branch = query_grads = pair_grads = None

    grad_mlp_w = lax.psum_scatter(grad_mlp_w, "dp", scatter_dimension=0, tiled=True)
    def summed_out(b):
        return lax.psum_scatter(kept[b]["out"], "tensor", scatter_dimension=0, tiled=True)

    kept[0]["out"] = summed_out(0)
    for b in range(micro):
        k = kept[b]
        k["grad_middle"], branch, grad_att, gain_two_grad = enter(
            b,
            valid_rows[b][None],
            k["part"],
            k["near_part"],
            k["far_part"],
            k["middle"],
            cot_rows,
            gain_two,
            attn_w,
            branch,
        )
        gain_two_grads.append(gain_two_grad[0:1])
        if b > 0:
            k["out"], grad_att = lax.optimization_barrier((k["out"], grad_att))
            k["out"] = summed_out(b)
            kept[b - 1]["pair_far"], grad_att = lax.optimization_barrier(
                (kept[b - 1]["pair_far"], grad_att)
            )
        query_grads, k["pair_kept"], pair_sent = attend_back(
            b, counts[b], queries, grad_att, cosine_t, sine_t, pairs_own, k["others"], query_grads
        )
        k["near_pair"] = near(pair_sent)
        k["pair_far"] = added(k["pair_kept"][row_share:], k["near_pair"][row_share:])
    for b in range(micro):
        k = kept[b]
        pair_grads = pairs_back(
            b, k["pair_kept"], k["near_pair"], far(k["pair_far"]), cosine, sine, pair_grads
        )

    input_grads, gain_one_grads = [], []
    for b in range(micro):
        k = kept[b]
        input_grad, gain_one_grad = finish(
            b, x_rows, query_grads, pair_grads, k["grad_middle"], gain_one, attn_w
        )
        gain_one_grads.append(gain_one_grad[0:1])
        input_grads.append(input_grad)

    odd = (tensor_index & 1) == 1
    high = (tensor_index & 2) == 2
    query_grad = [query_grads[:, c * third : (c + 1) * third] for c in range(3)]
    branch_grad = [branch[:, c * third : (c + 1) * third] for c in range(3)]
    key_grad, value_grad = pair_grads[:, :third], pair_grads[:, third:]

    def traded(left_even, right_even, left_odd, right_odd):
        def product(flag):
            left = left_even if left_even is left_odd else pick(flag, left_odd, left_even)
            return contract_rows(left, pick(flag, right_odd, right_even))

        sent = row_major(product(jnp.logical_not(odd)).astype(BF16))
        return row_major(product(odd)) + near(sent).astype(F32)

    query_low = traded(normed, query_grad[0], normed, query_grad[1])
    query_high = traded(normed, query_grad[2], attended, branch_grad[0])
    pair_low = traded(normed, key_grad, normed, value_grad)
    pair_high = traded(attended, branch_grad[1], attended, branch_grad[2])
    data_count = lax.axis_size("dp")
    gain_part = jnp.stack([sum(gain_one_grads), sum(gain_two_grads)])[:, 0]
    gain_part = jnp.moveaxis(gain_part.reshape(2, data_count, -1), 1, 0)
    gain_share = gain_part.shape[2]
    gain_part = jnp.pad(gain_part, ((0, 0), (0, 14), (0, third - gain_share)))
    first, second, gain_rows, grad_mlp_w = sum_over_data(
        (pick(high, pair_high, pair_low), pick(high, pair_low, pair_high)),
        (pick(high, query_high, query_low), pick(high, query_low, query_high)),
        gain_part,
        grad_mlp_w,
    )
    outputs = []
    for b in range(micro):
        k = kept[b]
        ffn_out = k["out"].astype(F32)
        outputs.append(jnp.where(valids[b], k["middle"] + ffn_out, 0.0).astype(BF16))
    quarter = jnp.concatenate([first, second, gain_rows], axis=0).astype(BF16)
    other = far(quarter)
    pair = jnp.stack([pick(high, other, quarter), pick(high, quarter, other)])
    other = near(pair)
    even_pair, odd_pair = pick(odd, other, pair).astype(F32), pick(odd, pair, other).astype(F32)
    share = first.shape[0]
    chunks = [even_pair[0], odd_pair[0], even_pair[1], odd_pair[1]]
    gain_sum = sum(c[2 * share :] for c in chunks)
    first_of = [c[:share] for c in chunks]
    second_of = [c[share : 2 * share] for c in chunks]
    grad_mlp_w = grad_mlp_w.astype(F32)
    return (
        jnp.stack(outputs)[:, None],
        jnp.stack(input_grads)[:, None],
        gain_sum[0, :gain_share],
        gain_sum[1, :gain_share],
        jnp.concatenate(second_of[:3], axis=1),
        first_of[0],
        first_of[1],
        grad_mlp_w[:, :hidden_share],
        grad_mlp_w[:, hidden_share : 2 * hidden_share],
        jnp.concatenate([second_of[3], first_of[2], first_of[3]], axis=1),
        grad_mlp_w[:, 2 * hidden_share :].T,
    )


def solution(mesh):
    in_specs = (
        P(None, "dp", "tensor", None),
        P(None, "dp"),
        P("dp"),
        P("dp"),
        P("dp", None),
        P("dp", None),
        P("dp", None),
        P("dp", "tensor"),
        P("dp", "tensor"),
        P("dp", None),
        P("tensor", "dp"),
        P(None, "dp", "tensor", None),
    )
    out_specs = (
        P(None, "dp", "tensor", None),
        P(None, "dp", "tensor", None),
        P("dp"),
        P("dp"),
        P("dp", None),
        P("dp", None),
        P("dp", None),
        P("dp", "tensor"),
        P("dp", "tensor"),
        P("dp", None),
        P("tensor", "dp"),
    )
    return jax.shard_map(shards, mesh=mesh, in_specs=in_specs, out_specs=out_specs, check_vma=False)
```

```python
import functools

import jax
import jax.numpy as jnp
from jax import lax
from jax.experimental import pallas as pl
from jax.experimental.layout import Layout, with_layout_constraint
from jax.experimental.pallas import tpu as pltpu
from jax.sharding import PartitionSpec as P

HEAD_SIZE = 64
EPSILON = 1e-05
ROPE_BASE = 10000.0
MASKED = -1e30
BF16 = jnp.bfloat16
F32 = jnp.float32

BLOCK_XOR = (0, 2, 1, 3)


def near(value):
    count = lax.axis_size("tensor")
    return lax.ppermute(value, "tensor", [(i, i ^ 1) for i in range(count)])


def far(value):
    count = lax.axis_size("tensor")
    return lax.ppermute(value, "tensor", [(i, i ^ 2) for i in range(count)])


def dot(left_side, right_side):
    return jnp.dot(left_side, right_side, preferred_element_type=F32)


def contract_rows(left_side, right_side):
    return lax.dot_general(
        left_side, right_side, (((0,), (0,)), ((), ())), preferred_element_type=F32
    )


def spread(own, came):
    index = lax.axis_index("tensor")
    odd, high = (index & 1) == 1, (index & 2) == 2
    pair = jnp.stack([jnp.where(high, came, own), jnp.where(high, own, came)])
    other = near(pair)
    rows = jnp.stack([jnp.where(odd, other, pair), jnp.where(odd, pair, other)], axis=1)
    return rows.reshape(-1, own.shape[1])


def dot_nt(left_side, right_side):
    return lax.dot_general(
        left_side, right_side, (((1,), (1,)), ((), ())), preferred_element_type=F32
    )


def dot_nn(left_side, right_side):
    return lax.dot_general(
        left_side, right_side, (((1,), (0,)), ((), ())), preferred_element_type=F32
    )


def head_of(ref, index):
    return ref[:, index * HEAD_SIZE : (index + 1) * HEAD_SIZE]


def row_scale_of(values):
    return lax.rsqrt(jnp.mean(values * values, axis=-1, keepdims=True) + EPSILON)


def turn(values, cosine, sine):
    lane = lax.broadcasted_iota(jnp.int32, (values.shape[0], 128), 1)
    first_half = lane % HEAD_SIZE < HEAD_SIZE // 2
    parts = []
    for start in range(0, values.shape[1], 128):
        part = values[:, start : start + 128]
        later = pltpu.roll(part, 128 - HEAD_SIZE // 2, 1)
        earlier = pltpu.roll(part, HEAD_SIZE // 2, 1)
        parts.append(part * cosine + jnp.where(first_half, later, earlier) * sine)
    return jnp.concatenate(parts, axis=1)


PAIR_CHUNKS = ((0, 0), (1, 0))
QUERY_CHUNKS = ((0, 1), (1, 1), (2, 1))
OUT_CHUNKS = ((3, 1), (2, 0), (3, 0))


def call(kernel, name, arrays, specs, outs, out_specs, scalars=(), aliases=None, **more):
    return pl.pallas_call(
        kernel,
        grid_spec=pltpu.PrefetchScalarGridSpec(
            num_scalar_prefetch=len(scalars),
            grid=more.get("grid", (1,)),
            in_specs=specs,
            out_specs=out_specs,
            scratch_shapes=more.get("scratch", ()),
        ),
        out_shape=outs,
        input_output_aliases=aliases or {},
        compiler_params=pltpu.CompilerParams(vmem_limit_bytes=KERNELS[name][0] << 20),
        cost_estimate=pl.CostEstimate(
            flops=int(KERNELS[name][1] * FLOPS_PER_MICROSECOND), transcendentals=0, bytes_accessed=1
        ),
        name=name,
    )(*scalars, *arrays)


def block(shape, at=(0, 0)):
    return pl.BlockSpec(shape, lambda *_: at)


def chunk_specs(width, chunks):
    return [block((width, width // 3), (owner, 0)) for owner, _ in chunks]


def chunk_arrays(weights, chunks):
    return [weights[half] for _, half in chunks]


def array(shape, kind=BF16):
    return jax.ShapeDtypeStruct(shape, kind)


ANY = pl.BlockSpec(memory_space=pl.ANY)
KERNELS = {
    "project_pairs": (24, 1.8),
    "project_queries": (24, 2.6),
    "attend": (28, 11.3),
    "leave": (20, 1.4),
    "feed": (58, 18.5),
    "feed_grads": (58, 17.0),
    "enter": (58, 2.5),
    "attend_back": (58, 17.3),
    "pairs_back": (12, 0.8),
    "finish": (28, 2.2),
}
FLOPS_PER_MICROSECOND = 1.15e9


def project_pairs_kernel(x_ref, gain_ref, cosine_ref, sine_ref, wk, wv, pair_ref, normed_ref):
    values = x_ref[...].astype(F32)
    normed = (values * row_scale_of(values) * gain_ref[...]).astype(BF16)
    normed_ref[...] = normed
    keys = turn(dot_nn(normed, wk[...]), cosine_ref[...], sine_ref[...]).astype(BF16)
    values = dot_nn(normed, wv[...]).astype(BF16)
    for i in range(keys.shape[1] // 128):
        pair_ref[:, 256 * i : 256 * i + 128] = keys[:, 128 * i : 128 * (i + 1)]
        pair_ref[:, 256 * i + 128 : 256 * (i + 1)] = values[:, 128 * i : 128 * (i + 1)]


def project_pairs(x_rows, gain, cosine, sine, weights):
    rows, width = x_rows.shape
    pair_width = 2 * (width // 3)
    return call(
        project_pairs_kernel,
        "project_pairs",
        (x_rows, gain, cosine, sine, *chunk_arrays(weights, PAIR_CHUNKS)),
        [block(x.shape) for x in (x_rows, gain, cosine, sine)] + chunk_specs(width, PAIR_CHUNKS),
        [array((rows, pair_width)), array((rows, width))],
        [block((rows, pair_width)), block((rows, width))],
    )


def project_queries_kernel(normed_ref, cosine_ref, sine_ref, w0, w1, w2, query_ref):
    third = w0.shape[1]
    for i, w in enumerate((w0, w1, w2)):
        turned = turn(dot_nn(normed_ref[...], w[...]), cosine_ref[...], sine_ref[...])
        query_ref[:, i * third : (i + 1) * third] = (turned * HEAD_SIZE ** (-0.5)).astype(BF16)


def project_queries(normed, cosine, sine, weights):
    rows, width = normed.shape
    return call(
        project_queries_kernel,
        "project_queries",
        (normed, cosine, sine, *chunk_arrays(weights, QUERY_CHUNKS)),
        [block(x.shape) for x in (normed, cosine, sine)] + chunk_specs(width, QUERY_CHUNKS),
        array((rows, width)),
        block((rows, width)),
    )


def attend_kernel(group, counts, q_ref, p0, p1, p2, p3, *rest):
    o_ref = rest[-1]
    rows = q_ref.shape[0]
    refs = (p0, p1, p2, p3)
    row = lax.broadcasted_iota(jnp.int32, (rows, rows), 0)
    col = lax.broadcasted_iota(jnp.int32, (rows, rows), 1)
    allowed = [jnp.logical_and(col <= row, col < counts[0])]
    allowed += [col < counts[j] for j in range(1, 4)]
    allowed = [jnp.concatenate([a] * group, axis=0) for a in allowed]
    for pair in range(2):
        queries = jnp.concatenate([head_of(q_ref, pair * group + i) for i in range(group)], axis=0)
        scores = [
            jnp.where(allowed[j], dot_nt(queries, head_of(refs[j], pair)), MASKED)
            for j in range(4)
        ]
        top = functools.reduce(jnp.maximum, [jnp.max(s, axis=1, keepdims=True) for s in scores])
        soft = [jnp.exp(s - top) for s in scores]
        total = functools.reduce(jnp.add, [jnp.sum(s, axis=1, keepdims=True) for s in soft])
        out = functools.reduce(
            jnp.add, [dot_nn(soft[j].astype(BF16), head_of(refs[j], 2 + pair)) for j in range(4)]
        )
        out = (out / total).astype(BF16)
        for i in range(group):
            start = (pair * group + i) * HEAD_SIZE
            o_ref[:, start : start + HEAD_SIZE] = out[i * rows : (i + 1) * rows]


def attention_sizes(queries, pairs_own):
    rows = queries.shape[0] // 2
    steps = pairs_own.shape[1] // (4 * HEAD_SIZE)
    group = queries.shape[1] // (2 * HEAD_SIZE * steps)
    return rows, steps, group


def attend(b, counts, queries, pairs_own, others, earlier):
    rows, steps, group = attention_sizes(queries, pairs_own)
    width = queries.shape[1]
    query_spec = pl.BlockSpec((rows, width // steps), lambda i, c: (b, i))
    own_spec = pl.BlockSpec((rows, 4 * HEAD_SIZE), lambda i, c: (b, i))
    pair_spec = pl.BlockSpec((rows, 4 * HEAD_SIZE), lambda i, c: (0, i))
    more = [] if earlier is None else [earlier]
    return call(
        functools.partial(attend_kernel, group),
        "attend",
        (queries, pairs_own, *others, *more),
        [query_spec, own_spec] + [pair_spec] * 3 + [ANY] * len(more),
        array(queries.shape),
        query_spec,
        (counts,),
        {6: 0} if more else None,
        grid=(steps,),
    )


def attend_back_kernel(group, counts, q_ref, g_ref, cos_ref, sin_ref, p0, p1, p2, p3, *rest):
    dq_ref, kept_ref, sent_ref, turned_ref = rest[-4:]
    rows = q_ref.shape[0]
    half = HEAD_SIZE // 2
    both = jnp.concatenate([p0[...], p1[...], p2[...], p3[...]], axis=0)
    keys, values = both[:, :128], both[:, 128:]
    keys_t = keys.T
    row = lax.broadcasted_iota(jnp.int32, (rows, rows), 0)
    col = lax.broadcasted_iota(jnp.int32, (rows, rows), 1)
    allowed = [jnp.logical_and(row <= col, row < counts[0])]
    allowed += [row < counts[j] for j in range(1, 4)]
    allowed = jnp.concatenate([jnp.concatenate([a] * group, axis=1) for a in allowed], axis=0)
    key_grads, value_grads = [], []
    for pair in range(2):
        lanes = slice(pair * HEAD_SIZE, (pair + 1) * HEAD_SIZE)
        key, value = keys[:, lanes], values[:, lanes]
        queries = jnp.concatenate([head_of(q_ref, pair * group + i) for i in range(group)], axis=0)
        grads = jnp.concatenate([head_of(g_ref, pair * group + i) for i in range(group)], axis=0)
        scores = jnp.where(allowed, dot_nt(key, queries), MASKED)
        soft = jnp.exp(scores - jnp.max(scores, axis=0, keepdims=True))
        soft = soft * (1.0 / jnp.sum(soft, axis=0, keepdims=True))
        grad_soft = dot_nt(value, grads)
        scaled = soft * grad_soft
        grad_scores = (scaled - soft * jnp.sum(scaled, axis=0, keepdims=True)).astype(BF16)
        value_grads.append(dot_nn(soft.astype(BF16), grads))
        key_grads.append(dot_nn(grad_scores, queries))
        query_grad = dot_nn(keys_t[lanes, :], grad_scores) * HEAD_SIZE ** (-0.5)
        for i in range(group):
            part = query_grad[:, i * rows : (i + 1) * rows]
            first, second = part[:half], part[half:]
            start = (pair * group + i) * HEAD_SIZE
            turned_ref[start : start + half, :] = first * cos_ref[...] + second * sin_ref[...]
            turned_ref[start + half : start + HEAD_SIZE, :] = (
                second * cos_ref[...] - first * sin_ref[...]
            )
    grads = jnp.concatenate(key_grads + value_grads, axis=1).astype(BF16)
    kept_ref[...] = grads[: 2 * rows]
    sent_ref[...] = grads[2 * rows :]
    dq_ref[...] = turned_ref[...].T.astype(BF16)


def attend_back(b, counts, queries, grads, cosine_t, sine_t, pairs_own, others, earlier):
    rows, steps, group = attention_sizes(queries, pairs_own)
    width = queries.shape[1]
    query_spec = pl.BlockSpec((rows, width // steps), lambda i, c: (b, i))
    grad_spec = pl.BlockSpec((rows, width // steps), lambda i, c: (0, i))
    own_spec = pl.BlockSpec((rows, 4 * HEAD_SIZE), lambda i, c: (b, i))
    pair_spec = pl.BlockSpec((rows, 4 * HEAD_SIZE), lambda i, c: (0, i))
    half_spec = pl.BlockSpec((2 * rows, 4 * HEAD_SIZE), lambda i, c: (0, i))
    more = [] if earlier is None else [earlier]
    return call(
        functools.partial(attend_back_kernel, group),
        "attend_back",
        (queries, grads, cosine_t, sine_t, pairs_own, *others, *more),
        [query_spec, grad_spec, block(cosine_t.shape), block(sine_t.shape), own_spec]
        + [pair_spec] * 3
        + [ANY] * len(more),
        [array(queries.shape)] + [array((2 * rows, pairs_own.shape[1]))] * 2,
        [query_spec, half_spec, half_spec],
        (counts,),
        {9: 0} if more else None,
        grid=(steps,),
        scratch=[pltpu.VMEM((width // steps, rows), F32)],
    )


def leave_kernel(x_ref, o_ref, gain_ref, w0, w1, w2, middle_ref, normed_ref):
    out = o_ref[...]
    added = jnp.concatenate([dot_nn(out, w[...]) for w in (w0, w1, w2)], axis=1)
    middle = x_ref[...].astype(F32) + added
    middle_ref[...] = middle
    normed_ref[...] = (middle * row_scale_of(middle) * gain_ref[...]).astype(BF16)


def leave(b, x_rows, attended, gain, weights):
    rows, width = x_rows.shape[0] // 2, x_rows.shape[1]
    here = block((rows, width), (b, 0))
    return call(
        leave_kernel,
        "leave",
        (x_rows, attended, gain, *chunk_arrays(weights, OUT_CHUNKS)),
        [here, here, block(gain.shape)] + chunk_specs(width, OUT_CHUNKS),
        [array((rows, width), F32), array((rows, width))],
        [block((rows, width))] * 2,
    )


def feed_kernel(steps, places, low_ref, high_ref, grad_ref, weight_ref, *rest):
    rows_ref, act_ref, inner_ref, out_ref, back_low, back_high = rest[-6:]
    step = pl.program_id(0)
    share = weight_ref.shape[1] // 3
    gate, up, down_t = (slice(i * share, (i + 1) * share) for i in range(3))

    @pl.when(step < steps // 2)
    def _():
        rows_ref[...] = low_ref[...]

    @pl.when(step >= steps // 2)
    def _():
        rows_ref[...] = high_ref[...]

    rows = rows_ref[...]
    gate_proj = dot_nn(rows, weight_ref[:, gate])
    up_proj = dot_nn(rows, weight_ref[:, up])
    grad_act = dot_nn(grad_ref[...], weight_ref[:, down_t])
    sigma = 1.0 / (1.0 + jnp.exp(-gate_proj))
    silu = gate_proj * sigma
    act = (silu * up_proj).astype(BF16)
    act_ref[...] = act
    grad_gate = (grad_act * up_proj * sigma * (1.0 + gate_proj * (1.0 - sigma))).astype(BF16)
    grad_up = (grad_act * silu).astype(BF16)
    inner_ref[:, gate] = grad_gate
    inner_ref[:, up] = grad_up
    back = dot_nt(grad_gate, weight_ref[:, gate]) + dot_nt(grad_up, weight_ref[:, up])
    out_ref[...] = dot_nt(act, weight_ref[:, down_t]).astype(BF16)

    @pl.when(step < steps // 2)
    def _():
        back_low[...] = back.astype(BF16)

    @pl.when(step >= steps // 2)
    def _():
        back_high[...] = back.astype(BF16)


def feed(b, places, low, high, grads, weights, earlier):
    half, width = low.shape
    share = weights.shape[1] // 3
    steps = 4
    rows = 2 * half // steps
    first = pl.BlockSpec((rows, width), lambda i, p: (jnp.minimum(i, steps // 2 - 1), 0))
    second = pl.BlockSpec((rows, width), lambda i, p: (jnp.maximum(i - steps // 2, 0), 0))

    def here(columns):
        return pl.BlockSpec((rows, columns), lambda i, p: (b * steps + i, 0))

    more = [] if earlier is None else list(earlier)
    return call(
        functools.partial(feed_kernel, steps),
        "feed",
        (low, high, grads, weights, *more),
        [
            first,
            second,
            here(width),
            pl.BlockSpec(weights.shape, lambda i, p: (0, 0), pipeline_mode=pl.Buffered(1)),
        ]
        + [ANY] * len(more),
        [array((4 * half, width)), array((4 * half, share)), array((4 * half, 2 * share))]
        + [array((2 * half, width))]
        + [array((half, width))] * 2,
        [here(width), here(share), here(2 * share)]
        + [pl.BlockSpec((rows, width), lambda i, p: (p[i], 0)), first, second],
        (places,),
        aliases={5: 0, 6: 1, 7: 2} if more else None,
        grid=(steps,),
    )


def feed_grads_kernel(rows_ref, grad_ref, inner_ref, act_ref, out_ref):
    share = act_ref.shape[1]
    out_ref[:, : 2 * share] = dot_nn(rows_ref[...].T, inner_ref[...]).astype(BF16)
    out_ref[:, 2 * share :] = dot_nn(grad_ref[...].T, act_ref[...]).astype(BF16)


def feed_grads(rows, grads, inner_grads, activated):
    count, width = rows.shape
    share = activated.shape[1]
    steps = 3
    left = pl.BlockSpec((count, width // steps), lambda i: (0, i))

    def held(columns):
        return pl.BlockSpec((count, columns), lambda i: (0, 0), pipeline_mode=pl.Buffered(1))

    return call(
        feed_grads_kernel,
        "feed_grads",
        (rows, grads, inner_grads, activated),
        [left, left, held(2 * share), held(share)],
        array((width, 3 * share)),
        pl.BlockSpec((width // steps, 3 * share), lambda i: (i, 0)),
        grid=(steps,),
    )


def enter_kernel(
    count, part_ref, near_ref, far_ref, middle_ref, cot_ref, gain_ref, w0, w1, w2, *rest
):
    grad_middle_ref, branch_ref, out_ref, gain_grad_ref = rest[-4:]
    rows, width = middle_ref.shape
    third = width // 3
    middle = middle_ref[...]
    grad_normed = (
        part_ref[...].astype(F32) + near_ref[...].astype(F32) + far_ref[...].astype(F32)
    )
    scale = row_scale_of(middle)
    row = lax.broadcasted_iota(jnp.int32, (rows, width), 0)
    grad_row = jnp.where(row < count[0], cot_ref[...].astype(F32), 0.0)
    gain_grad = jnp.sum(grad_normed * middle * scale, axis=0, keepdims=True)
    gain_grad_ref[...] = jnp.broadcast_to(gain_grad, gain_grad_ref.shape)
    inner = grad_normed * gain_ref[...]
    grad_middle = grad_row + (
        scale * inner - middle * scale**3 * jnp.mean(inner * middle, axis=-1, keepdims=True)
    )
    grad_middle_ref[...] = grad_middle
    branch = grad_middle.astype(BF16)
    branch_ref[...] = branch
    weights = (w0, w1, w2)
    out = dot_nt(branch[:, :third], w0[...])
    for c in range(1, 3):
        out = out + dot_nt(branch[:, c * third : (c + 1) * third], weights[c][...])
    out_ref[...] = out.astype(BF16)


def enter(b, count, part, near_part, far_part, middle, cot_rows, gain, weights, earlier):
    rows, width = middle.shape
    full, here = block((rows, width)), block((rows, width), (b, 0))
    more = [] if earlier is None else [earlier]
    return call(
        enter_kernel,
        "enter",
        (part, near_part, far_part, middle, cot_rows, gain)
        + (*chunk_arrays(weights, OUT_CHUNKS), *more),
        [full, full, full, full, here, block(gain.shape)]
        + chunk_specs(width, OUT_CHUNKS)
        + [ANY] * len(more),
        [
            array((rows, width), F32),
            array((2 * rows, width)),
            array((rows, width)),
            array((8, width), F32),
        ],
        [full, here, full, block((8, width))],
        (count,),
        {10: 1} if more else None,
    )


def pairs_back_kernel(kept_ref, near_ref, far_ref, cosine_ref, sine_ref, *rest):
    pair_ref = rest[-1]
    width = pair_ref.shape[1] // 2
    for i in range(width // 128):
        lanes = slice(256 * i, 256 * (i + 1))
        total = (
            kept_ref[:, lanes].astype(F32)
            + near_ref[:, lanes].astype(F32)
            + far_ref[:, lanes].astype(F32)
        )
        turned = turn(total[:, :128], cosine_ref[...], -sine_ref[...])
        pair_ref[:, 128 * i : 128 * (i + 1)] = turned.astype(BF16)
        pair_ref[:, width + 128 * i : width + 128 * (i + 1)] = total[:, 128:].astype(BF16)


def pairs_back(b, kept, near_part, far_part, cosine, sine, earlier):
    rows, width = far_part.shape
    first = block((rows, width))
    table = block((rows, 128))
    more = [] if earlier is None else [earlier]
    return call(
        pairs_back_kernel,
        "pairs_back",
        (kept, near_part, far_part, cosine, sine, *more),
        [first, first, first, table, table] + [ANY] * len(more),
        array((2 * rows, width)),
        block((rows, width), (b, 0)),
        aliases={5: 0} if more else None,
    )


def finish_kernel(
    x_ref, query_ref, pair_ref, middle_ref, gain_ref, wk, wv, w0, w1, w2, grad_ref, gain_grad_ref
):
    third = x_ref.shape[1] // 3
    grads = [pair_ref[:, :third], pair_ref[:, third:]]
    grads += [query_ref[:, c * third : (c + 1) * third] for c in range(3)]
    grad_normed = dot_nt(grads[0], wk[...])
    for grad, w in zip(grads[1:], (wv, w0, w1, w2)):
        grad_normed = grad_normed + dot_nt(grad, w[...])
    values = x_ref[...].astype(F32)
    scale = row_scale_of(values)
    gain_grad = jnp.sum(grad_normed * values * scale, axis=0, keepdims=True)
    gain_grad_ref[...] = jnp.broadcast_to(gain_grad, gain_grad_ref.shape)
    inner = grad_normed * gain_ref[...]
    grad_ref[...] = (
        middle_ref[...]
        + scale * inner
        - values * scale**3 * jnp.mean(inner * values, axis=-1, keepdims=True)
    ).astype(BF16)


def finish(b, x_rows, query_grads, pair_grads, grad_middle, gain, weights):
    rows, width = grad_middle.shape
    here = block((rows, width), (b, 0))
    return call(
        finish_kernel,
        "finish",
        (x_rows, query_grads, pair_grads, grad_middle, gain)
        + (*chunk_arrays(weights, PAIR_CHUNKS + QUERY_CHUNKS),),
        [here, here, block((rows, pair_grads.shape[1]), (b, 0)), block((rows, width))]
        + [block(gain.shape)]
        + chunk_specs(width, PAIR_CHUNKS + QUERY_CHUNKS),
        [array((rows, width)), array((8, width), F32)],
        [block((rows, width)), block((8, width))],
    )


def row_major(value):
    return with_layout_constraint(value, Layout(major_to_minor=tuple(range(value.ndim))))


def added(first, second):
    return (first.astype(F32) + second.astype(F32)).astype(BF16)


def pick(flag, first, second):
    return jnp.where(flag, first, second)


def sum_over_data(part_a, part_b, extra, earlier):
    data_count = lax.axis_size("dp")
    data_index = lax.axis_index("dp")
    columns = part_a[0].shape[1]

    def split(value):
        return value.reshape(data_count, -1, columns)

    if data_count != 8:
        total = part_a[0] + far(part_a[1].astype(BF16)).astype(F32)
        other = part_b[0] + far(part_b[1].astype(BF16)).astype(F32)
        rows = jnp.concatenate([split(total), split(other), extra], axis=1).astype(BF16)
        rows = lax.psum_scatter(rows, "dp", scatter_dimension=0, tiled=True)[0].astype(F32)
        share = total.shape[0] // data_count
        return rows[:share], rows[share : 2 * share], rows[2 * share :], earlier

    groups = data_count // 2
    odd = (data_index & 1) == 1
    group = lax.shift_right_logical(data_index, 1)

    def beside(value):
        even_rows, odd_rows = value[..., 0, :, :], value[..., 1, :, :]
        sent = pick(odd, even_rows, odd_rows).astype(BF16)
        came = lax.ppermute(sent, "dp", [(i, i ^ 1) for i in range(data_count)])
        return pick(odd, odd_rows, even_rows).astype(F32) + came.astype(F32)

    def along(value):
        low = value.astype(BF16)
        total = lax.dynamic_index_in_dim(
            value, group, 0, keepdims=False, allow_negative_indices=False
        )
        for step in range(1, groups):
            sent = lax.dynamic_index_in_dim(
                low, (group + step) & (groups - 1), 0, keepdims=False, allow_negative_indices=False
            )
            moves = [(i, (i + 2 * step) % data_count) for i in range(data_count)]
            total = total + lax.ppermute(sent, "dp", moves).astype(F32)
        return total

    second = jnp.stack([split(p) for p in part_b], axis=0)
    second = beside(second.reshape(2, groups, 2, -1, columns))
    first = split(part_a[0] + far(part_a[1].astype(BF16)).astype(F32))
    first = jnp.concatenate([first, extra], axis=1).reshape(groups, 2, -1, columns)
    first, earlier = lax.optimization_barrier((beside(first), earlier))
    second = along(jnp.moveaxis(second, 1, 0))
    first = along(first)
    second = second[0] + far(second[1].astype(BF16)).astype(F32)
    share = second.shape[0]
    return first[:share], second, first[share:], earlier


def shards(
    inputs,
    lengths,
    gain_attn,
    gain_mlp,
    w_query,
    key_weight,
    value_weight,
    w_gate,
    w_up,
    w_out,
    w_down,
    cotangent,
):
    micro = inputs.shape[0]
    row_share = inputs.shape[2]
    width = inputs.shape[3]
    tensor_count = lax.axis_size("tensor")
    tensor_index = lax.axis_index("tensor")
    hidden_share = w_gate.shape[1]

    third = width // 3

    out_parts = [w_out[:, c * third : (c + 1) * third] for c in range(3)]
    query_parts = [w_query[:, c * third : (c + 1) * third] for c in range(3)]
    attn_quarter = lax.select_n(
        tensor_index,
        jnp.concatenate([key_weight, query_parts[0]], axis=1),
        jnp.concatenate([value_weight, query_parts[1]], axis=1),
        jnp.concatenate([out_parts[1], query_parts[2]], axis=1),
        jnp.concatenate([out_parts[2], out_parts[0]], axis=1),
    )
    attn_own = lax.all_gather(attn_quarter, "dp", axis=0, tiled=True)
    mlp_local = jnp.concatenate([w_gate, w_up, w_down.T], axis=1)
    mlp_full = lax.all_gather(mlp_local, "dp", axis=0, tiled=True)
    gains = lax.all_gather(jnp.stack([gain_attn, gain_mlp]), "dp", axis=1, tiled=True).astype(F32)
    gain_one, gain_two = gains[0:1], gains[1:2]

    query_pos = tensor_index * row_share + jnp.arange(row_share, dtype=jnp.int32)
    exponent = jnp.arange(HEAD_SIZE // 2, dtype=F32) * (2.0 / HEAD_SIZE)
    angles = query_pos.astype(F32)[:, None] * (ROPE_BASE ** (-exponent))[None, :]
    cosine, sine = jnp.cos(angles), jnp.sin(angles)
    cosine_t, sine_t = cosine.T, sine.T
    cosine = jnp.concatenate([cosine] * 4, axis=1)
    sine = jnp.concatenate([-sine, sine, -sine, sine], axis=1)

    def counts_of(b):
        counts = []
        for x in BLOCK_XOR:
            block = tensor_index ^ x
            count = jnp.clip(lengths[b, 0] - block * row_share, 0, row_share)
            counts.append(jnp.where(block <= tensor_index, count, 0))
        return jnp.stack(counts).astype(jnp.int32)

    counts = [counts_of(b) for b in range(micro)]
    valid_rows = [
        jnp.clip(lengths[b, 0] - tensor_index * row_share, 0, row_share).astype(jnp.int32)
        for b in range(micro)
    ]
    valids = [
        (jnp.arange(row_share, dtype=jnp.int32) < valid_rows[b])[:, None] for b in range(micro)
    ]

    grad_own = jnp.stack(
        [jnp.where(valids[b], cotangent[b, 0], jnp.zeros((), BF16)) for b in range(micro)]
    )
    grad_far = far(grad_own)
    grad_near = near(jnp.stack([grad_own, grad_far]))
    grad_ffn = jnp.concatenate(
        [p[b] for b in range(micro) for p in (grad_own, grad_far, grad_near[0], grad_near[1])],
        axis=0,
    )

    low, high_own = attn_own[:, :third], attn_own[:, third:]
    came, high_own = lax.optimization_barrier((far(low), high_own))
    attn_w = (spread(low, came), spread(high_own, far(high_own)))
    x_rows = inputs[:, 0].reshape(micro * row_share, width)
    cot_rows = cotangent[:, 0].reshape(micro * row_share, width)
    cosine_all = jnp.concatenate([cosine] * micro, axis=0)
    sine_all = jnp.concatenate([sine] * micro, axis=0)
    pairs_own, normed = project_pairs(x_rows, gain_one, cosine_all, sine_all, attn_w)
    queries = project_queries(normed, cosine_all, sine_all, attn_w)
    kept = []
    attended = None
    for b in range(micro):
        own = pairs_own[b * row_share : (b + 1) * row_share]
        if b > 0:
            own, queries = lax.optimization_barrier((own, queries))
        across = far(own)
        if b == 0:
            across, queries = lax.optimization_barrier((across, queries))
        else:
            across, _ = lax.optimization_barrier((across, attended))
        others = [across, near(own), near(across)]
        attended = attend(b, counts[b], queries, pairs_own, others, attended)
        middle, hidden_own = leave(b, x_rows, attended, gain_two, attn_w)
        kept.append(dict(others=others, middle=middle, own=hidden_own, across=far(hidden_own)))
    mlp_full, _ = lax.optimization_barrier((mlp_full, kept[-1]["own"]))
    kept[0]["across"], _ = lax.optimization_barrier((kept[0]["across"], attended))
    for k in kept:
        k["low"] = jnp.concatenate([k["own"], k["across"]], axis=0)
        k["high"] = near(k["low"])

    places = jnp.stack([tensor_index ^ x for x in BLOCK_XOR]).astype(jnp.int32)
    shared = None
    for b in range(micro):
        k = kept[b]
        *shared, k["out"], k["part"], back_high = feed(
            b, places, k["low"], k["high"], grad_ffn, mlp_full, shared
        )
        if b > 0:
            back_high, kept[b - 1]["far_part"] = lax.optimization_barrier(
                (back_high, far(kept[b - 1]["far_part"]))
            )
        k["near_part"] = near(back_high)
        k["far_part"] = added(k["part"][row_share:], k["near_part"][row_share:])
    hidden_rows, activated, inner_grads = shared
    grad_mlp_w = feed_grads(hidden_rows, grad_ffn, inner_grads, activated)
    grad_mlp_w, kept[0]["middle"], kept[-1]["far_part"] = lax.optimization_barrier(
        (grad_mlp_w, kept[0]["middle"], kept[-1]["far_part"])
    )
    kept[-1]["far_part"] = far(kept[-1]["far_part"])

    gain_two_grads = []
    branch = query_grads = pair_grads = None

    grad_mlp_w = lax.psum_scatter(grad_mlp_w, "dp", scatter_dimension=0, tiled=True)
    def summed_out(b):
        return lax.psum_scatter(kept[b]["out"], "tensor", scatter_dimension=0, tiled=True)

    kept[0]["out"] = summed_out(0)
    for b in range(micro):
        k = kept[b]
        k["grad_middle"], branch, grad_att, gain_two_grad = enter(
            b,
            valid_rows[b][None],
            k["part"],
            k["near_part"],
            k["far_part"],
            k["middle"],
            cot_rows,
            gain_two,
            attn_w,
            branch,
        )
        gain_two_grads.append(gain_two_grad[0:1])
        if b > 0:
            k["out"], grad_att = lax.optimization_barrier((k["out"], grad_att))
            k["out"] = summed_out(b)
            kept[b - 1]["pair_far"], grad_att = lax.optimization_barrier(
                (kept[b - 1]["pair_far"], grad_att)
            )
        query_grads, k["pair_kept"], pair_sent = attend_back(
            b, counts[b], queries, grad_att, cosine_t, sine_t, pairs_own, k["others"], query_grads
        )
        k["near_pair"] = near(pair_sent)
        k["pair_far"] = added(k["pair_kept"][row_share:], k["near_pair"][row_share:])
    for b in range(micro):
        k = kept[b]
        pair_grads = pairs_back(
            b, k["pair_kept"], k["near_pair"], far(k["pair_far"]), cosine, sine, pair_grads
        )

    input_grads, gain_one_grads = [], []
    for b in range(micro):
        k = kept[b]
        input_grad, gain_one_grad = finish(
            b, x_rows, query_grads, pair_grads, k["grad_middle"], gain_one, attn_w
        )
        gain_one_grads.append(gain_one_grad[0:1])
        input_grads.append(input_grad)

    odd = (tensor_index & 1) == 1
    high = (tensor_index & 2) == 2
    query_grad = [query_grads[:, c * third : (c + 1) * third] for c in range(3)]
    branch_grad = [branch[:, c * third : (c + 1) * third] for c in range(3)]
    key_grad, value_grad = pair_grads[:, :third], pair_grads[:, third:]

    def traded(left_even, right_even, left_odd, right_odd):
        def product(flag):
            left = left_even if left_even is left_odd else pick(flag, left_odd, left_even)
            return contract_rows(left, pick(flag, right_odd, right_even))

        sent = row_major(product(jnp.logical_not(odd)).astype(BF16))
        return row_major(product(odd)) + near(sent).astype(F32)

    query_low = traded(normed, query_grad[0], normed, query_grad[1])
    query_high = traded(normed, query_grad[2], attended, branch_grad[0])
    pair_low = traded(normed, key_grad, normed, value_grad)
    pair_high = traded(attended, branch_grad[1], attended, branch_grad[2])
    data_count = lax.axis_size("dp")
    gain_part = jnp.stack([sum(gain_one_grads), sum(gain_two_grads)])[:, 0]
    gain_part = jnp.moveaxis(gain_part.reshape(2, data_count, -1), 1, 0)
    gain_share = gain_part.shape[2]
    gain_part = jnp.pad(gain_part, ((0, 0), (0, 14), (0, third - gain_share)))
    first, second, gain_rows, grad_mlp_w = sum_over_data(
        (pick(high, pair_high, pair_low), pick(high, pair_low, pair_high)),
        (pick(high, query_high, query_low), pick(high, query_low, query_high)),
        gain_part,
        grad_mlp_w,
    )
    outputs = []
    for b in range(micro):
        k = kept[b]
        ffn_out = k["out"].astype(F32)
        outputs.append(jnp.where(valids[b], k["middle"] + ffn_out, 0.0).astype(BF16))
    quarter = jnp.concatenate([first, second, gain_rows], axis=0).astype(BF16)
    other = far(quarter)
    pair = jnp.stack([pick(high, other, quarter), pick(high, quarter, other)])
    other = near(pair)
    even_pair, odd_pair = pick(odd, other, pair).astype(F32), pick(odd, pair, other).astype(F32)
    share = first.shape[0]
    chunks = [even_pair[0], odd_pair[0], even_pair[1], odd_pair[1]]
    gain_sum = sum(c[2 * share :] for c in chunks)
    first_of = [c[:share] for c in chunks]
    second_of = [c[share : 2 * share] for c in chunks]
    grad_mlp_w = grad_mlp_w.astype(F32)
    return (
        jnp.stack(outputs)[:, None],
        jnp.stack(input_grads)[:, None],
        gain_sum[0, :gain_share],
        gain_sum[1, :gain_share],
        jnp.concatenate(second_of[:3], axis=1),
        first_of[0],
        first_of[1],
        grad_mlp_w[:, :hidden_share],
        grad_mlp_w[:, hidden_share : 2 * hidden_share],
        jnp.concatenate([second_of[3], first_of[2], first_of[3]], axis=1),
        grad_mlp_w[:, 2 * hidden_share :].T,
    )


def solution(mesh):
    in_specs = (
        P(None, "dp", "tensor", None),
        P(None, "dp"),
        P("dp"),
        P("dp"),
        P("dp", None),
        P("dp", None),
        P("dp", None),
        P("dp", "tensor"),
        P("dp", "tensor"),
        P("dp", None),
        P("tensor", "dp"),
        P(None, "dp", "tensor", None),
    )
    out_specs = (
        P(None, "dp", "tensor", None),
        P(None, "dp", "tensor", None),
        P("dp"),
        P("dp"),
        P("dp", None),
        P("dp", None),
        P("dp", None),
        P("dp", "tensor"),
        P("dp", "tensor"),
        P("dp", None),
        P("tensor", "dp"),
    )
    return jax.shard_map(shards, mesh=mesh, in_specs=in_specs, out_specs=out_specs, check_vma=False)
```
